32 devices in a mesh: lon: 16 (over z, x, core), lev: 2 (over y).
Axes of the slice: x: 2, y: 2, z: 4, core: 2. Of those that a mesh axis runs over, the one named last changes fastest.
Arguments:
- cotangent: float32 [5, 8, 2880, 1024], P(None, 'lev', 'lon'), may hold values from -6 to 6
- zonal_coef: float32 [8, 2880, 1024], P('lev', 'lon'), may hold values from -0.5 to 0.5
- merid_coef: float32 [8, 2880, 1024], P('lev', 'lon'), may hold values from -0.5 to 0.5
- vertical_wind: float32 [8, 2880, 1024], P('lev', 'lon'), may hold values from -0.5 to 0.5
- cutoff: int32 [64], replicated, may hold values from 1 to 360, as said below
Outputs:
- adjoint_state: float32 [5, 8, 2880, 1024], P(None, 'lev', 'lon')
The draws below stay inside these ranges and needn't reach their ends.
Inputs may be any that keep to these rules, and one draw needn't show every extreme that they name: Every draw holds a row with cutoff exactly 360 and a row with cutoff exactly 1.
All inputs are finite; a program needn't handle non-finite values.
Results may differ from the reference program's by a relative error of at most 0.00023.
Values sent between devices are 32-bit elements; how exact they have to be, the bound alone decides.
A program may use at most 192 MiB of HBM per device.

```python
import jax
import jax.numpy as jnp

NLON = 2880
NLEV = 8
NLAT = 1024
POLAR = 32
KMAX = 360


def draw_cutoff(key, part):
    first_key, second_key, third_key = jax.random.split(jax.random.fold_in(key, 17), 3)
    values = jax.random.randint(first_key, (2 * POLAR,), 1, KMAX + 1)
    position = jax.random.randint(second_key, (), 0, 2 * POLAR)
    offset = jax.random.randint(third_key, (), 1, 2 * POLAR)
    values = values.at[position].set(KMAX)
    values = values.at[(position + offset) % (2 * POLAR)].set(1)
    return values.astype(jnp.int32)


def level_of(stream_key, shape, shards, smallest, high):
    level = 1.0
    for axis_at, parts in shards:
        heights = jax.random.uniform(jax.random.fold_in(jax.random.fold_in(stream_key, 6), axis_at), (parts,), jnp.float32, smallest / len(shards), high / len(shards))
        level = level * jnp.repeat(jnp.exp(heights), shape[axis_at] // parts).reshape((-1,) + (1,) * (len(shape) - 1 - axis_at))
    return level


def normal_values(rng, extent, width, bound, cuts=(), kind=jnp.bfloat16):
    loudness = level_of(rng, extent, cuts, -0.22, 0.18) if cuts else 1.0
    entries = jax.random.normal(rng, extent, jnp.float32) * width * loudness
    return jnp.minimum(jnp.maximum(entries, -bound), bound).astype(kind)


def setup_inputs(seed: int = 0) -> dict:
    key_of = jax.random.split(jax.random.key(seed), 6)
    return {
        "cotangent": normal_values(key_of[0], (5, NLEV, NLON, NLAT), 1.0, 6.0, ((1, 2), (2, 16)), jnp.float32),
        "zonal_coef": jnp.clip(jax.random.uniform(key_of[1], (NLEV, NLON, NLAT), jnp.float32, -0.5, 0.5) * level_of(key_of[1], (NLEV, NLON, NLAT), ((0, 2), (1, 16)), -0.4, 0.0), -0.5, 0.5),
        "merid_coef": jnp.clip(jax.random.uniform(key_of[2], (NLEV, NLON, NLAT), jnp.float32, -0.5, 0.5) * level_of(key_of[2], (NLEV, NLON, NLAT), ((0, 2), (1, 16)), -0.4, 0.0), -0.5, 0.5),
        "vertical_wind": jnp.clip(jax.random.uniform(key_of[3], (NLEV, NLON, NLAT), jnp.float32, -0.5, 0.5) * level_of(key_of[3], (NLEV, NLON, NLAT), ((0, 2), (1, 16)), -0.4, 0.0), -0.5, 0.5),
        "cutoff": draw_cutoff(jax.random.fold_in(key_of[5], 71), 0),
    }


COUPLE_G = 0.3
COUPLE_H = 0.3
COUPLE_B = 0.2


def diff_lon(field):
    return jnp.roll(field, -1, axis=2) - jnp.roll(field, 1, axis=2)


def diff_lat(field):
    padded = jnp.pad(field, ((0, 0), (0, 0), (0, 0), (1, 1)))
    return padded[..., 2:] - padded[..., :-2]


def reference(cotangent, zonal_coef, merid_coef, vertical_wind, cutoff):
    weighted = vertical_wind[None] * cotangent
    padded = jnp.pad(weighted, ((0, 0), (1, 1), (0, 0), (0, 0)))
    adjoint_one = cotangent + (padded[:, 2:] - padded[:, :-2])
    below_sums = jnp.flip(jnp.cumsum(jnp.flip(cotangent[2], 0), 0), 0)
    adjoint_one = adjoint_one.at[3].add(-COUPLE_B * below_sums)
    polar_rows = jnp.concatenate([adjoint_one[..., :POLAR], adjoint_one[..., NLAT - POLAR:]], axis=3)
    spectrum = jnp.fft.rfft(polar_rows, axis=2)
    wavenum = jnp.arange(NLON // 2 + 1, dtype=jnp.int32)[:, None]
    keep_mask = wavenum <= cutoff[None, :]
    spectrum = jnp.where(keep_mask[None, None], spectrum, 0.0)
    smoothed = jnp.fft.irfft(spectrum, n=NLON, axis=2).astype(adjoint_one.dtype)
    filtered = jnp.concatenate([smoothed[..., :POLAR], adjoint_one[..., POLAR:NLAT - POLAR], smoothed[..., POLAR:]], axis=3)
    zonal_part = zonal_coef[None] * filtered
    zonal_flux = jnp.stack([zonal_part[0] + COUPLE_H * filtered[3], zonal_part[1], zonal_part[2], zonal_part[3] + COUPLE_G * filtered[0], zonal_part[4]])
    merid_part = merid_coef[None] * filtered
    merid_flux = jnp.stack([merid_part[0], merid_part[1] + COUPLE_H * filtered[3], merid_part[2], merid_part[3] + COUPLE_G * filtered[1], merid_part[4]])
    return adjoint_one + diff_lon(zonal_flux) + diff_lat(merid_flux)
```

```python
import functools
import math

import jax
import jax.numpy as jnp
import numpy as np
from jax import lax
from jax.experimental import pallas as pl
from jax.experimental.pallas import tpu as pltpu
from jax.sharding import PartitionSpec as P

POLAR = 32
KMAX = 360
COUPLE_G = 0.3
COUPLE_H = 0.3
COUPLE_B = 0.2
MESH = pl.DeviceIdType.MESH
HIGHEST = lax.Precision.HIGHEST
ROOM = 61 << 20


def angles(left, right, period):
    phase = (left * right) % period * (2.0 * math.pi / period)
    return np.cos(phase).astype(np.float32), np.sin(phase).astype(np.float32)


def filter_kernel(
    peers, packed, x_ref, fwd_ref, inv_ref, ct_ref, st_ref, mask_ref, out_ref, held, made,
    own_sem, send_a, recv_a, send_b, recv_b,
):
    me = lax.axis_index("lon")
    kpad = ct_ref.shape[2]
    barrier = pltpu.get_barrier_semaphore()

    def greet(o, _):
        pl.semaphore_signal(
            barrier, inc=1, device_id={"lon": lax.rem(me + o, peers)}, device_id_type=MESH
        )
        return 0

    lax.fori_loop(1, peers, greet, 0)
    pl.semaphore_wait(barrier, peers - 1)

    def out_copy(o):
        d = lax.rem(me + o, peers)
        return pltpu.make_async_remote_copy(
            src_ref=x_ref.at[d], dst_ref=held.at[me], send_sem=send_a.at[d],
            recv_sem=recv_a.at[me], device_id={"lon": d}, device_id_type=MESH,
        )

    def in_copy(o):
        s = lax.rem(me + o, peers)
        return pltpu.make_async_remote_copy(
            src_ref=x_ref.at[s], dst_ref=held.at[s], send_sem=send_a.at[s],
            recv_sem=recv_a.at[s], device_id={"lon": s}, device_id_type=MESH,
        )

    def back_copy(o):
        d = lax.rem(me + o, peers)
        return pltpu.make_async_remote_copy(
            src_ref=made.at[d], dst_ref=out_ref.at[me], send_sem=send_b.at[d],
            recv_sem=recv_b.at[me], device_id={"lon": d}, device_id_type=MESH,
        )

    def home_copy(o):
        s = lax.rem(me + o, peers)
        return pltpu.make_async_remote_copy(
            src_ref=made.at[s], dst_ref=out_ref.at[s], send_sem=send_b.at[s],
            recv_sem=recv_b.at[s], device_id={"lon": s}, device_id_type=MESH,
        )

    lax.fori_loop(1, peers, lambda o, c: (out_copy(o).start(), c)[1], 0)
    own = pltpu.make_async_copy(x_ref.at[me], held.at[me], own_sem)
    own.start()
    own.wait()
    cols = mask_ref.shape[0]
    half = cols // 2
    zero = jnp.zeros((cols, kpad), jnp.float32)
    dot = functools.partial(jnp.dot, precision=HIGHEST, preferred_element_type=jnp.float32)

    def gather(s, carry):
        a, b = carry
        if packed:
            ends = held[s, cols:]
            ends = jnp.concatenate([ends[:, :64], ends[:, 64:]], 0)
            both = dot(held[s, :cols], fwd_ref[:128]) + dot(ends, fwd_ref[128:])
        else:
            both = dot(held[s], fwd_ref[...])
        c, v = both[:, :kpad], both[:, kpad:]
        ct, st = ct_ref[s], st_ref[s]
        return a + (ct * c - st * v), b + (st * c + ct * v)

    def arrive(o, carry):
        in_copy(o).wait_recv()
        return gather(lax.rem(me + o, peers), carry)

    a, b = lax.fori_loop(1, peers, arrive, gather(me, (zero, zero)))
    a = a * mask_ref[...]
    b = b * mask_ref[...]

    def spread(d):
        ct, st = ct_ref[d], st_ref[d]
        p, q = a * ct + b * st, b * ct - a * st
        if packed:
            y = dot(p, inv_ref[0]) + dot(q, inv_ref[1])
            made[d, :cols] = y[:, :128]
            made[d, cols:] = jnp.concatenate([y[:half, 128:], y[half:, 128:]], 1)
        else:
            made[d] = dot(p, inv_ref[0]) + dot(q, inv_ref[1])

    def depart(o, _):
        spread(lax.rem(me + o, peers))
        pl.when(o > 1)(lambda: back_copy(o - 1).start())
        return 0

    lax.fori_loop(1, peers, depart, 0)
    spread(me)
    back_copy(peers - 1).start()
    mine = pltpu.make_async_copy(made.at[me], out_ref.at[me], own_sem)
    mine.start()
    mine.wait()
    lax.fori_loop(1, peers, lambda o, c: (home_copy(o).wait_recv(), c)[1], 0)
    lax.fori_loop(1, peers, lambda o, c: (out_copy(o).wait_send(), c)[1], 0)
    lax.fori_loop(1, peers, lambda o, c: (back_copy(o).wait_send(), c)[1], 0)


def polar_filter(x, cutoff, peers):
    _, cols, lon_dev = x.shape
    nlon = peers * lon_dev
    rows = cutoff.shape[0] // peers
    kpad = (KMAX + 1 + 127) // 128 * 128
    wave = np.arange(kpad)
    fwd = np.concatenate(angles(np.arange(lon_dev)[:, None], wave[None, :], nlon), axis=1)
    inv = np.stack(angles(wave[:, None], np.arange(-1, lon_dev + 1)[None, :] % nlon, nlon))
    over, wider = lon_dev - 128, lon_dev + 2 - 128
    packed = over > 0 and wider <= 64 and cols % 16 == 0
    half = cols // 2
    if packed:
        fwd = np.pad(fwd, ((0, 64 - over), (0, 0)))
        inv = np.pad(inv, ((0, 0), (0, 0), (0, 64 - wider)))
        ends = jnp.pad(x[..., 128:], ((0, 0), (0, 0), (0, 64 - over)))
        x = jnp.concatenate([x[..., :128], jnp.concatenate([ends[:, :half], ends[:, half:]], 2)], 1)
        shape = (peers, cols + half, 128)
    else:
        shape = (peers, cols, lon_dev + 2)
    ct, st = angles(np.arange(peers)[:, None, None] * lon_dev, wave[None, None, :], nlon)
    mine = lax.dynamic_slice_in_dim(cutoff, lax.axis_index("lon") * rows, rows)
    weight = np.where(wave == 0, 1.0 / nlon, 2.0 / nlon).astype(np.float32)
    mask = jnp.where(jnp.asarray(wave, jnp.int32)[None, :] <= mine[:, None], weight[None, :], 0.0)
    mask = jnp.tile(mask, (cols // rows, 1))
    vmem = pl.BlockSpec(memory_space=pltpu.VMEM)
    dma = pltpu.SemaphoreType.DMA
    y = pl.pallas_call(
        functools.partial(filter_kernel, peers, packed),
        out_shape=jax.ShapeDtypeStruct(shape, jnp.float32),
        in_specs=[vmem] * 6,
        out_specs=vmem,
        scratch_shapes=[
            pltpu.VMEM(x.shape, jnp.float32),
            pltpu.VMEM(shape, jnp.float32),
            dma(()), dma((peers,)), dma((peers,)), dma((peers,)), dma((peers,)),
        ],
        compiler_params=pltpu.CompilerParams(
            collective_id=0, has_side_effects=True, vmem_limit_bytes=24 << 20
        ),
        cost_estimate=pl.CostEstimate(flops=8_000_000_000, bytes_accessed=60_000_000, transcendentals=0),
        name="polar_filter",
    )(x, fwd, inv, ct, st, mask)
    if not packed:
        return y
    ends = jnp.concatenate([y[:, cols:, :wider], y[:, cols:, 64 : 64 + wider]], 1)
    return jnp.concatenate([y[:, :cols], ends], 2)


def to_rows(x):
    *lead, levels, lon, lat = x.shape
    n = len(lead)
    x = x.reshape(*lead, levels, lon, lat // 128, 128)
    x = x.transpose(*range(n), n + 1, n + 2, n, n + 3)
    return x.reshape(*lead, lon, lat // 128 * levels, 128)


def from_rows(x, levels):
    *lead, lon, rows, _ = x.shape
    n = len(lead)
    x = x.reshape(*lead, lon, rows // levels, levels, 128)
    x = x.transpose(*range(n), n + 2, n, n + 1, n + 3)
    return x.reshape(*lead, levels, lon, rows // levels * 128)


def chunk_of(lon):
    return max(d for d in range(1, 21) if lon % d == 0)


def edge_kernel(levels, choose, seat, cot, vw, *outs):
    fields, chunk, rows, _ = cot.shape
    tiles = rows // levels
    flat_c = cot.reshape(fields * chunk * rows, 128)
    flat_v = vw.reshape(chunk * rows, 128)
    sends = outs[: 1 if choose else 2]

    def level(ref, count, k):
        return ref[pl.ds(k, count * tiles, stride=levels), :] if levels > 1 else ref[...]

    def product(k, sign, out):
        c = level(flat_c, fields * chunk, k).reshape(fields, chunk, tiles, 128)
        v = level(flat_v, chunk, k).reshape(1, chunk, tiles, 128)
        out[:fields] = sign * (v * c)

    flat_t = cot.at[2].reshape(chunk * rows, 128)
    total = level(flat_t, chunk, 0)
    for k in range(1, levels):
        total = total + level(flat_t, chunk, k)
    total = total.reshape(chunk, tiles, 128)
    if choose:
        sends[0][fields] = jnp.where(seat[0] == 0, 0.0, total)
        pl.when(seat[0] == 0)(lambda: product(levels - 1, -1.0, sends[0]))
        pl.when(seat[0] != 0)(lambda: product(0, 1.0, sends[0]))
    else:
        product(0, 1.0, sends[0])
        product(levels - 1, -1.0, sends[1])
        outs[2][...] = total


def edges_of(seat, cot, vw, levels, choose):
    fields, lon, rows, _ = cot.shape
    tiles = rows // levels
    chunk = chunk_of(lon)
    n = 1 if choose else 2
    wide = fields + 1 if choose else fields
    return pl.pallas_call(
        functools.partial(edge_kernel, levels, choose),
        out_shape=[jax.ShapeDtypeStruct((wide, lon, tiles, 128), jnp.float32)] * n
        + [jax.ShapeDtypeStruct((lon, tiles, 128), jnp.float32)] * (n - 1),
        grid_spec=pltpu.PrefetchScalarGridSpec(
            num_scalar_prefetch=1,
            grid=(lon // chunk,),
            in_specs=[
                pl.BlockSpec((fields, chunk, rows, 128), lambda g, s: (0, g, 0, 0)),
                pl.BlockSpec((chunk, rows, 128), lambda g, s: (g, 0, 0)),
            ],
            out_specs=[pl.BlockSpec((wide, chunk, tiles, 128), lambda g, s: (0, g, 0, 0))] * n
            + [pl.BlockSpec((chunk, tiles, 128), lambda g, s: (g, 0, 0))] * (n - 1),
        ),
        compiler_params=pltpu.CompilerParams(vmem_limit_bytes=24 << 20),
        cost_estimate=pl.CostEstimate(flops=10_000_000, bytes_accessed=22_000_000, transcendentals=0),
        name="edges",
    )(seat, cot, vw)


def coupled(coef, fields, first):
    flux = [coef * f for f in fields]
    flux[first] = flux[first] + COUPLE_H * fields[3]
    flux[3] = flux[3] + COUPLE_G * fields[first]
    return flux


def stencil_kernel(levels, steps, n_edge, seat, cot, vw, zc, mc, smooth, halo, *rest):
    edges = rest[:n_edge]
    tail = edges[0].at[5] if n_edge == 1 else rest[n_edge]
    rest = rest[1:] if n_edge > 1 else rest
    edge_at = (1 - seat[0]) * (levels - 1)
    out, ready, final, wait, prior, spread, below_ref, sems, last_sem = rest[n_edge:]
    _, chunk, rows, _ = cot.shape
    tiles = rows // levels
    g = pl.program_id(0)
    slot = lax.rem(g, 2)
    lane = lax.broadcasted_iota(jnp.int32, (rows, 128), 1)
    row = lax.broadcasted_iota(jnp.int32, (rows, 128), 0)
    k = lax.rem(row, levels)
    cap_lane = lax.broadcasted_iota(jnp.int32, (2 * levels, 128), 1)
    cap_row = lax.broadcasted_iota(jnp.int32, (2 * levels, 128), 0)
    north = (cap_row < levels) & (cap_lane < POLAR)
    south = (cap_row >= levels) & (cap_lane >= 128 - POLAR)

    def first_copy():
        return pltpu.make_async_copy(
            ready.at[0, :, pl.ds(1, chunk - 1)], out.at[:, pl.ds(0, chunk - 1)], sems.at[0]
        )

    def copy(at):
        s = lax.rem(at, 2)
        return pltpu.make_async_copy(
            ready.at[s], out.at[:, pl.ds(at * chunk - 1, chunk)], sems.at[s]
        )

    @pl.when(g == 0)
    def _():
        spread[...] = jnp.zeros_like(spread)
        for f in range(5):
            prior[f] = halo[f, 0]
            wait[f] = jnp.zeros((rows, 128), jnp.float32)

    pl.when(g == 2)(lambda: first_copy().wait())
    pl.when(g > 2)(lambda: copy(g - 2).wait())

    def put(ref, at, value):
        if levels > 1:
            ref[pl.ds(at, tiles, stride=levels), :] = value
        else:
            ref[...] = value

    def one(l, _):
        for f in range(5):
            if n_edge == 1:
                put(spread.at[0, f], edge_at, edges[0][f, l])
            else:
                put(spread.at[0, f], levels - 1, edges[0][f, l])
                put(spread.at[1, f], 0, edges[1][f, l])
        for at in range(levels):
            put(below_ref, at, tail[l])
        wind = vw[l]
        base, fields = [], []
        for f in range(5):
            c = cot[f, l]
            w = wind * c
            a = c
            if levels > 1:
                up = jnp.where(k < levels - 1, pltpu.roll(w, rows - 1, 0), 0.0)
                a = a + (up - jnp.where(k > 0, pltpu.roll(w, 1, 0), 0.0))
            for n in range(n_edge):
                a = a + spread[n, f]
            if f == 3:
                theta = cot[2, l]
                below = below_ref[...] + theta
                for r in range(1, levels):
                    below = below + jnp.where(k < levels - r, pltpu.roll(theta, rows - r, 0), 0.0)
                a = a - COUPLE_B * below
            base.append(a)
            s = smooth[f, l]
            top = jnp.where(north, s, a[: 2 * levels])
            low = jnp.where(south, s, a[rows - 2 * levels :])
            fields.append(jnp.concatenate([top, a[2 * levels : rows - 2 * levels], low], 0))
        zonal = coupled(zc[l], fields, 0)
        merid = coupled(mc[l], fields, 1)
        for f in range(5):
            ready[slot, f, l] = wait[f] + zonal[f]
            left = pltpu.roll(merid[f], 1, 1)
            over = jnp.where(row < levels, 0.0, pltpu.roll(left, levels, 0))
            left = jnp.where(lane == 0, over, left)
            right = pltpu.roll(merid[f], 127, 1)
            over = jnp.where(row >= rows - levels, 0.0, pltpu.roll(right, rows - levels, 0))
            right = jnp.where(lane == 127, over, right)
            wait[f] = base[f] + (right - left) - prior[f]
            prior[f] = zonal[f]
        return 0

    lax.fori_loop(0, chunk, one, 0)
    pl.when(g == 0)(lambda: first_copy().start())
    pl.when(g > 0)(lambda: copy(g).start())

    @pl.when(g == steps - 1)
    def _():
        for f in range(5):
            final[f, 0] = wait[f] + halo[f, 1]
        end = pltpu.make_async_copy(final, out.at[:, pl.ds(steps * chunk - 1, 1)], last_sem)
        end.start()
        copy(g - 1).wait() if steps > 2 else first_copy().wait()
        copy(g).wait()
        end.wait()


def stencil(seat, cot, vw, zc, mc, smooth, halo, edges, levels):
    _, lon, rows, _ = cot.shape
    tiles = rows // levels
    chunk = chunk_of(lon)
    steps = lon // chunk
    field = lambda n: pl.BlockSpec((5, chunk, n, 128), lambda g, s: (0, g, 0, 0))
    plain = lambda n: pl.BlockSpec((chunk, n, 128), lambda g, s: (g, 0, 0))
    return pl.pallas_call(
        functools.partial(stencil_kernel, levels, steps, min(len(edges), 2)),
        out_shape=jax.ShapeDtypeStruct(cot.shape, jnp.float32),
        grid_spec=pltpu.PrefetchScalarGridSpec(
            num_scalar_prefetch=1,
            grid=(steps,),
            in_specs=[field(rows), plain(rows), plain(rows), plain(rows), field(2 * levels),
                      pl.BlockSpec((5, 2, rows, 128), lambda g, s: (0, 0, 0, 0))]
            + [pl.BlockSpec((6, chunk, tiles, 128), lambda g, s: (0, g, 0, 0))]
            if len(edges) == 1
            else [field(rows), plain(rows), plain(rows), plain(rows), field(2 * levels),
                  pl.BlockSpec((5, 2, rows, 128), lambda g, s: (0, 0, 0, 0)),
                  field(tiles), field(tiles), plain(tiles)],
            out_specs=pl.BlockSpec(memory_space=pl.ANY),
            scratch_shapes=[
                pltpu.VMEM((2, 5, chunk, rows, 128), jnp.float32),
                pltpu.VMEM((5, 1, rows, 128), jnp.float32),
                pltpu.VMEM((5, rows, 128), jnp.float32),
                pltpu.VMEM((5, rows, 128), jnp.float32),
                pltpu.VMEM((min(len(edges), 2), 5, rows, 128), jnp.float32),
                pltpu.VMEM((rows, 128), jnp.float32),
                pltpu.SemaphoreType.DMA((2,)),
                pltpu.SemaphoreType.DMA(()),
            ],
        ),
        compiler_params=pltpu.CompilerParams(vmem_limit_bytes=40 << 20),
        cost_estimate=pl.CostEstimate(
            flops=30 * 5 * lon * rows * 128, bytes_accessed=4 * 14 * lon * rows * 128, transcendentals=0
        ),
        name="stencil",
    )(seat, cot, vw, zc, mc, smooth, halo, *edges)


def swap_levels(first, last, total):
    count = lax.axis_size("lev")
    if count == 2:
        seat = lax.axis_index("lev")
        lead = jnp.concatenate([first, total[None]], 0)
        trail = jnp.concatenate([last, jnp.zeros_like(total)[None]], 0)
        got = lax.ppermute(jnp.where(seat == 0, trail, lead), "lev", [(0, 1), (1, 0)])
        return jnp.where(seat == 0, got[:5], 0.0), jnp.where(seat == 1, got[:5], 0.0), got[5]
    up = lax.ppermute(first, "lev", [(i + 1, i) for i in range(count - 1)])
    down = lax.ppermute(last, "lev", [(i, i + 1) for i in range(count - 1)])
    return up, down, later_sum(total)


def later_sum(local):
    count = lax.axis_size("lev")
    total = jnp.zeros_like(local)
    for r in range(1, count):
        total = total + lax.ppermute(local, "lev", [(i + r, i) for i in range(count - r)])
    return total


def ask_levels(cot, vw):
    return swap_levels(vw[0] * cot[:, 0], vw[-1] * cot[:, -1], cot[2].sum(0))


def adjoint_part(cot, vw, up, down, later):
    weighted = vw[None] * cot
    above = jnp.concatenate([weighted[:, 1:], up[:, None]], 1)
    under = jnp.concatenate([down[:, None], weighted[:, :-1]], 1)
    below = [later + cot[2, -1]]
    for k in range(cot.shape[1] - 2, -1, -1):
        below.insert(0, below[0] + cot[2, k])
    parts = cot + (above - under)
    return jnp.concatenate(
        [parts[:3], parts[3:4] - COUPLE_B * jnp.stack(below)[None], parts[4:]], 0
    )


def polar_cut(x):
    return jnp.concatenate([x[..., :POLAR], x[..., x.shape[-1] - POLAR :]], -1)


def plain_body(cotangent, zonal_coef, merid_coef, vertical_wind, cutoff):
    levels, lon_dev, lat = cotangent.shape[1:]
    peers = lax.axis_size("lon")
    count = lax.axis_size("lev")
    seat = lax.axis_index("lev").astype(jnp.int32)[None]
    cot, vw = to_rows(cotangent), to_rows(vertical_wind)
    polar_cot = jnp.swapaxes(polar_cut(cotangent), 2, 3)
    polar_vw = jnp.swapaxes(polar_cut(vertical_wind), 1, 2)
    polar_got = ask_levels(polar_cot, polar_vw)
    ends_cot, ends_vw = cotangent[:, :, :: lon_dev - 1], vertical_wind[:, :: lon_dev - 1]
    ends_got = ask_levels(ends_cot, ends_vw)

    sends = edges_of(seat, cot, vw, levels, count == 2)
    polar_got, ends_got, sends = lax.optimization_barrier((polar_got, ends_got, sends))
    if count == 2:
        edges = [lax.ppermute(sends[0], "lev", [(0, 1), (1, 0)])]
    else:
        edges = [
            lax.ppermute(sends[0], "lev", [(i + 1, i) for i in range(count - 1)]),
            lax.ppermute(sends[1], "lev", [(i, i + 1) for i in range(count - 1)]),
            later_sum(sends[2]),
        ]
    polar = adjoint_part(polar_cot, polar_vw, *polar_got)
    ends_adj = adjoint_part(ends_cot, ends_vw, *ends_got)

    rows = 2 * POLAR // peers
    grouped = polar.reshape(5 * levels, peers, rows, lon_dev)
    grouped = jnp.swapaxes(grouped, 0, 1).reshape(peers, 5 * levels * rows, lon_dev)

    pack = jnp.concatenate([ends_adj.reshape(5 * levels, 2, lat), zonal_coef[:, :: lon_dev - 1]], 0)
    up = [(i, (i + 1) % peers) for i in range(peers)]
    down = [(j, i) for i, j in up]
    beyond = jnp.stack([lax.ppermute(pack[:, 1], "lon", up), lax.ppermute(pack[:, 0], "lon", down)], 1)
    halo_adj = beyond[: 5 * levels].reshape(5, levels, 2, lat)
    halo_zc = beyond[5 * levels :]

    smoothed = polar_filter(grouped, cutoff, peers)
    smoothed = smoothed.reshape(2, peers // 2, 5, levels, rows, lon_dev + 2)
    smoothed = smoothed.transpose(2, 5, 0, 3, 1, 4).reshape(5, lon_dev + 2, 2, levels, POLAR)
    north, south = smoothed[:, :, 0], smoothed[:, :, 1]
    gap = ((0, 0), (0, 0), (0, 0))
    smooth = jnp.concatenate(
        [jnp.pad(north, (*gap, (0, 128 - POLAR))), jnp.pad(south, (*gap, (128 - POLAR, 0)))], 2
    )[:, 1 : lon_dev + 1]
    outer = [jnp.swapaxes(x[:, :: lon_dev + 1], 1, 2) for x in (north, south)]
    halo_f = jnp.concatenate([outer[0], halo_adj[..., POLAR : lat - POLAR], outer[1]], 3)
    halo = jnp.stack(coupled(halo_zc, [halo_f[f] for f in range(5)], 0))
    out = stencil(
        seat, cot, vw, to_rows(zonal_coef), to_rows(merid_coef), smooth, to_rows(halo), edges, levels
    )
    return from_rows(out, levels)


def lane_of(shape):
    return lax.broadcasted_iota(jnp.int32, shape, len(shape) - 1)


def pair_up(a, b, lane):
    inner = jnp.where(lane < 64, pltpu.roll(b, POLAR, 1), pltpu.roll(b, 128 - POLAR, 1))
    return jnp.where((lane >= POLAR) & (lane < 128 - POLAR), inner, a)


def second_of(pair, lane):
    return jnp.where(lane < 64, pltpu.roll(pair, 128 - POLAR, 1), pltpu.roll(pair, POLAR, 1))


def polar_level(levels, north, south, k, lane):
    lon, rows, _ = north.shape
    near = north.reshape(lon * rows, 128)[pl.ds(k, lon, stride=rows), :]
    far = south.reshape(lon * rows, 128)[pl.ds(levels + k, lon, stride=rows), :]
    return jnp.where(lane < 64, near, far)


def polar_specs(lon, rows, levels):
    wide = 2 * levels
    last = rows // wide - 1
    return [
        pl.BlockSpec((1, lon, wide, 128), lambda f, s: (f, 0, 0, 0)),
        pl.BlockSpec((1, lon, wide, 128), lambda f, s: (f, 0, last, 0)),
        pl.BlockSpec((lon, wide, 128), lambda f, s: (0, 0, 0)),
        pl.BlockSpec((lon, wide, 128), lambda f, s: (0, last, 0)),
    ]


def polar_send_kernel(levels, seat, cn, cs, vn, vs, out):
    lon = vn.shape[0]
    lane = lane_of((lon, 128))
    f = pl.program_id(0)

    def product(k):
        return polar_level(levels, cn.at[0], cs.at[0], k, lane) * polar_level(levels, vn, vs, k, lane)

    w = jnp.where(seat[0] == 0, -product(levels - 1), product(0))

    @pl.when(f == 2)
    def _():
        total = polar_level(levels, cn.at[0], cs.at[0], 0, lane)
        for k in range(1, levels):
            total = total + polar_level(levels, cn.at[0], cs.at[0], k, lane)
        out[2] = jnp.where(seat[0] == 0, 0.0, total)

    for i in range(5):

        @pl.when(f == i)
        def _(i=i):
            if i == 4:
                out[2] = pair_up(w, out[2], lane)
            elif i % 2:
                out[i // 2] = pair_up(out[i // 2], w, lane)
            else:
                out[i // 2] = w


def polar_send(seat, cot, vw, levels):
    _, lon, rows, _ = cot.shape
    return pl.pallas_call(
        functools.partial(polar_send_kernel, levels),
        out_shape=jax.ShapeDtypeStruct((3, lon, 128), jnp.float32),
        grid_spec=pltpu.PrefetchScalarGridSpec(
            num_scalar_prefetch=1,
            grid=(5,),
            in_specs=polar_specs(lon, rows, levels),
            out_specs=pl.BlockSpec((3, lon, 128), lambda f, s: (0, 0, 0)),
        ),
        compiler_params=pltpu.CompilerParams(vmem_limit_bytes=ROOM),
        cost_estimate=pl.CostEstimate(flops=3_000_000, bytes_accessed=9_000_000, transcendentals=0),
        name="polar_send",
    )(seat, cot, cot, vw, vw)


def prep_kernel(levels, nq, seat, cn, cs, vn, vs, got, x, below, z, zt):
    lon = vn.shape[0]
    span = 2 * POLAR // nq
    half = 5 * span // 2
    lane = lane_of((lon, 128))
    f = pl.program_id(0)

    @pl.when(f == 0)
    def _():
        z[...] = jnp.zeros_like(z)

    def field(i):
        c = [polar_level(levels, cn.at[0], cs.at[0], k, lane) for k in range(levels)]
        w = [c[k] * polar_level(levels, vn, vs, k, lane) for k in range(levels)]
        pair = got[i // 2]
        edge = second_of(pair, lane) if i % 2 else pair
        if i == 2:
            run = second_of(got[2], lane)
            for k in range(levels - 1, -1, -1):
                run = run + c[k]
                below[k] = run
        for k in range(0, levels, 2):
            pieces = []
            for at in (k, k + 1):
                a = c[at]
                if at < levels - 1:
                    a = a + w[at + 1]
                if at > 0:
                    a = a - w[at - 1]
                if at == levels - 1:
                    a = a + jnp.where(seat[0] == 0, edge, 0.0)
                if at == 0:
                    a = a + jnp.where(seat[0] == 0, 0.0, edge)
                if i == 3:
                    a = a - COUPLE_B * below[at]
                pieces.append(a)
            z[:lon] = pair_up(pieces[0], pieces[1], lane)
            zt[...] = z[...].T
            for n, (at, q) in enumerate(slots_of(k, nq)):
                d = at * nq + q
                x[d, i * span : (i + 1) * span] = zt[n * span : (n + 1) * span, :128]
                for h in range(0, span, 8):
                    to = i * span + h
                    end = zt[n * span + h : n * span + h + 8, 128:]
                    if to < half:
                        x[d, 5 * span + to : 5 * span + to + 8] = end
                    else:
                        to += 5 * span - half
                        x[d, to : to + 8] += pltpu.roll(end, 64, 1)

    for i in range(5):
        pl.when(f == i)(functools.partial(field, i))


def slots_of(k, nq):
    north, south = range(nq // 2), range(nq // 2, nq)
    return (
        [(k, q) for q in north] + [(k + 1, q) for q in north]
        + [(k + 1, q) for q in south] + [(k, q) for q in south]
    )


def polar_prep(seat, cot, vw, got, levels, nq):
    _, lon, rows, _ = cot.shape
    span = 2 * POLAR // nq
    shape = (levels * nq, 5 * span + 5 * span // 2, 128)
    return pl.pallas_call(
        functools.partial(prep_kernel, levels, nq),
        out_shape=jax.ShapeDtypeStruct(shape, jnp.float32),
        grid_spec=pltpu.PrefetchScalarGridSpec(
            num_scalar_prefetch=1,
            grid=(5,),
            in_specs=polar_specs(lon, rows, levels)
            + [pl.BlockSpec((3, lon, 128), lambda f, s: (0, 0, 0))],
            out_specs=pl.BlockSpec(shape, lambda f, s: (0, 0, 0)),
            scratch_shapes=[
                pltpu.VMEM((levels, lon, 128), jnp.float32),
                pltpu.VMEM((256, 128), jnp.float32),
                pltpu.VMEM((128, 256), jnp.float32),
            ],
        ),
        compiler_params=pltpu.CompilerParams(vmem_limit_bytes=ROOM),
        cost_estimate=pl.CostEstimate(flops=6_000_000, bytes_accessed=11_000_000, transcendentals=0),
        name="polar_prep",
    )(seat, cot, cot, vw, vw, got)


def wave_kernel(
    peers, x_ref, fwd_ref, inv_ref, ct_ref, st_ref, mask_ref, out_ref, held, made,
    own_sem, send_a, recv_a, send_b, recv_b,
):
    me = lax.axis_index("lon")
    kpad = ct_ref.shape[2]
    cols = x_ref.shape[1] // 3 * 2
    half = cols // 2
    barrier = pltpu.get_barrier_semaphore()

    def greet(o, _):
        pl.semaphore_signal(
            barrier, inc=1, device_id={"lon": lax.rem(me + o, peers)}, device_id_type=MESH
        )
        return 0

    lax.fori_loop(1, peers, greet, 0)
    pl.semaphore_wait(barrier, peers - 1)

    def ahead(o):
        return lax.rem(me + o, peers)

    def behind(o):
        return lax.rem(me + peers - o, peers)

    def out_copy(d):
        return pltpu.make_async_remote_copy(
            src_ref=x_ref.at[d], dst_ref=held.at[me], send_sem=send_a.at[d],
            recv_sem=recv_a.at[me], device_id={"lon": d}, device_id_type=MESH,
        )

    def in_copy(s):
        return pltpu.make_async_remote_copy(
            src_ref=x_ref.at[s], dst_ref=held.at[s], send_sem=send_a.at[s],
            recv_sem=recv_a.at[s], device_id={"lon": s}, device_id_type=MESH,
        )

    def back_copy(d):
        return pltpu.make_async_remote_copy(
            src_ref=made.at[d], dst_ref=out_ref.at[me], send_sem=send_b.at[d],
            recv_sem=recv_b.at[me], device_id={"lon": d}, device_id_type=MESH,
        )

    def home_copy(s):
        return pltpu.make_async_remote_copy(
            src_ref=made.at[s], dst_ref=out_ref.at[s], send_sem=send_b.at[s],
            recv_sem=recv_b.at[s], device_id={"lon": s}, device_id_type=MESH,
        )

    lax.fori_loop(1, peers, lambda o, c: (out_copy(ahead(o)).start(), c)[1], 0)
    own = pltpu.make_async_copy(x_ref.at[me], held.at[me], own_sem)
    own.start()
    own.wait()
    zero = jnp.zeros((cols, kpad), jnp.float32)
    dot = functools.partial(jnp.dot, precision=HIGHEST, preferred_element_type=jnp.float32)

    def gather(s, carry):
        a, b = carry
        ends = held[s, cols:]
        ends = jnp.concatenate([ends[:, :64], ends[:, 64:]], 0)
        both = dot(held[s, :cols], fwd_ref[:128]) + dot(ends, fwd_ref[128:])
        c, v = both[:, :kpad], both[:, kpad:]
        ct, st = ct_ref[s], st_ref[s]
        return a + (ct * c - st * v), b + (st * c + ct * v)

    def arrive(o, carry):
        s = behind(o)
        in_copy(s).wait_recv()
        return gather(s, carry)

    a, b = lax.fori_loop(1, peers, arrive, gather(me, (zero, zero)))
    mask = jnp.concatenate([mask_ref[...]] * 5, 0)
    a = a * mask
    b = b * mask

    def spread(d):
        ct, st = ct_ref[d], st_ref[d]
        p, q = a * ct + b * st, b * ct - a * st
        y = dot(p, inv_ref[0]) + dot(q, inv_ref[1])
        made[d, :cols] = y[:, :128]
        made[d, cols:] = jnp.concatenate([y[:half, 128:], y[half:, 128:]], 1)

    def depart(o, _):
        spread(ahead(o))
        pl.when(o > 1)(lambda: back_copy(ahead(o - 1)).start())
        return 0

    lax.fori_loop(1, peers, depart, 0)
    spread(me)
    back_copy(ahead(peers - 1)).start()
    mine = pltpu.make_async_copy(made.at[me], out_ref.at[me], own_sem)
    mine.start()
    mine.wait()
    lax.fori_loop(1, peers, lambda o, c: (home_copy(behind(o)).wait_recv(), c)[1], 0)
    lax.fori_loop(1, peers, lambda o, c: (out_copy(ahead(o)).wait_send(), c)[1], 0)
    lax.fori_loop(1, peers, lambda o, c: (back_copy(ahead(o)).wait_send(), c)[1], 0)


def polar_waves(x, cutoff, lon_dev, peers, nq):
    nlon = peers * lon_dev
    span = cutoff.shape[0] // nq
    kpad = (KMAX + 1 + 127) // 128 * 128
    wave = np.arange(kpad)
    fwd = np.concatenate(angles(np.arange(lon_dev)[:, None], wave[None, :], nlon), axis=1)
    inv = np.stack(angles(wave[:, None], np.arange(lon_dev)[None, :], nlon))
    short = 192 - lon_dev
    fwd = np.pad(fwd, ((0, short), (0, 0)))
    inv = np.pad(inv, ((0, 0), (0, 0), (0, short)))
    ct, st = angles(np.arange(peers)[:, None, None] * lon_dev, wave[None, None, :], nlon)
    mine = lax.dynamic_slice_in_dim(cutoff, lax.axis_index("lon") % nq * span, span)
    weight = np.where(wave == 0, 1.0 / nlon, 2.0 / nlon).astype(np.float32)
    mask = jnp.where(jnp.asarray(wave, jnp.int32)[None, :] <= mine[:, None], weight[None, :], 0.0)
    vmem = pl.BlockSpec(memory_space=pltpu.VMEM)
    dma = pltpu.SemaphoreType.DMA
    return pl.pallas_call(
        functools.partial(wave_kernel, peers),
        out_shape=jax.ShapeDtypeStruct(x.shape, jnp.float32),
        in_specs=[vmem] * 6,
        out_specs=vmem,
        scratch_shapes=[
            pltpu.VMEM(x.shape, jnp.float32),
            pltpu.VMEM(x.shape, jnp.float32),
            dma(()), dma((peers,)), dma((peers,)), dma((peers,)), dma((peers,)),
        ],
        compiler_params=pltpu.CompilerParams(
            collective_id=1, has_side_effects=True, vmem_limit_bytes=24 << 20
        ),
        cost_estimate=pl.CostEstimate(flops=8_000_000_000, bytes_accessed=60_000_000, transcendentals=0),
        name="polar_waves",
    )(x, fwd, inv, ct, st, mask)


def post_kernel(levels, nq, lon, y, out, zt, z):
    span = 2 * POLAR // nq
    half = 5 * span // 2
    wide = 2 * levels
    flat = out.at[0].reshape(lon * wide, 128)
    f = pl.program_id(0)

    def field(i):
        for k in range(0, levels, 2):
            for n, (at, q) in enumerate(slots_of(k, nq)):
                d = at * nq + q
                zt[n * span : (n + 1) * span, :128] = y[d, i * span : (i + 1) * span]
                for h in range(0, span, 8):
                    to = i * span + h
                    if to < half:
                        end = y[d, 5 * span + to : 5 * span + to + 8]
                    else:
                        to += 5 * span - half
                        end = pltpu.roll(y[d, to : to + 8], 64, 1)
                    zt[n * span + h : n * span + h + 8, 128:] = end
            z[...] = zt[...].T
            first = z[:lon]
            flat[pl.ds(k, lon, stride=wide), :] = first
            flat[pl.ds(levels + k, lon, stride=wide), :] = first
            flat[pl.ds(k + 1, lon, stride=wide), :] = pltpu.roll(first, 128 - POLAR, 1)
            flat[pl.ds(levels + k + 1, lon, stride=wide), :] = pltpu.roll(first, POLAR, 1)

    for i in range(5):
        pl.when(f == i)(functools.partial(field, i))


def polar_post(y, lon, levels, nq):
    return pl.pallas_call(
        functools.partial(post_kernel, levels, nq, lon),
        out_shape=jax.ShapeDtypeStruct((5, lon, 2 * levels, 128), jnp.float32),
        grid=(5,),
        in_specs=[pl.BlockSpec(y.shape, lambda f: (0, 0, 0))],
        out_specs=pl.BlockSpec((1, lon, 2 * levels, 128), lambda f: (f, 0, 0, 0)),
        scratch_shapes=[pltpu.VMEM((128, 256), jnp.float32), pltpu.VMEM((256, 128), jnp.float32)],
        compiler_params=pltpu.CompilerParams(vmem_limit_bytes=ROOM),
        cost_estimate=pl.CostEstimate(flops=1_000_000, bytes_accessed=5_000_000, transcendentals=0),
        name="polar_post",
    )(y)


def edge_part(seat, cot, vw, levels, at, steps, chunk):
    fields, lon, rows, _ = cot.shape
    tiles = rows // levels
    return pl.pallas_call(
        functools.partial(edge_kernel, levels, True),
        out_shape=[jax.ShapeDtypeStruct((fields + 1, steps * chunk, tiles, 128), jnp.float32)],
        grid_spec=pltpu.PrefetchScalarGridSpec(
            num_scalar_prefetch=1,
            grid=(steps,),
            in_specs=[
                pl.BlockSpec((fields, chunk, rows, 128), lambda g, s: (0, at(g), 0, 0)),
                pl.BlockSpec((chunk, rows, 128), lambda g, s: (at(g), 0, 0)),
            ],
            out_specs=[pl.BlockSpec((fields + 1, chunk, tiles, 128), lambda g, s: (0, g, 0, 0))],
        ),
        compiler_params=pltpu.CompilerParams(vmem_limit_bytes=ROOM),
        cost_estimate=pl.CostEstimate(
            flops=50_000 * steps * chunk, bytes_accessed=120_000 * steps * chunk, transcendentals=0
        ),
        name="edge_part",
    )(seat, cot, vw)[0]


def column_maker(levels, seat, cot, vw, smooth, edges, spread, below_ref):
    _, _, rows, _ = cot.shape
    tiles = rows // levels
    edge_at = (1 - seat[0]) * (levels - 1)
    row = lax.broadcasted_iota(jnp.int32, (rows, 128), 0)
    k = lax.rem(row, levels)
    cap_lane = lax.broadcasted_iota(jnp.int32, (2 * levels, 128), 1)
    cap_row = lax.broadcasted_iota(jnp.int32, (2 * levels, 128), 0)
    north = (cap_row < levels) & (cap_lane < POLAR)
    south = (cap_row >= levels) & (cap_lane >= 128 - POLAR)

    def column(l):
        for f in range(5):
            spread[f, pl.ds(edge_at, tiles, stride=levels), :] = edges[f, l]
        for at in range(levels):
            below_ref[pl.ds(at, tiles, stride=levels), :] = edges[5, l]
        wind = vw[l]
        base, fields = [], []
        for f in range(5):
            c = cot[f, l]
            w = wind * c
            up = jnp.where(k < levels - 1, pltpu.roll(w, rows - 1, 0), 0.0)
            a = c + (up - jnp.where(k > 0, pltpu.roll(w, 1, 0), 0.0))
            a = a + spread[f]
            if f == 3:
                theta = cot[2, l]
                below = below_ref[...] + theta
                for r in range(1, levels):
                    below = below + jnp.where(k < levels - r, pltpu.roll(theta, rows - r, 0), 0.0)
                a = a - COUPLE_B * below
            base.append(a)
            s = smooth[f, l]
            top = jnp.where(north, s, a[: 2 * levels])
            low = jnp.where(south, s, a[rows - 2 * levels :])
            fields.append(jnp.concatenate([top, a[2 * levels : rows - 2 * levels], low], 0))
        return base, fields

    return column


def border_kernel(levels, seat, cot, vw, zc, smooth, edges, out, spread, below_ref):
    @pl.when(pl.program_id(0) == 0)
    def _():
        spread[...] = jnp.zeros_like(spread)

    _, fields = column_maker(levels, seat, cot, vw, smooth, edges, spread, below_ref)(0)
    zonal = coupled(zc[0], fields, 0)
    for f in range(5):
        out[0, f] = zonal[f]


def borders(seat, cot, vw, zc, smooth, edges, levels):
    _, lon, rows, _ = cot.shape
    tiles = rows // levels
    field = lambda n: pl.BlockSpec((5, 1, n, 128), lambda g, s: (0, g * (lon - 1), 0, 0))
    plain = pl.BlockSpec((1, rows, 128), lambda g, s: (g * (lon - 1), 0, 0))
    return pl.pallas_call(
        functools.partial(border_kernel, levels),
        out_shape=jax.ShapeDtypeStruct((2, 5, rows, 128), jnp.float32),
        grid_spec=pltpu.PrefetchScalarGridSpec(
            num_scalar_prefetch=1,
            grid=(2,),
            in_specs=[field(rows), plain, plain, field(2 * levels),
                      pl.BlockSpec((6, 1, tiles, 128), lambda g, s: (0, g, 0, 0))],
            out_specs=pl.BlockSpec((1, 5, rows, 128), lambda g, s: (g, 0, 0, 0)),
            scratch_shapes=[
                pltpu.VMEM((5, rows, 128), jnp.float32),
                pltpu.VMEM((rows, 128), jnp.float32),
            ],
        ),
        compiler_params=pltpu.CompilerParams(vmem_limit_bytes=ROOM),
        cost_estimate=pl.CostEstimate(flops=1_000_000, bytes_accessed=500_000, transcendentals=0),
        name="borders",
    )(seat, cot, vw, zc, smooth, edges)


def strip_kernel(levels, start, steps, first, last, seat, cot, vw, zc, mc, smooth, edges, *rest):
    rest = list(rest)
    if first:
        left = rest.pop(0)
    else:
        wait_in, prior_in, _ = rest.pop(0), rest.pop(0), rest.pop(0)
    if last:
        right = rest.pop(0)
    out, wait, prior, ready, spread, below_ref, sems = rest[:7]
    _, chunk, rows, _ = cot.shape
    g = pl.program_id(0)
    slot = lax.rem(g, 2)
    lane = lax.broadcasted_iota(jnp.int32, (rows, 128), 1)
    row = lax.broadcasted_iota(jnp.int32, (rows, 128), 0)

    def first_copy():
        return pltpu.make_async_copy(
            ready.at[0, :, pl.ds(1, chunk - 1)], out.at[:, pl.ds(0, chunk - 1)], sems.at[0]
        )

    def copy(at):
        s = lax.rem(at, 2)
        return pltpu.make_async_copy(
            ready.at[s], out.at[:, pl.ds(start + at * chunk - 1, chunk)], sems.at[s]
        )

    def act(at, what):
        if first:
            pl.when(at == 0)(lambda: getattr(first_copy(), what)())
            pl.when(at > 0)(lambda: getattr(copy(at), what)())
        else:
            getattr(copy(at), what)()

    @pl.when(g == 0)
    def _():
        spread[...] = jnp.zeros_like(spread)
        if first:
            prior[...] = left[...]
            wait[...] = jnp.zeros_like(wait)
        else:
            prior[...] = prior_in[...]
            wait[...] = wait_in[...]

    pl.when(g >= 2)(lambda: act(g - 2, "wait"))
    column = column_maker(levels, seat, cot, vw, smooth, edges, spread, below_ref)

    def one(l, _):
        base, fields = column(l)
        zonal = coupled(zc[l], fields, 0)
        merid = coupled(mc[l], fields, 1)
        for f in range(5):
            ready[slot, f, l] = wait[f] + zonal[f]
            near = pltpu.roll(merid[f], 1, 1)
            over = jnp.where(row < levels, 0.0, pltpu.roll(near, levels, 0))
            near = jnp.where(lane == 0, over, near)
            far = pltpu.roll(merid[f], 127, 1)
            over = jnp.where(row >= rows - levels, 0.0, pltpu.roll(far, rows - levels, 0))
            far = jnp.where(lane == 127, over, far)
            wait[f] = base[f] + (far - near) - prior[f]
            prior[f] = zonal[f]
        return 0

    lax.fori_loop(0, chunk, one, 0)
    act(g, "start")

    @pl.when(g == steps - 1)
    def _():
        if last:
            final, last_sem = rest[7:]
            for f in range(5):
                final[f, 0] = wait[f] + right[f]
            end = pltpu.make_async_copy(
                final, out.at[:, pl.ds(start + steps * chunk - 1, 1)], last_sem
            )
            end.start()
        if steps > 1:
            act(g - 1, "wait")
        act(g, "wait")
        if last:
            end.wait()


def strip(seat, cot, vw, zc, mc, smooth, edges, state, right, levels, start, steps, chunk):
    _, lon, rows, _ = cot.shape
    tiles = rows // levels
    at = start // chunk
    first, last = len(state) == 1, right is not None
    field = lambda n: pl.BlockSpec((5, chunk, n, 128), lambda g, s: (0, at + g, 0, 0))
    plain = pl.BlockSpec((chunk, rows, 128), lambda g, s: (at + g, 0, 0))
    whole = pl.BlockSpec((5, rows, 128), lambda g, s: (0, 0, 0))
    place = pl.BlockSpec(memory_space=pl.ANY)
    in_specs = [field(rows), plain, plain, plain, field(2 * levels),
                pl.BlockSpec((6, chunk, tiles, 128), lambda g, s: (0, g, 0, 0))]
    in_specs += [whole] if first else [whole, whole, place]
    args = [seat, cot, vw, zc, mc, smooth, edges, *state]
    aliases = {} if first else {len(args) - 1: 0}
    if last:
        in_specs.append(whole)
        args.append(right)
    one = jax.ShapeDtypeStruct((5, rows, 128), jnp.float32)
    held = [pltpu.VMEM((5, rows, 128), jnp.float32)] * 2
    scratch = [
        pltpu.VMEM((2, 5, chunk, rows, 128), jnp.float32),
        pltpu.VMEM((5, rows, 128), jnp.float32),
        pltpu.VMEM((rows, 128), jnp.float32),
        pltpu.SemaphoreType.DMA((2,)),
    ]
    if last:
        scratch = held + scratch + [
            pltpu.VMEM((5, 1, rows, 128), jnp.float32), pltpu.SemaphoreType.DMA(()),
        ]
    got = pl.pallas_call(
        functools.partial(strip_kernel, levels, start, steps, first, last),
        out_shape=[jax.ShapeDtypeStruct(cot.shape, jnp.float32)] + ([] if last else [one, one]),
        grid_spec=pltpu.PrefetchScalarGridSpec(
            num_scalar_prefetch=1,
            grid=(steps,),
            in_specs=in_specs,
            out_specs=[place] + ([] if last else [whole, whole]),
            scratch_shapes=scratch,
        ),
        input_output_aliases=aliases,
        compiler_params=pltpu.CompilerParams(vmem_limit_bytes=ROOM),
        cost_estimate=pl.CostEstimate(
            flops=30 * 5 * steps * chunk * rows * 128,
            bytes_accessed=4 * 14 * steps * chunk * rows * 128,
            transcendentals=0,
        ),
        name="strip",
    )(*args)
    return got[0] if last else [got[1], got[2], got[0]]


def parts_of(steps):
    cuts = sorted({round(steps * share) for share in (0.23, 0.45, 0.67, 0.84, 0.95, 1.0)} - {0})
    return list(zip([0] + cuts[:-1], cuts))


def fast_body(cotangent, zonal_coef, merid_coef, vertical_wind, cutoff):
    levels, lon_dev, lat = cotangent.shape[1:]
    peers = lax.axis_size("lon")
    nq = peers // levels
    seat = lax.axis_index("lev").astype(jnp.int32)[None]
    cot, vw = to_rows(cotangent), to_rows(vertical_wind)
    zc, mc = to_rows(zonal_coef), to_rows(merid_coef)
    trade = lambda a: lax.ppermute(a, "lev", [(0, 1), (1, 0)])

    sent = polar_send(seat, cot, vw, levels)
    polar_got = trade(sent)
    ends = edge_part(seat, cot, vw, levels, lambda g: g * (lon_dev - 1), 2, 1)
    ends_got = trade(ends)
    chunk = max(d for d in range(2, 13) if lon_dev % d == 0)
    parts = parts_of(lon_dev // chunk)
    token, edges = seat, []
    token, _ = lax.optimization_barrier((token, sent))
    for a, b in parts:
        part = edge_part(token, cot, vw, levels, lambda g, a=a: a + g, b - a, chunk)
        edges.append(trade(part))
        token, _ = lax.optimization_barrier((token, part))

    polar_got, ends_got, token = lax.optimization_barrier((polar_got, ends_got, token))
    x = polar_prep(token, cot, vw, polar_got, levels, nq)
    y = polar_waves(x, cutoff, lon_dev, peers, nq)
    smooth = polar_post(y, lon_dev, levels, nq)
    flux = borders(seat, cot, vw, zc, smooth, ends_got, levels)
    up = [(i, (i + 1) % peers) for i in range(peers)]
    left = lax.ppermute(flux[1], "lon", up)
    right = lax.ppermute(flux[0], "lon", [(j, i) for i, j in up])
    state = [left]
    for n, (a, b) in enumerate(parts):
        end = right if n == len(parts) - 1 else None
        state = strip(
            seat, cot, vw, zc, mc, smooth, edges[n], state, end, levels, a * chunk, b - a, chunk
        )
    return from_rows(state, levels)


def body(cotangent, zonal_coef, merid_coef, vertical_wind, cutoff):
    levels, lon_dev, lat = cotangent.shape[1:]
    peers, count = lax.axis_size("lon"), lax.axis_size("lev")
    span = 2 * POLAR * levels // peers
    fast = (
        count == 2 and levels * 2 == 8 and peers % (2 * levels) == 0 and lat % 256 == 0
        and span % 16 == 0 and 128 < lon_dev <= 192 and cutoff.shape[0] == 2 * POLAR
    )
    return (fast_body if fast else plain_body)(
        cotangent, zonal_coef, merid_coef, vertical_wind, cutoff
    )


def solution(mesh):
    return jax.shard_map(
        body,
        mesh=mesh,
        in_specs=(
            P(None, "lev", "lon", None),
            P("lev", "lon", None),
            P("lev", "lon", None),
            P("lev", "lon", None),
            P(),
        ),
        out_specs=P(None, "lev", "lon", None),
        check_vma=False,
    )
```

```python
import functools
import math

import jax
import jax.numpy as jnp
import numpy as np
from jax import lax
from jax.experimental import pallas as pl
from jax.experimental.pallas import tpu as pltpu
from jax.sharding import PartitionSpec as P

POLAR = 32
KMAX = 360
COUPLE_G = 0.3
COUPLE_H = 0.3
COUPLE_B = 0.2
MESH = pl.DeviceIdType.MESH
HIGHEST = lax.Precision.HIGHEST
ROOM = 61 << 20
SOME = 36 << 20


def angles(left, right, period):
    phase = (left * right) % period * (2.0 * math.pi / period)
    return np.cos(phase).astype(np.float32), np.sin(phase).astype(np.float32)


def filter_kernel(
    peers, packed, x_ref, fwd_ref, inv_ref, ct_ref, st_ref, mask_ref, out_ref, held, made,
    own_sem, send_a, recv_a, send_b, recv_b,
):
    me = lax.axis_index("lon")
    kpad = ct_ref.shape[2]
    barrier = pltpu.get_barrier_semaphore()

    def greet(o, _):
        pl.semaphore_signal(
            barrier, inc=1, device_id={"lon": lax.rem(me + o, peers)}, device_id_type=MESH
        )
        return 0

    lax.fori_loop(1, peers, greet, 0)
    pl.semaphore_wait(barrier, peers - 1)

    def out_copy(o):
        d = lax.rem(me + o, peers)
        return pltpu.make_async_remote_copy(
            src_ref=x_ref.at[d], dst_ref=held.at[me], send_sem=send_a.at[d],
            recv_sem=recv_a.at[me], device_id={"lon": d}, device_id_type=MESH,
        )

    def in_copy(o):
        s = lax.rem(me + o, peers)
        return pltpu.make_async_remote_copy(
            src_ref=x_ref.at[s], dst_ref=held.at[s], send_sem=send_a.at[s],
            recv_sem=recv_a.at[s], device_id={"lon": s}, device_id_type=MESH,
        )

    def back_copy(o):
        d = lax.rem(me + o, peers)
        return pltpu.make_async_remote_copy(
            src_ref=made.at[d], dst_ref=out_ref.at[me], send_sem=send_b.at[d],
            recv_sem=recv_b.at[me], device_id={"lon": d}, device_id_type=MESH,
        )

    def home_copy(o):
        s = lax.rem(me + o, peers)
        return pltpu.make_async_remote_copy(
            src_ref=made.at[s], dst_ref=out_ref.at[s], send_sem=send_b.at[s],
            recv_sem=recv_b.at[s], device_id={"lon": s}, device_id_type=MESH,
        )

    lax.fori_loop(1, peers, lambda o, c: (out_copy(o).start(), c)[1], 0)
    own = pltpu.make_async_copy(x_ref.at[me], held.at[me], own_sem)
    own.start()
    own.wait()
    cols = mask_ref.shape[0]
    half = cols // 2
    zero = jnp.zeros((cols, kpad), jnp.float32)
    dot = functools.partial(jnp.dot, precision=HIGHEST, preferred_element_type=jnp.float32)

    def gather(s, carry):
        a, b = carry
        if packed:
            ends = held[s, cols:]
            ends = jnp.concatenate([ends[:, :64], ends[:, 64:]], 0)
            both = dot(held[s, :cols], fwd_ref[:128]) + dot(ends, fwd_ref[128:])
        else:
            both = dot(held[s], fwd_ref[...])
        c, v = both[:, :kpad], both[:, kpad:]
        ct, st = ct_ref[s], st_ref[s]
        return a + (ct * c - st * v), b + (st * c + ct * v)

    def arrive(o, carry):
        in_copy(o).wait_recv()
        return gather(lax.rem(me + o, peers), carry)

    a, b = lax.fori_loop(1, peers, arrive, gather(me, (zero, zero)))
    a = a * mask_ref[...]
    b = b * mask_ref[...]

    def spread(d):
        ct, st = ct_ref[d], st_ref[d]
        p, q = a * ct + b * st, b * ct - a * st
        if packed:
            y = dot(p, inv_ref[0]) + dot(q, inv_ref[1])
            made[d, :cols] = y[:, :128]
            made[d, cols:] = jnp.concatenate([y[:half, 128:], y[half:, 128:]], 1)
        else:
            made[d] = dot(p, inv_ref[0]) + dot(q, inv_ref[1])

    def depart(o, _):
        spread(lax.rem(me + o, peers))
        pl.when(o > 1)(lambda: back_copy(o - 1).start())
        return 0

    lax.fori_loop(1, peers, depart, 0)
    spread(me)
    back_copy(peers - 1).start()
    mine = pltpu.make_async_copy(made.at[me], out_ref.at[me], own_sem)
    mine.start()
    mine.wait()
    lax.fori_loop(1, peers, lambda o, c: (home_copy(o).wait_recv(), c)[1], 0)
    lax.fori_loop(1, peers, lambda o, c: (out_copy(o).wait_send(), c)[1], 0)
    lax.fori_loop(1, peers, lambda o, c: (back_copy(o).wait_send(), c)[1], 0)


def polar_filter(x, cutoff, peers):
    _, cols, lon_dev = x.shape
    nlon = peers * lon_dev
    rows = cutoff.shape[0] // peers
    kpad = (KMAX + 1 + 127) // 128 * 128
    wave = np.arange(kpad)
    fwd = np.concatenate(angles(np.arange(lon_dev)[:, None], wave[None, :], nlon), axis=1)
    inv = np.stack(angles(wave[:, None], np.arange(-1, lon_dev + 1)[None, :] % nlon, nlon))
    over, wider = lon_dev - 128, lon_dev + 2 - 128
    packed = over > 0 and wider <= 64 and cols % 16 == 0
    half = cols // 2
    if packed:
        fwd = np.pad(fwd, ((0, 64 - over), (0, 0)))
        inv = np.pad(inv, ((0, 0), (0, 0), (0, 64 - wider)))
        ends = jnp.pad(x[..., 128:], ((0, 0), (0, 0), (0, 64 - over)))
        x = jnp.concatenate([x[..., :128], jnp.concatenate([ends[:, :half], ends[:, half:]], 2)], 1)
        shape = (peers, cols + half, 128)
    else:
        shape = (peers, cols, lon_dev + 2)
    ct, st = angles(np.arange(peers)[:, None, None] * lon_dev, wave[None, None, :], nlon)
    mine = lax.dynamic_slice_in_dim(cutoff, lax.axis_index("lon") * rows, rows)
    weight = np.where(wave == 0, 1.0 / nlon, 2.0 / nlon).astype(np.float32)
    mask = jnp.where(jnp.asarray(wave, jnp.int32)[None, :] <= mine[:, None], weight[None, :], 0.0)
    mask = jnp.tile(mask, (cols // rows, 1))
    vmem = pl.BlockSpec(memory_space=pltpu.VMEM)
    dma = pltpu.SemaphoreType.DMA
    y = pl.pallas_call(
        functools.partial(filter_kernel, peers, packed),
        out_shape=jax.ShapeDtypeStruct(shape, jnp.float32),
        in_specs=[vmem] * 6,
        out_specs=vmem,
        scratch_shapes=[
            pltpu.VMEM(x.shape, jnp.float32),
            pltpu.VMEM(shape, jnp.float32),
            dma(()), dma((peers,)), dma((peers,)), dma((peers,)), dma((peers,)),
        ],
        compiler_params=pltpu.CompilerParams(
            collective_id=0, has_side_effects=True, vmem_limit_bytes=24 << 20
        ),
        cost_estimate=pl.CostEstimate(flops=8_000_000_000, bytes_accessed=60_000_000, transcendentals=0),
        name="polar_filter",
    )(x, fwd, inv, ct, st, mask)
    if not packed:
        return y
    ends = jnp.concatenate([y[:, cols:, :wider], y[:, cols:, 64 : 64 + wider]], 1)
    return jnp.concatenate([y[:, :cols], ends], 2)


def to_rows(x):
    *lead, levels, lon, lat = x.shape
    n = len(lead)
    x = x.reshape(*lead, levels, lon, lat // 128, 128)
    x = x.transpose(*range(n), n + 1, n + 2, n, n + 3)
    return x.reshape(*lead, lon, lat // 128 * levels, 128)


def from_rows(x, levels):
    *lead, lon, rows, _ = x.shape
    n = len(lead)
    x = x.reshape(*lead, lon, rows // levels, levels, 128)
    x = x.transpose(*range(n), n + 2, n, n + 1, n + 3)
    return x.reshape(*lead, levels, lon, rows // levels * 128)


def chunk_of(lon):
    return max(d for d in range(1, 21) if lon % d == 0)


def edge_kernel(levels, choose, seat, cot, vw, *outs):
    fields, chunk, rows, _ = cot.shape
    tiles = rows // levels
    flat_c = cot.reshape(fields * chunk * rows, 128)
    flat_v = vw.reshape(chunk * rows, 128)
    sends = outs[: 1 if choose else 2]

    def level(ref, count, k):
        return ref[pl.ds(k, count * tiles, stride=levels), :] if levels > 1 else ref[...]

    def product(k, sign, out):
        c = level(flat_c, fields * chunk, k).reshape(fields, chunk, tiles, 128)
        v = level(flat_v, chunk, k).reshape(1, chunk, tiles, 128)
        out[:fields] = sign * (v * c)

    flat_t = cot.at[2].reshape(chunk * rows, 128)
    total = level(flat_t, chunk, 0)
    for k in range(1, levels):
        total = total + level(flat_t, chunk, k)
    total = total.reshape(chunk, tiles, 128)
    if choose:
        sends[0][fields] = jnp.where(seat[0] == 0, 0.0, total)
        pl.when(seat[0] == 0)(lambda: product(levels - 1, -1.0, sends[0]))
        pl.when(seat[0] != 0)(lambda: product(0, 1.0, sends[0]))
    else:
        product(0, 1.0, sends[0])
        product(levels - 1, -1.0, sends[1])
        outs[2][...] = total


def edges_of(seat, cot, vw, levels, choose):
    fields, lon, rows, _ = cot.shape
    tiles = rows // levels
    chunk = chunk_of(lon)
    n = 1 if choose else 2
    wide = fields + 1 if choose else fields
    return pl.pallas_call(
        functools.partial(edge_kernel, levels, choose),
        out_shape=[jax.ShapeDtypeStruct((wide, lon, tiles, 128), jnp.float32)] * n
        + [jax.ShapeDtypeStruct((lon, tiles, 128), jnp.float32)] * (n - 1),
        grid_spec=pltpu.PrefetchScalarGridSpec(
            num_scalar_prefetch=1,
            grid=(lon // chunk,),
            in_specs=[
                pl.BlockSpec((fields, chunk, rows, 128), lambda g, s: (0, g, 0, 0)),
                pl.BlockSpec((chunk, rows, 128), lambda g, s: (g, 0, 0)),
            ],
            out_specs=[pl.BlockSpec((wide, chunk, tiles, 128), lambda g, s: (0, g, 0, 0))] * n
            + [pl.BlockSpec((chunk, tiles, 128), lambda g, s: (g, 0, 0))] * (n - 1),
        ),
        compiler_params=pltpu.CompilerParams(vmem_limit_bytes=24 << 20),
        cost_estimate=pl.CostEstimate(flops=10_000_000, bytes_accessed=22_000_000, transcendentals=0),
        name="edges",
    )(seat, cot, vw)


def coupled(coef, fields, first):
    flux = [coef * f for f in fields]
    flux[first] = flux[first] + COUPLE_H * fields[3]
    flux[3] = flux[3] + COUPLE_G * fields[first]
    return flux


def stencil_kernel(levels, steps, n_edge, seat, cot, vw, zc, mc, smooth, halo, *rest):
    edges = rest[:n_edge]
    tail = edges[0].at[5] if n_edge == 1 else rest[n_edge]
    rest = rest[1:] if n_edge > 1 else rest
    edge_at = (1 - seat[0]) * (levels - 1)
    out, ready, final, wait, prior, spread, below_ref, sems, last_sem = rest[n_edge:]
    _, chunk, rows, _ = cot.shape
    tiles = rows // levels
    g = pl.program_id(0)
    slot = lax.rem(g, 2)
    lane = lax.broadcasted_iota(jnp.int32, (rows, 128), 1)
    row = lax.broadcasted_iota(jnp.int32, (rows, 128), 0)
    k = lax.rem(row, levels)
    cap_lane = lax.broadcasted_iota(jnp.int32, (2 * levels, 128), 1)
    cap_row = lax.broadcasted_iota(jnp.int32, (2 * levels, 128), 0)
    north = (cap_row < levels) & (cap_lane < POLAR)
    south = (cap_row >= levels) & (cap_lane >= 128 - POLAR)

    def first_copy():
        return pltpu.make_async_copy(
            ready.at[0, :, pl.ds(1, chunk - 1)], out.at[:, pl.ds(0, chunk - 1)], sems.at[0]
        )

    def copy(at):
        s = lax.rem(at, 2)
        return pltpu.make_async_copy(
            ready.at[s], out.at[:, pl.ds(at * chunk - 1, chunk)], sems.at[s]
        )

    @pl.when(g == 0)
    def _():
        spread[...] = jnp.zeros_like(spread)
        for f in range(5):
            prior[f] = halo[f, 0]
            wait[f] = jnp.zeros((rows, 128), jnp.float32)

    pl.when(g == 2)(lambda: first_copy().wait())
    pl.when(g > 2)(lambda: copy(g - 2).wait())

    def put(ref, at, value):
        if levels > 1:
            ref[pl.ds(at, tiles, stride=levels), :] = value
        else:
            ref[...] = value

    def one(l, _):
        for f in range(5):
            if n_edge == 1:
                put(spread.at[0, f], edge_at, edges[0][f, l])
            else:
                put(spread.at[0, f], levels - 1, edges[0][f, l])
                put(spread.at[1, f], 0, edges[1][f, l])
        for at in range(levels):
            put(below_ref, at, tail[l])
        wind = vw[l]
        base, fields = [], []
        for f in range(5):
            c = cot[f, l]
            w = wind * c
            a = c
            if levels > 1:
                up = jnp.where(k < levels - 1, pltpu.roll(w, rows - 1, 0), 0.0)
                a = a + (up - jnp.where(k > 0, pltpu.roll(w, 1, 0), 0.0))
            for n in range(n_edge):
                a = a + spread[n, f]
            if f == 3:
                theta = cot[2, l]
                below = below_ref[...] + theta
                for r in range(1, levels):
                    below = below + jnp.where(k < levels - r, pltpu.roll(theta, rows - r, 0), 0.0)
                a = a - COUPLE_B * below
            base.append(a)
            s = smooth[f, l]
            top = jnp.where(north, s, a[: 2 * levels])
            low = jnp.where(south, s, a[rows - 2 * levels :])
            fields.append(jnp.concatenate([top, a[2 * levels : rows - 2 * levels], low], 0))
        zonal = coupled(zc[l], fields, 0)
        merid = coupled(mc[l], fields, 1)
        for f in range(5):
            ready[slot, f, l] = wait[f] + zonal[f]
            left = pltpu.roll(merid[f], 1, 1)
            over = jnp.where(row < levels, 0.0, pltpu.roll(left, levels, 0))
            left = jnp.where(lane == 0, over, left)
            right = pltpu.roll(merid[f], 127, 1)
            over = jnp.where(row >= rows - levels, 0.0, pltpu.roll(right, rows - levels, 0))
            right = jnp.where(lane == 127, over, right)
            wait[f] = base[f] + (right - left) - prior[f]
            prior[f] = zonal[f]
        return 0

    lax.fori_loop(0, chunk, one, 0)
    pl.when(g == 0)(lambda: first_copy().start())
    pl.when(g > 0)(lambda: copy(g).start())

    @pl.when(g == steps - 1)
    def _():
        for f in range(5):
            final[f, 0] = wait[f] + halo[f, 1]
        end = pltpu.make_async_copy(final, out.at[:, pl.ds(steps * chunk - 1, 1)], last_sem)
        end.start()
        copy(g - 1).wait() if steps > 2 else first_copy().wait()
        copy(g).wait()
        end.wait()


def stencil(seat, cot, vw, zc, mc, smooth, halo, edges, levels):
    _, lon, rows, _ = cot.shape
    tiles = rows // levels
    chunk = chunk_of(lon)
    steps = lon // chunk
    field = lambda n: pl.BlockSpec((5, chunk, n, 128), lambda g, s: (0, g, 0, 0))
    plain = lambda n: pl.BlockSpec((chunk, n, 128), lambda g, s: (g, 0, 0))
    return pl.pallas_call(
        functools.partial(stencil_kernel, levels, steps, min(len(edges), 2)),
        out_shape=jax.ShapeDtypeStruct(cot.shape, jnp.float32),
        grid_spec=pltpu.PrefetchScalarGridSpec(
            num_scalar_prefetch=1,
            grid=(steps,),
            in_specs=[field(rows), plain(rows), plain(rows), plain(rows), field(2 * levels),
                      pl.BlockSpec((5, 2, rows, 128), lambda g, s: (0, 0, 0, 0))]
            + [pl.BlockSpec((6, chunk, tiles, 128), lambda g, s: (0, g, 0, 0))]
            if len(edges) == 1
            else [field(rows), plain(rows), plain(rows), plain(rows), field(2 * levels),
                  pl.BlockSpec((5, 2, rows, 128), lambda g, s: (0, 0, 0, 0)),
                  field(tiles), field(tiles), plain(tiles)],
            out_specs=pl.BlockSpec(memory_space=pl.ANY),
            scratch_shapes=[
                pltpu.VMEM((2, 5, chunk, rows, 128), jnp.float32),
                pltpu.VMEM((5, 1, rows, 128), jnp.float32),
                pltpu.VMEM((5, rows, 128), jnp.float32),
                pltpu.VMEM((5, rows, 128), jnp.float32),
                pltpu.VMEM((min(len(edges), 2), 5, rows, 128), jnp.float32),
                pltpu.VMEM((rows, 128), jnp.float32),
                pltpu.SemaphoreType.DMA((2,)),
                pltpu.SemaphoreType.DMA(()),
            ],
        ),
        compiler_params=pltpu.CompilerParams(vmem_limit_bytes=40 << 20),
        cost_estimate=pl.CostEstimate(
            flops=30 * 5 * lon * rows * 128, bytes_accessed=4 * 14 * lon * rows * 128, transcendentals=0
        ),
        name="stencil",
    )(seat, cot, vw, zc, mc, smooth, halo, *edges)


def swap_levels(first, last, total):
    count = lax.axis_size("lev")
    if count == 2:
        seat = lax.axis_index("lev")
        lead = jnp.concatenate([first, total[None]], 0)
        trail = jnp.concatenate([last, jnp.zeros_like(total)[None]], 0)
        got = lax.ppermute(jnp.where(seat == 0, trail, lead), "lev", [(0, 1), (1, 0)])
        return jnp.where(seat == 0, got[:5], 0.0), jnp.where(seat == 1, got[:5], 0.0), got[5]
    up = lax.ppermute(first, "lev", [(i + 1, i) for i in range(count - 1)])
    down = lax.ppermute(last, "lev", [(i, i + 1) for i in range(count - 1)])
    return up, down, later_sum(total)


def later_sum(local):
    count = lax.axis_size("lev")
    total = jnp.zeros_like(local)
    for r in range(1, count):
        total = total + lax.ppermute(local, "lev", [(i + r, i) for i in range(count - r)])
    return total


def ask_levels(cot, vw):
    return swap_levels(vw[0] * cot[:, 0], vw[-1] * cot[:, -1], cot[2].sum(0))


def adjoint_part(cot, vw, up, down, later):
    weighted = vw[None] * cot
    above = jnp.concatenate([weighted[:, 1:], up[:, None]], 1)
    under = jnp.concatenate([down[:, None], weighted[:, :-1]], 1)
    below = [later + cot[2, -1]]
    for k in range(cot.shape[1] - 2, -1, -1):
        below.insert(0, below[0] + cot[2, k])
    parts = cot + (above - under)
    return jnp.concatenate(
        [parts[:3], parts[3:4] - COUPLE_B * jnp.stack(below)[None], parts[4:]], 0
    )


def polar_cut(x):
    return jnp.concatenate([x[..., :POLAR], x[..., x.shape[-1] - POLAR :]], -1)


def plain_body(cotangent, zonal_coef, merid_coef, vertical_wind, cutoff):
    levels, lon_dev, lat = cotangent.shape[1:]
    peers = lax.axis_size("lon")
    count = lax.axis_size("lev")
    seat = lax.axis_index("lev").astype(jnp.int32)[None]
    cot, vw = to_rows(cotangent), to_rows(vertical_wind)
    polar_cot = jnp.swapaxes(polar_cut(cotangent), 2, 3)
    polar_vw = jnp.swapaxes(polar_cut(vertical_wind), 1, 2)
    polar_got = ask_levels(polar_cot, polar_vw)
    ends_cot, ends_vw = cotangent[:, :, :: lon_dev - 1], vertical_wind[:, :: lon_dev - 1]
    ends_got = ask_levels(ends_cot, ends_vw)

    sends = edges_of(seat, cot, vw, levels, count == 2)
    polar_got, ends_got, sends = lax.optimization_barrier((polar_got, ends_got, sends))
    if count == 2:
        edges = [lax.ppermute(sends[0], "lev", [(0, 1), (1, 0)])]
    else:
        edges = [
            lax.ppermute(sends[0], "lev", [(i + 1, i) for i in range(count - 1)]),
            lax.ppermute(sends[1], "lev", [(i, i + 1) for i in range(count - 1)]),
            later_sum(sends[2]),
        ]
    polar = adjoint_part(polar_cot, polar_vw, *polar_got)
    ends_adj = adjoint_part(ends_cot, ends_vw, *ends_got)

    rows = 2 * POLAR // peers
    grouped = polar.reshape(5 * levels, peers, rows, lon_dev)
    grouped = jnp.swapaxes(grouped, 0, 1).reshape(peers, 5 * levels * rows, lon_dev)

    pack = jnp.concatenate([ends_adj.reshape(5 * levels, 2, lat), zonal_coef[:, :: lon_dev - 1]], 0)
    up = [(i, (i + 1) % peers) for i in range(peers)]
    down = [(j, i) for i, j in up]
    beyond = jnp.stack([lax.ppermute(pack[:, 1], "lon", up), lax.ppermute(pack[:, 0], "lon", down)], 1)
    halo_adj = beyond[: 5 * levels].reshape(5, levels, 2, lat)
    halo_zc = beyond[5 * levels :]

    smoothed = polar_filter(grouped, cutoff, peers)
    smoothed = smoothed.reshape(2, peers // 2, 5, levels, rows, lon_dev + 2)
    smoothed = smoothed.transpose(2, 5, 0, 3, 1, 4).reshape(5, lon_dev + 2, 2, levels, POLAR)
    north, south = smoothed[:, :, 0], smoothed[:, :, 1]
    gap = ((0, 0), (0, 0), (0, 0))
    smooth = jnp.concatenate(
        [jnp.pad(north, (*gap, (0, 128 - POLAR))), jnp.pad(south, (*gap, (128 - POLAR, 0)))], 2
    )[:, 1 : lon_dev + 1]
    outer = [jnp.swapaxes(x[:, :: lon_dev + 1], 1, 2) for x in (north, south)]
    halo_f = jnp.concatenate([outer[0], halo_adj[..., POLAR : lat - POLAR], outer[1]], 3)
    halo = jnp.stack(coupled(halo_zc, [halo_f[f] for f in range(5)], 0))
    out = stencil(
        seat, cot, vw, to_rows(zonal_coef), to_rows(merid_coef), smooth, to_rows(halo), edges, levels
    )
    return from_rows(out, levels)


def lane_of(shape):
    return lax.broadcasted_iota(jnp.int32, shape, len(shape) - 1)


def pair_up(a, b, lane):
    inner = jnp.where(lane < 64, pltpu.roll(b, POLAR, 1), pltpu.roll(b, 128 - POLAR, 1))
    return jnp.where((lane >= POLAR) & (lane < 128 - POLAR), inner, a)


def second_of(pair, lane):
    return jnp.where(lane < 64, pltpu.roll(pair, 128 - POLAR, 1), pltpu.roll(pair, POLAR, 1))


def polar_level(levels, north, south, k, lane):
    lon, rows, _ = north.shape
    near = north.reshape(lon * rows, 128)[pl.ds(k, lon, stride=rows), :]
    far = south.reshape(lon * rows, 128)[pl.ds(levels + k, lon, stride=rows), :]
    return jnp.where(lane < 64, near, far)


def edge_block(levels, front, cot, vw, out):
    fields, chunk, rows, _ = cot.shape
    tiles = rows // levels
    flat_c = cot.reshape(fields * chunk * rows, 128)
    flat_v = vw.reshape(chunk * rows, 128)
    flat_t = cot.at[2].reshape(chunk * rows, 128)

    def product(k, sign):
        c = flat_c[pl.ds(k, fields * chunk * tiles, stride=levels), :]
        v = flat_v[pl.ds(k, chunk * tiles, stride=levels), :]
        c = c.reshape(fields, chunk, tiles, 128)
        out[:fields] = sign * (v.reshape(1, chunk, tiles, 128) * c)

    total = flat_t[pl.ds(0, chunk * tiles, stride=levels), :]
    for k in range(1, levels):
        total = total + flat_t[pl.ds(k, chunk * tiles, stride=levels), :]
    out[fields] = jnp.where(front, 0.0, total.reshape(chunk, tiles, 128))
    pl.when(front)(lambda: product(levels - 1, -1.0))
    pl.when(jnp.logical_not(front))(lambda: product(0, 1.0))


def open_kernel(levels, seat, cot, vw, sent, ends, local, cn, cs, vn, vs, ec, ev, below, sems):
    _, lon, rows, _ = cot.shape
    wide = 2 * levels
    lane = lane_of((lon, 128))
    front = seat[0] == 0
    near, far = pl.ds(0, wide), pl.ds(rows - wide, wide)
    jobs = [(vw.at[:, near], vn), (vw.at[:, far], vs)]
    order = (2, 0, 1, 3, 4)
    for f in order:
        jobs += [(cot.at[f, :, near], cn.at[f]), (cot.at[f, :, far], cs.at[f])]
    for n, e in enumerate((0, lon - 1)):
        jobs += [(cot.at[:, e], ec.at[:, n]), (vw.at[e], ev.at[n])]
    jobs = [pltpu.make_async_copy(a, b, sems.at[n]) for n, (a, b) in enumerate(jobs)]
    for job in jobs:
        job.start()
    jobs[0].wait()
    jobs[1].wait()
    v = [polar_level(levels, vn, vs, k, lane) for k in range(levels)]
    for n, f in enumerate(order):
        jobs[2 + 2 * n].wait()
        jobs[3 + 2 * n].wait()
        c = [polar_level(levels, cn.at[f], cs.at[f], k, lane) for k in range(levels)]
        w = [a * b for a, b in zip(v, c)]
        edge = jnp.where(front, -w[levels - 1], w[0])
        if f == 2:
            run = c[levels - 1]
            below[levels - 1] = run
            for k in range(levels - 2, -1, -1):
                run = run + c[k]
                below[k] = run
            total = jnp.where(front, 0.0, run)
            sent[2] = total
        if f == 4:
            sent[2] = pair_up(edge, sent[2], lane)
        elif f == 2:
            sent[1] = edge
        elif f % 2:
            sent[f // 2] = pair_up(sent[f // 2], edge, lane)
        else:
            sent[f // 2] = edge
        for k in range(0, levels, 2):
            pieces = []
            for at in (k, k + 1):
                a = c[at]
                if at < levels - 1:
                    a = a + w[at + 1]
                if at > 0:
                    a = a - w[at - 1]
                if f == 3:
                    a = a - COUPLE_B * below[at]
                pieces.append(a)
            local[f * levels // 2 + k // 2] = pair_up(pieces[0], pieces[1], lane)
    for job in jobs[12:]:
        job.wait()
    edge_block(levels, front, ec, ev, ends)


def opening(seat, cot, vw, levels):
    _, lon, rows, _ = cot.shape
    tiles, wide = rows // levels, 2 * levels
    f32 = jnp.float32
    place = pl.BlockSpec(memory_space=pl.ANY)
    vmem = pl.BlockSpec(memory_space=pltpu.VMEM)
    return pl.pallas_call(
        functools.partial(open_kernel, levels),
        out_shape=[
            jax.ShapeDtypeStruct((3, lon, 128), f32),
            jax.ShapeDtypeStruct((6, 2, tiles, 128), f32),
            jax.ShapeDtypeStruct((5 * levels // 2, lon, 128), f32),
        ],
        in_specs=[pl.BlockSpec(memory_space=pltpu.SMEM), place, place],
        out_specs=[vmem] * 3,
        scratch_shapes=[
            pltpu.VMEM((5, lon, wide, 128), f32), pltpu.VMEM((5, lon, wide, 128), f32),
            pltpu.VMEM((lon, wide, 128), f32), pltpu.VMEM((lon, wide, 128), f32),
            pltpu.VMEM((5, 2, rows, 128), f32), pltpu.VMEM((2, rows, 128), f32),
            pltpu.VMEM((levels, lon, 128), f32), pltpu.SemaphoreType.DMA((16,)),
        ],
        compiler_params=pltpu.CompilerParams(vmem_limit_bytes=SOME),
        cost_estimate=pl.CostEstimate(flops=9_000_000, bytes_accessed=10_000_000, transcendentals=0),
        name="opening",
    )(seat, cot, vw)


def edge_run_kernel(levels, start, chunk, count, seat, cot, vw, out, cbuf, vbuf, sems):
    def jobs(n):
        at = pl.ds(start + n * chunk, chunk)
        return (
            pltpu.make_async_copy(cot.at[:, at], cbuf.at[n], sems.at[n, 0]),
            pltpu.make_async_copy(vw.at[at], vbuf.at[n], sems.at[n, 1]),
        )

    for n in range(count):
        for job in jobs(n):
            job.start()
    for n in range(count):
        for job in jobs(n):
            job.wait()
        edge_block(
            levels, seat[0] == 0, cbuf.at[n], vbuf.at[n], out.at[:, pl.ds(n * chunk, chunk)]
        )


def edge_run(seat, cot, vw, levels, start, chunk, count):
    fields, lon, rows, _ = cot.shape
    tiles = rows // levels
    place = pl.BlockSpec(memory_space=pl.ANY)
    size = count * chunk
    return pl.pallas_call(
        functools.partial(edge_run_kernel, levels, start, chunk, count),
        out_shape=jax.ShapeDtypeStruct((fields + 1, size, tiles, 128), jnp.float32),
        in_specs=[pl.BlockSpec(memory_space=pltpu.SMEM), place, place],
        out_specs=pl.BlockSpec(memory_space=pltpu.VMEM),
        scratch_shapes=[
            pltpu.VMEM((count, fields, chunk, rows, 128), jnp.float32),
            pltpu.VMEM((count, chunk, rows, 128), jnp.float32),
            pltpu.SemaphoreType.DMA((count, 2)),
        ],
        compiler_params=pltpu.CompilerParams(vmem_limit_bytes=SOME),
        cost_estimate=pl.CostEstimate(
            flops=50_000 * size, bytes_accessed=120_000 * size, transcendentals=0
        ),
        name="edge_run",
    )(seat, cot, vw)


def slots_of(k, nq):
    north, south = range(nq // 2), range(nq // 2, nq)
    return (
        [(k, q) for q in north] + [(k + 1, q) for q in north]
        + [(k + 1, q) for q in south] + [(k, q) for q in south]
    )


def polar_kernel(
    peers, levels, late, chunk,
    cot, vw, zc, fwd, inv, local, got, ends, ct_ref, st_ref, mask_ref,
    smooth, left, right, *rest,
):
    late_out, rest = rest[: len(late)], rest[len(late) :]
    (fwd_ref, inv_ref, x_ref, held, made, back, z, zt, ec, ev, ez, es, flux, spread, below_ref, cbuf, vbuf, ebuf,
     own_sem, wave_sem, send_a, recv_a, send_b, recv_b, col_sem, halo_send, halo_recv, late_in, late_sem) = rest
    me = lax.axis_index("lon")
    front = lax.axis_index("lev") == 0
    _, lon, rows, _ = cot.shape
    wide = 2 * levels
    nq = peers // levels
    span = 2 * POLAR // nq
    cols = 5 * span
    half = cols // 2
    kpad = ct_ref.shape[2]
    lane = lane_of((lon, 128))
    barrier = pltpu.get_barrier_semaphore()

    def ahead(o):
        return lax.rem(me + o, peers)

    def behind(o):
        return lax.rem(me + peers - o, peers)

    def greet(o, _):
        pl.semaphore_signal(barrier, inc=1, device_id={"lon": ahead(o)}, device_id_type=MESH)
        return 0

    lax.fori_loop(1, peers, greet, 0)

    column_jobs = []
    for n, e in enumerate((0, lon - 1)):
        for m, (a, b) in enumerate(
            ((cot.at[:, e], ec.at[:, n]), (vw.at[e], ev.at[n]), (zc.at[e], ez.at[n]))
        ):
            column_jobs.append(pltpu.make_async_copy(a, b, col_sem.at[3 * n + m]))
    late_jobs, late_outs, n = [], [], 0
    for out, (start, size) in zip(late_out, late):
        for at in range(0, size, chunk):
            where = pl.ds(start + at, chunk)
            late_jobs.append((
                pltpu.make_async_copy(cot.at[:, where], cbuf.at[n], late_in.at[n, 0]),
                pltpu.make_async_copy(vw.at[where], vbuf.at[n], late_in.at[n, 1]),
            ))
            late_outs.append(
                pltpu.make_async_copy(ebuf.at[n], out.at[:, pl.ds(at, chunk)], late_sem.at[n])
            )
            n += 1
    wave_jobs = [
        pltpu.make_async_copy(fwd, fwd_ref, wave_sem.at[0]),
        pltpu.make_async_copy(inv, inv_ref, wave_sem.at[1]),
    ]
    for job in column_jobs + wave_jobs:
        job.start()
    for jobs in late_jobs:
        for job in jobs:
            job.start()

    z[...] = jnp.zeros_like(z)
    for f in range(5):
        pair = got[f // 2]
        edge = second_of(pair, lane) if f % 2 else pair
        tail = second_of(got[2], lane) if f == 3 else None
        for k in range(0, levels, 2):
            add = []
            for at in (k, k + 1):
                a = jnp.zeros((lon, 128), jnp.float32)
                if at == levels - 1:
                    a = a + jnp.where(front, edge, 0.0)
                if at == 0:
                    a = a + jnp.where(front, 0.0, edge)
                if f == 3:
                    a = a - COUPLE_B * tail
                add.append(a)
            z[:lon] = local[f * levels // 2 + k // 2] + pair_up(add[0], add[1], lane)
            zt[...] = z[...].T
            for n, (at, q) in enumerate(slots_of(k, nq)):
                d = at * nq + q
                x_ref[d, f * span : (f + 1) * span] = zt[n * span : (n + 1) * span, :128]
                for h in range(0, span, 8):
                    to = f * span + h
                    end = zt[n * span + h : n * span + h + 8, 128:]
                    if to < half:
                        x_ref[d, cols + to : cols + to + 8] = end
                    else:
                        to += cols - half
                        x_ref[d, to : to + 8] += pltpu.roll(end, 64, 1)

    def out_copy(d):
        return pltpu.make_async_remote_copy(
            src_ref=x_ref.at[d], dst_ref=held.at[me], send_sem=send_a.at[d],
            recv_sem=recv_a.at[me], device_id={"lon": d}, device_id_type=MESH,
        )

    def in_copy(s):
        return pltpu.make_async_remote_copy(
            src_ref=x_ref.at[s], dst_ref=held.at[s], send_sem=send_a.at[s],
            recv_sem=recv_a.at[s], device_id={"lon": s}, device_id_type=MESH,
        )

    def back_copy(d):
        return pltpu.make_async_remote_copy(
            src_ref=made.at[d], dst_ref=back.at[me], send_sem=send_b.at[d],
            recv_sem=recv_b.at[me], device_id={"lon": d}, device_id_type=MESH,
        )

    def home_copy(s):
        return pltpu.make_async_remote_copy(
            src_ref=made.at[s], dst_ref=back.at[s], send_sem=send_b.at[s],
            recv_sem=recv_b.at[s], device_id={"lon": s}, device_id_type=MESH,
        )

    pl.semaphore_wait(barrier, peers - 1)
    lax.fori_loop(1, peers, lambda o, c: (out_copy(ahead(o)).start(), c)[1], 0)
    own = pltpu.make_async_copy(x_ref.at[me], held.at[me], own_sem)
    own.start()

    for n, jobs in enumerate(late_jobs):
        for job in jobs:
            job.wait()
        edge_block(levels, front, cbuf.at[n], vbuf.at[n], ebuf.at[n])
        late_outs[n].start()

    for job in wave_jobs:
        job.wait()
    own.wait()
    zero = jnp.zeros((cols, kpad), jnp.float32)
    dot = functools.partial(jnp.dot, precision=HIGHEST, preferred_element_type=jnp.float32)

    def gather(s, carry):
        a, b = carry
        ends = held[s, cols:]
        ends = jnp.concatenate([ends[:, :64], ends[:, 64:]], 0)
        both = dot(held[s, :cols], fwd_ref[:128]) + dot(ends, fwd_ref[128:])
        c, v = both[:, :kpad], both[:, kpad:]
        ct, st = ct_ref[s], st_ref[s]
        return a + (ct * c - st * v), b + (st * c + ct * v)

    def arrive(o, carry):
        s = behind(o)
        in_copy(s).wait_recv()
        return gather(s, carry)

    a, b = lax.fori_loop(1, peers, arrive, gather(me, (zero, zero)))
    mask = jnp.concatenate([mask_ref[...]] * 5, 0)
    a = a * mask
    b = b * mask

    def turn(d):
        ct, st = ct_ref[d], st_ref[d]
        p, q = a * ct + b * st, b * ct - a * st
        y = dot(p, inv_ref[0]) + dot(q, inv_ref[1])
        made[d, :cols] = y[:, :128]
        made[d, cols:] = jnp.concatenate([y[:half, 128:], y[half:, 128:]], 1)

    def depart(o, _):
        turn(ahead(o))
        pl.when(o > 1)(lambda: back_copy(ahead(o - 1)).start())
        return 0

    lax.fori_loop(1, peers, depart, 0)
    turn(me)
    back_copy(ahead(peers - 1)).start()
    mine = pltpu.make_async_copy(made.at[me], back.at[me], own_sem)
    mine.start()
    for job in late_outs:
        job.wait()
    for job in column_jobs:
        job.wait()
    mine.wait()
    lax.fori_loop(1, peers, lambda o, c: (home_copy(behind(o)).wait_recv(), c)[1], 0)

    for f in range(5):
        flat = smooth.at[f].reshape(lon * wide, 128)
        for k in range(0, levels, 2):
            for n, (at, q) in enumerate(slots_of(k, nq)):
                d = at * nq + q
                zt[n * span : (n + 1) * span, :128] = back[d, f * span : (f + 1) * span]
                for h in range(0, span, 8):
                    to = f * span + h
                    if to < half:
                        end = back[d, cols + to : cols + to + 8]
                    else:
                        to += cols - half
                        end = pltpu.roll(back[d, to : to + 8], 64, 1)
                    zt[n * span + h : n * span + h + 8, 128:] = end
            z[...] = zt[...].T
            first = z[:lon]
            flat[pl.ds(k, lon, stride=wide), :] = first
            flat[pl.ds(levels + k, lon, stride=wide), :] = first
            flat[pl.ds(k + 1, lon, stride=wide), :] = pltpu.roll(first, 128 - POLAR, 1)
            flat[pl.ds(levels + k + 1, lon, stride=wide), :] = pltpu.roll(first, POLAR, 1)

    for f in range(5):
        for n, e in enumerate((0, lon - 1)):
            es[f, n] = smooth[f, e]
    spread[...] = jnp.zeros_like(spread)
    column = column_maker(levels, front, ec, ev, es, ends, spread, below_ref)
    for n in range(2):
        _, fields = column(n)
        for v in range(rows // 8):
            zonal = coupled(ez[n, 8 * v : 8 * v + 8], [fields[f][v] for f in range(5)], 0)
            for f in range(5):
                flux[n, f, 8 * v : 8 * v + 8] = zonal[f]
    to_left = pltpu.make_async_remote_copy(
        src_ref=flux.at[0], dst_ref=right, send_sem=halo_send.at[0], recv_sem=halo_recv.at[0],
        device_id={"lon": behind(1)}, device_id_type=MESH,
    )
    to_right = pltpu.make_async_remote_copy(
        src_ref=flux.at[1], dst_ref=left, send_sem=halo_send.at[1], recv_sem=halo_recv.at[1],
        device_id={"lon": ahead(1)}, device_id_type=MESH,
    )
    to_left.start()
    to_right.start()
    lax.fori_loop(1, peers, lambda o, c: (out_copy(ahead(o)).wait_send(), c)[1], 0)
    lax.fori_loop(1, peers, lambda o, c: (back_copy(ahead(o)).wait_send(), c)[1], 0)
    to_left.wait()
    to_right.wait()


def hold(a):
    return pltpu.with_memory_space_constraint(jnp.asarray(a), pltpu.HBM)


def polar_path(cot, vw, zc, local, got, ends, cutoff, levels, peers, late, chunk):
    _, lon, rows, _ = cot.shape
    tiles, wide = rows // levels, 2 * levels
    nq = peers // levels
    nlon = peers * lon
    span = cutoff.shape[0] // nq
    kpad = (KMAX + 1 + 127) // 128 * 128
    wave = np.arange(kpad)
    fwd = np.concatenate(angles(np.arange(lon)[:, None], wave[None, :], nlon), axis=1)
    inv = np.stack(angles(wave[:, None], np.arange(lon)[None, :], nlon))
    short = 192 - lon
    fwd = np.pad(fwd, ((0, short), (0, 0)))
    inv = np.pad(inv, ((0, 0), (0, 0), (0, short)))
    ct, st = angles(np.arange(peers)[:, None, None] * lon, wave[None, None, :], nlon)
    mine = lax.dynamic_slice_in_dim(cutoff, lax.axis_index("lon") % nq * span, span)
    weight = np.where(wave == 0, 1.0 / nlon, 2.0 / nlon).astype(np.float32)
    mask = jnp.where(jnp.asarray(wave, jnp.int32)[None, :] <= mine[:, None], weight[None, :], 0.0)
    vmem = pl.BlockSpec(memory_space=pltpu.VMEM)
    place = pl.BlockSpec(memory_space=pltpu.HBM)
    dma = pltpu.SemaphoreType.DMA
    f32 = jnp.float32
    shape = (peers, 5 * span + 5 * span // 2, 128)
    blocks = sum(size for _, size in late) // chunk
    return pl.pallas_call(
        functools.partial(polar_kernel, peers, levels, late, chunk),
        out_shape=[
            jax.ShapeDtypeStruct((5, lon, wide, 128), f32),
            jax.ShapeDtypeStruct((5, rows, 128), f32),
            jax.ShapeDtypeStruct((5, rows, 128), f32),
        ] + [jax.ShapeDtypeStruct((6, size, tiles, 128), f32) for _, size in late],
        in_specs=[place] * 5 + [vmem] * 6,
        out_specs=[vmem] * 3 + [place] * len(late),
        scratch_shapes=[
            pltpu.VMEM(fwd.shape, f32), pltpu.VMEM(inv.shape, f32),
            pltpu.VMEM(shape, f32), pltpu.VMEM(shape, f32), pltpu.VMEM(shape, f32),
            pltpu.VMEM(shape, f32), pltpu.VMEM((256, 128), f32), pltpu.VMEM((128, 256), f32),
            pltpu.VMEM((5, 2, rows, 128), f32), pltpu.VMEM((2, rows, 128), f32),
            pltpu.VMEM((2, rows, 128), f32), pltpu.VMEM((5, 2, wide, 128), f32),
            pltpu.VMEM((2, 5, rows, 128), f32), pltpu.VMEM((5, rows, 128), f32),
            pltpu.VMEM((rows, 128), f32),
            pltpu.VMEM((blocks, 5, chunk, rows, 128), f32),
            pltpu.VMEM((blocks, chunk, rows, 128), f32),
            pltpu.VMEM((blocks, 6, chunk, tiles, 128), f32),
            dma(()), dma((2,)), dma((peers,)), dma((peers,)), dma((peers,)), dma((peers,)),
            dma((6,)), dma((2,)), dma((2,)), dma((blocks, 2)), dma((blocks,)),
        ],
        compiler_params=pltpu.CompilerParams(
            collective_id=1, has_side_effects=True, vmem_limit_bytes=30 << 20
        ),
        cost_estimate=pl.CostEstimate(flops=8_000_000_000, bytes_accessed=60_000_000, transcendentals=0),
        name="polar_path",
    )(cot, vw, zc, hold(fwd), hold(inv), local, got, ends, ct, st, mask)


def column_maker(levels, front, cot, vw, smooth, edges, spread, below_ref):
    _, _, rows, _ = cot.shape
    tiles = rows // levels
    parts = rows // 8
    edge_at = jnp.where(front, levels - 1, 0)
    row = lax.broadcasted_iota(jnp.int32, (8, 128), 0)
    lane = lane_of((8, 128))
    k = lax.rem(row, levels)
    north = (row < levels) & (lane < POLAR)
    south = (row >= levels) & (lane >= 128 - POLAR)

    def column(l):
        for f in range(5):
            spread[f, pl.ds(edge_at, tiles, stride=levels), :] = edges[f, l]
        for at in range(levels):
            below_ref[pl.ds(at, tiles, stride=levels), :] = edges[5, l]
        base, fields = [], []
        at = [pl.ds(8 * v, 8) for v in range(parts)]
        wind = [vw[l, at[v]] for v in range(parts)]
        for f in range(5):
            whole, inner = [], []
            for v in range(parts):
                c = cot[f, l, at[v]]
                w = wind[v] * c
                a = c + jnp.where(k < levels - 1, pltpu.roll(w, 7, 0), 0.0)
                a = a - jnp.where(k > 0, pltpu.roll(w, 1, 0), 0.0) + spread[f, at[v]]
                if f == 3:
                    run, r = cot[2, l, at[v]], 1
                    while r < levels:
                        run = run + jnp.where(k < levels - r, pltpu.roll(run, 8 - r, 0), 0.0)
                        r *= 2
                    a = a - COUPLE_B * (run + below_ref[at[v]])
                whole.append(a)
                if v == 0:
                    a = jnp.where(north, smooth[f, l], a)
                if v == parts - 1:
                    a = jnp.where(south, smooth[f, l], a)
                inner.append(a)
            base.append(whole)
            fields.append(inner)
        return base, fields

    return column


def lat_change(levels, m):
    row = lax.broadcasted_iota(jnp.int32, (8, 128), 0)
    lane = lane_of((8, 128))
    top = row < levels
    near = [pltpu.roll(a, 1, 1) for a in m]
    far = [pltpu.roll(a, 127, 1) for a in m]
    turned = [pltpu.roll(jnp.where(lane == 0, a, b), levels, 0) for a, b in zip(near, far)]
    zero = jnp.zeros((8, 128), jnp.float32)
    out = []
    for v in range(len(m)):
        before = turned[v - 1] if v else zero
        after = turned[v + 1] if v + 1 < len(m) else zero
        low = jnp.where(lane == 0, jnp.where(top, before, turned[v]), near[v])
        high = jnp.where(lane == 127, jnp.where(top, turned[v], after), far[v])
        out.append(high - low)
    return out


def strip_kernel(levels, start, steps, first, last, seat, cot, vw, zc, mc, smooth, edges, *rest):
    rest = list(rest)
    if first:
        left = rest.pop(0)
    else:
        wait_in, prior_in, _ = rest.pop(0), rest.pop(0), rest.pop(0)
    if last:
        right = rest.pop(0)
    out, wait, prior, ready, spread, below_ref, sems = rest[:7]
    _, chunk, rows, _ = cot.shape
    parts = rows // 8
    g = pl.program_id(0)
    slot = lax.rem(g, 2)

    def first_copy():
        return pltpu.make_async_copy(
            ready.at[0, :, pl.ds(1, chunk - 1)], out.at[:, pl.ds(0, chunk - 1)], sems.at[0]
        )

    def copy(at):
        s = lax.rem(at, 2)
        return pltpu.make_async_copy(
            ready.at[s], out.at[:, pl.ds(start + at * chunk - 1, chunk)], sems.at[s]
        )

    def act(at, what):
        if first:
            pl.when(at == 0)(lambda: getattr(first_copy(), what)())
            pl.when(at > 0)(lambda: getattr(copy(at), what)())
        else:
            getattr(copy(at), what)()

    @pl.when(g == 0)
    def _():
        spread[...] = jnp.zeros_like(spread)
        if first:
            prior[...] = left[...]
            wait[...] = jnp.zeros_like(wait)
        else:
            prior[...] = prior_in[...]
            wait[...] = wait_in[...]

    pl.when(g >= 2)(lambda: act(g - 2, "wait"))
    column = column_maker(levels, seat[0] == 0, cot, vw, smooth, edges, spread, below_ref)
    rows_of = [pl.ds(8 * v, 8) for v in range(parts)]

    def one(l, _):
        base, fields = column(l)
        zonal, merid = [], []
        for v in range(parts):
            mine = [fields[f][v] for f in range(5)]
            zonal.append(coupled(zc[l, rows_of[v]], mine, 0))
            merid.append(coupled(mc[l, rows_of[v]], mine, 1))
        for f in range(5):
            change = lat_change(levels, [merid[v][f] for v in range(parts)])
            for v in range(parts):
                at = rows_of[v]
                ready[slot, f, l, at] = wait[f, at] + zonal[v][f]
                wait[f, at] = base[f][v] + change[v] - prior[f, at]
                prior[f, at] = zonal[v][f]
        return 0

    lax.fori_loop(0, chunk, one, 0)
    act(g, "start")

    @pl.when(g == steps - 1)
    def _():
        if last:
            final, last_sem = rest[7:]
            for f in range(5):
                final[f, 0] = wait[f] + right[f]
            end = pltpu.make_async_copy(
                final, out.at[:, pl.ds(start + steps * chunk - 1, 1)], last_sem
            )
            end.start()
        if steps > 1:
            act(g - 1, "wait")
        act(g, "wait")
        if last:
            end.wait()


def strip(seat, cot, vw, zc, mc, smooth, edges, state, right, levels, start, steps, chunk):
    _, lon, rows, _ = cot.shape
    tiles = rows // levels
    at = start // chunk
    first, last = len(state) == 1, right is not None
    field = lambda n: pl.BlockSpec((5, chunk, n, 128), lambda g, s: (0, at + g, 0, 0))
    plain = pl.BlockSpec((chunk, rows, 128), lambda g, s: (at + g, 0, 0))
    whole = pl.BlockSpec((5, rows, 128), lambda g, s: (0, 0, 0))
    place = pl.BlockSpec(memory_space=pl.ANY)
    in_specs = [field(rows), plain, plain, plain, field(2 * levels),
                pl.BlockSpec((6, chunk, tiles, 128), lambda g, s: (0, g, 0, 0))]
    in_specs += [whole] if first else [whole, whole, place]
    args = [seat, cot, vw, zc, mc, smooth, edges, *state]
    aliases = {} if first else {len(args) - 1: 0}
    if last:
        in_specs.append(whole)
        args.append(right)
    one = jax.ShapeDtypeStruct((5, rows, 128), jnp.float32)
    held = [pltpu.VMEM((5, rows, 128), jnp.float32)] * 2
    scratch = [
        pltpu.VMEM((2, 5, chunk, rows, 128), jnp.float32),
        pltpu.VMEM((5, rows, 128), jnp.float32),
        pltpu.VMEM((rows, 128), jnp.float32),
        pltpu.SemaphoreType.DMA((2,)),
    ]
    if last:
        scratch = held + scratch + [
            pltpu.VMEM((5, 1, rows, 128), jnp.float32), pltpu.SemaphoreType.DMA(()),
        ]
    got = pl.pallas_call(
        functools.partial(strip_kernel, levels, start, steps, first, last),
        out_shape=[jax.ShapeDtypeStruct(cot.shape, jnp.float32)] + ([] if last else [one, one]),
        grid_spec=pltpu.PrefetchScalarGridSpec(
            num_scalar_prefetch=1,
            grid=(steps,),
            in_specs=in_specs,
            out_specs=[place] + ([] if last else [whole, whole]),
            scratch_shapes=scratch,
        ),
        input_output_aliases=aliases,
        compiler_params=pltpu.CompilerParams(vmem_limit_bytes=SOME),
        cost_estimate=pl.CostEstimate(
            flops=30 * 5 * steps * chunk * rows * 128,
            bytes_accessed=4 * 14 * steps * chunk * rows * 128,
            transcendentals=0,
        ),
        name="strip",
    )(*args)
    return got[0] if last else [got[1], got[2], got[0]]


def fast_body(cotangent, zonal_coef, merid_coef, vertical_wind, cutoff):
    levels, lon_dev, lat = cotangent.shape[1:]
    peers = lax.axis_size("lon")
    seat = lax.axis_index("lev").astype(jnp.int32)[None]
    cot, vw = to_rows(cotangent), to_rows(vertical_wind)
    zc, mc = to_rows(zonal_coef), to_rows(merid_coef)
    cot, vw, zc, mc = (hold(a) for a in (cot, vw, zc, mc))
    trade = lambda a: lax.ppermute(a, "lev", [(0, 1), (1, 0)])
    chunk = max(d for d in range(2, 21) if lon_dev % d == 0)
    blocks = lon_dev // chunk
    cuts = sorted({max(1, blocks * n // 9) for n in (3, 6, 8)} | {blocks})
    parts = [(a * chunk, (b - a) * chunk) for a, b in zip([0] + cuts[:-1], cuts)]

    sent, ends, local = opening(seat, cot, vw, levels)
    polar_got, ends_got = trade(sent), trade(ends)
    token, _ = lax.optimization_barrier((seat, sent))
    edges = []
    for start, size in parts[:2]:
        part = edge_run(token, cot, vw, levels, start, chunk, size // chunk)
        edges.append(trade(part))
        token, _ = lax.optimization_barrier((token, part))
    polar_got, ends_got, token = lax.optimization_barrier((polar_got, ends_got, token))
    smooth, left, right, *later = polar_path(
        cot, vw, zc, local, polar_got, ends_got, cutoff, levels, peers, tuple(parts[2:]), chunk
    )
    edges += [trade(part) for part in later]
    state = [left]
    for n, (start, size) in enumerate(parts):
        end = right if n == len(parts) - 1 else None
        state = strip(
            seat, cot, vw, zc, mc, smooth, edges[n], state, end, levels, start, size // chunk, chunk
        )
    return from_rows(state, levels)


def body(cotangent, zonal_coef, merid_coef, vertical_wind, cutoff):
    levels, lon_dev, lat = cotangent.shape[1:]
    peers, count = lax.axis_size("lon"), lax.axis_size("lev")
    span = 2 * POLAR * levels // peers
    fast = (
        count == 2 and levels * 2 == 8 and peers % (2 * levels) == 0 and lat % 256 == 0
        and span % 16 == 0 and 128 < lon_dev <= 192 and cutoff.shape[0] == 2 * POLAR
    )
    return (fast_body if fast else plain_body)(
        cotangent, zonal_coef, merid_coef, vertical_wind, cutoff
    )


def solution(mesh):
    return jax.shard_map(
        body,
        mesh=mesh,
        in_specs=(
            P(None, "lev", "lon", None),
            P("lev", "lon", None),
            P("lev", "lon", None),
            P("lev", "lon", None),
            P(),
        ),
        out_specs=P(None, "lev", "lon", None),
        check_vma=False,
    )
```

```python
import functools
import math

import jax
import jax.numpy as jnp
import numpy as np
from jax import lax
from jax.experimental import pallas as pl
from jax.experimental.pallas import tpu as pltpu
from jax.sharding import PartitionSpec as P

POLAR = 32
KMAX = 360
COUPLE_G = 0.3
COUPLE_H = 0.3
COUPLE_B = 0.2
MESH = pl.DeviceIdType.MESH
HIGHEST = lax.Precision.HIGHEST
ROOM = 61 << 20
SOME = 36 << 20


def angles(left, right, period):
    phase = (left * right) % period * (2.0 * math.pi / period)
    return np.cos(phase).astype(np.float32), np.sin(phase).astype(np.float32)


def filter_kernel(
    peers, packed, x_ref, fwd_ref, inv_ref, ct_ref, st_ref, mask_ref, out_ref, held, made,
    own_sem, send_a, recv_a, send_b, recv_b,
):
    me = lax.axis_index("lon")
    kpad = ct_ref.shape[2]
    barrier = pltpu.get_barrier_semaphore()

    def greet(o, _):
        pl.semaphore_signal(
            barrier, inc=1, device_id={"lon": lax.rem(me + o, peers)}, device_id_type=MESH
        )
        return 0

    lax.fori_loop(1, peers, greet, 0)
    pl.semaphore_wait(barrier, peers - 1)

    def out_copy(o):
        d = lax.rem(me + o, peers)
        return pltpu.make_async_remote_copy(
            src_ref=x_ref.at[d], dst_ref=held.at[me], send_sem=send_a.at[d],
            recv_sem=recv_a.at[me], device_id={"lon": d}, device_id_type=MESH,
        )

    def in_copy(o):
        s = lax.rem(me + o, peers)
        return pltpu.make_async_remote_copy(
            src_ref=x_ref.at[s], dst_ref=held.at[s], send_sem=send_a.at[s],
            recv_sem=recv_a.at[s], device_id={"lon": s}, device_id_type=MESH,
        )

    def back_copy(o):
        d = lax.rem(me + o, peers)
        return pltpu.make_async_remote_copy(
            src_ref=made.at[d], dst_ref=out_ref.at[me], send_sem=send_b.at[d],
            recv_sem=recv_b.at[me], device_id={"lon": d}, device_id_type=MESH,
        )

    def home_copy(o):
        s = lax.rem(me + o, peers)
        return pltpu.make_async_remote_copy(
            src_ref=made.at[s], dst_ref=out_ref.at[s], send_sem=send_b.at[s],
            recv_sem=recv_b.at[s], device_id={"lon": s}, device_id_type=MESH,
        )

    lax.fori_loop(1, peers, lambda o, c: (out_copy(o).start(), c)[1], 0)
    own = pltpu.make_async_copy(x_ref.at[me], held.at[me], own_sem)
    own.start()
    own.wait()
    cols = mask_ref.shape[0]
    half = cols // 2
    zero = jnp.zeros((cols, kpad), jnp.float32)
    dot = functools.partial(jnp.dot, precision=HIGHEST, preferred_element_type=jnp.float32)

    def gather(s, carry):
        a, b = carry
        if packed:
            ends = held[s, cols:]
            ends = jnp.concatenate([ends[:, :64], ends[:, 64:]], 0)
            both = dot(held[s, :cols], fwd_ref[:128]) + dot(ends, fwd_ref[128:])
        else:
            both = dot(held[s], fwd_ref[...])
        c, v = both[:, :kpad], both[:, kpad:]
        ct, st = ct_ref[s], st_ref[s]
        return a + (ct * c - st * v), b + (st * c + ct * v)

    def arrive(o, carry):
        in_copy(o).wait_recv()
        return gather(lax.rem(me + o, peers), carry)

    a, b = lax.fori_loop(1, peers, arrive, gather(me, (zero, zero)))
    a = a * mask_ref[...]
    b = b * mask_ref[...]

    def spread(d):
        ct, st = ct_ref[d], st_ref[d]
        p, q = a * ct + b * st, b * ct - a * st
        if packed:
            y = dot(p, inv_ref[0]) + dot(q, inv_ref[1])
            made[d, :cols] = y[:, :128]
            made[d, cols:] = jnp.concatenate([y[:half, 128:], y[half:, 128:]], 1)
        else:
            made[d] = dot(p, inv_ref[0]) + dot(q, inv_ref[1])

    def depart(o, _):
        spread(lax.rem(me + o, peers))
        pl.when(o > 1)(lambda: back_copy(o - 1).start())
        return 0

    lax.fori_loop(1, peers, depart, 0)
    spread(me)
    back_copy(peers - 1).start()
    mine = pltpu.make_async_copy(made.at[me], out_ref.at[me], own_sem)
    mine.start()
    mine.wait()
    lax.fori_loop(1, peers, lambda o, c: (home_copy(o).wait_recv(), c)[1], 0)
    lax.fori_loop(1, peers, lambda o, c: (out_copy(o).wait_send(), c)[1], 0)
    lax.fori_loop(1, peers, lambda o, c: (back_copy(o).wait_send(), c)[1], 0)


def polar_filter(x, cutoff, peers):
    _, cols, lon_dev = x.shape
    nlon = peers * lon_dev
    rows = cutoff.shape[0] // peers
    kpad = (KMAX + 1 + 127) // 128 * 128
    wave = np.arange(kpad)
    fwd = np.concatenate(angles(np.arange(lon_dev)[:, None], wave[None, :], nlon), axis=1)
    inv = np.stack(angles(wave[:, None], np.arange(-1, lon_dev + 1)[None, :] % nlon, nlon))
    over, wider = lon_dev - 128, lon_dev + 2 - 128
    packed = over > 0 and wider <= 64 and cols % 16 == 0
    half = cols // 2
    if packed:
        fwd = np.pad(fwd, ((0, 64 - over), (0, 0)))
        inv = np.pad(inv, ((0, 0), (0, 0), (0, 64 - wider)))
        ends = jnp.pad(x[..., 128:], ((0, 0), (0, 0), (0, 64 - over)))
        x = jnp.concatenate([x[..., :128], jnp.concatenate([ends[:, :half], ends[:, half:]], 2)], 1)
        shape = (peers, cols + half, 128)
    else:
        shape = (peers, cols, lon_dev + 2)
    ct, st = angles(np.arange(peers)[:, None, None] * lon_dev, wave[None, None, :], nlon)
    mine = lax.dynamic_slice_in_dim(cutoff, lax.axis_index("lon") * rows, rows)
    weight = np.where(wave == 0, 1.0 / nlon, 2.0 / nlon).astype(np.float32)
    mask = jnp.where(jnp.asarray(wave, jnp.int32)[None, :] <= mine[:, None], weight[None, :], 0.0)
    mask = jnp.tile(mask, (cols // rows, 1))
    vmem = pl.BlockSpec(memory_space=pltpu.VMEM)
    dma = pltpu.SemaphoreType.DMA
    y = pl.pallas_call(
        functools.partial(filter_kernel, peers, packed),
        out_shape=jax.ShapeDtypeStruct(shape, jnp.float32),
        in_specs=[vmem] * 6,
        out_specs=vmem,
        scratch_shapes=[
            pltpu.VMEM(x.shape, jnp.float32),
            pltpu.VMEM(shape, jnp.float32),
            dma(()), dma((peers,)), dma((peers,)), dma((peers,)), dma((peers,)),
        ],
        compiler_params=pltpu.CompilerParams(
            collective_id=0, has_side_effects=True, vmem_limit_bytes=24 << 20
        ),
        cost_estimate=pl.CostEstimate(flops=8_000_000_000, bytes_accessed=60_000_000, transcendentals=0),
        name="polar_filter",
    )(x, fwd, inv, ct, st, mask)
    if not packed:
        return y
    ends = jnp.concatenate([y[:, cols:, :wider], y[:, cols:, 64 : 64 + wider]], 1)
    return jnp.concatenate([y[:, :cols], ends], 2)


def to_rows(x):
    *lead, levels, lon, lat = x.shape
    n = len(lead)
    x = x.reshape(*lead, levels, lon, lat // 128, 128)
    x = x.transpose(*range(n), n + 1, n + 2, n, n + 3)
    return x.reshape(*lead, lon, lat // 128 * levels, 128)


def from_rows(x, levels):
    *lead, lon, rows, _ = x.shape
    n = len(lead)
    x = x.reshape(*lead, lon, rows // levels, levels, 128)
    x = x.transpose(*range(n), n + 2, n, n + 1, n + 3)
    return x.reshape(*lead, levels, lon, rows // levels * 128)


def chunk_of(lon):
    return max(d for d in range(1, 21) if lon % d == 0)


def edge_kernel(levels, choose, seat, cot, vw, *outs):
    fields, chunk, rows, _ = cot.shape
    tiles = rows // levels
    flat_c = cot.reshape(fields * chunk * rows, 128)
    flat_v = vw.reshape(chunk * rows, 128)
    sends = outs[: 1 if choose else 2]

    def level(ref, count, k):
        return ref[pl.ds(k, count * tiles, stride=levels), :] if levels > 1 else ref[...]

    def product(k, sign, out):
        c = level(flat_c, fields * chunk, k).reshape(fields, chunk, tiles, 128)
        v = level(flat_v, chunk, k).reshape(1, chunk, tiles, 128)
        out[:fields] = sign * (v * c)

    flat_t = cot.at[2].reshape(chunk * rows, 128)
    total = level(flat_t, chunk, 0)
    for k in range(1, levels):
        total = total + level(flat_t, chunk, k)
    total = total.reshape(chunk, tiles, 128)
    if choose:
        sends[0][fields] = jnp.where(seat[0] == 0, 0.0, total)
        pl.when(seat[0] == 0)(lambda: product(levels - 1, -1.0, sends[0]))
        pl.when(seat[0] != 0)(lambda: product(0, 1.0, sends[0]))
    else:
        product(0, 1.0, sends[0])
        product(levels - 1, -1.0, sends[1])
        outs[2][...] = total


def edges_of(seat, cot, vw, levels, choose):
    fields, lon, rows, _ = cot.shape
    tiles = rows // levels
    chunk = chunk_of(lon)
    n = 1 if choose else 2
    wide = fields + 1 if choose else fields
    return pl.pallas_call(
        functools.partial(edge_kernel, levels, choose),
        out_shape=[jax.ShapeDtypeStruct((wide, lon, tiles, 128), jnp.float32)] * n
        + [jax.ShapeDtypeStruct((lon, tiles, 128), jnp.float32)] * (n - 1),
        grid_spec=pltpu.PrefetchScalarGridSpec(
            num_scalar_prefetch=1,
            grid=(lon // chunk,),
            in_specs=[
                pl.BlockSpec((fields, chunk, rows, 128), lambda g, s: (0, g, 0, 0)),
                pl.BlockSpec((chunk, rows, 128), lambda g, s: (g, 0, 0)),
            ],
            out_specs=[pl.BlockSpec((wide, chunk, tiles, 128), lambda g, s: (0, g, 0, 0))] * n
            + [pl.BlockSpec((chunk, tiles, 128), lambda g, s: (g, 0, 0))] * (n - 1),
        ),
        compiler_params=pltpu.CompilerParams(vmem_limit_bytes=24 << 20),
        cost_estimate=pl.CostEstimate(flops=10_000_000, bytes_accessed=22_000_000, transcendentals=0),
        name="edges",
    )(seat, cot, vw)


def coupled(coef, fields, first):
    flux = [coef * f for f in fields]
    flux[first] = flux[first] + COUPLE_H * fields[3]
    flux[3] = flux[3] + COUPLE_G * fields[first]
    return flux


def stencil_kernel(levels, steps, n_edge, seat, cot, vw, zc, mc, smooth, halo, *rest):
    edges = rest[:n_edge]
    tail = edges[0].at[5] if n_edge == 1 else rest[n_edge]
    rest = rest[1:] if n_edge > 1 else rest
    edge_at = (1 - seat[0]) * (levels - 1)
    out, ready, final, wait, prior, spread, below_ref, sems, last_sem = rest[n_edge:]
    _, chunk, rows, _ = cot.shape
    tiles = rows // levels
    g = pl.program_id(0)
    slot = lax.rem(g, 2)
    lane = lax.broadcasted_iota(jnp.int32, (rows, 128), 1)
    row = lax.broadcasted_iota(jnp.int32, (rows, 128), 0)
    k = lax.rem(row, levels)
    cap_lane = lax.broadcasted_iota(jnp.int32, (2 * levels, 128), 1)
    cap_row = lax.broadcasted_iota(jnp.int32, (2 * levels, 128), 0)
    north = (cap_row < levels) & (cap_lane < POLAR)
    south = (cap_row >= levels) & (cap_lane >= 128 - POLAR)

    def first_copy():
        return pltpu.make_async_copy(
            ready.at[0, :, pl.ds(1, chunk - 1)], out.at[:, pl.ds(0, chunk - 1)], sems.at[0]
        )

    def copy(at):
        s = lax.rem(at, 2)
        return pltpu.make_async_copy(
            ready.at[s], out.at[:, pl.ds(at * chunk - 1, chunk)], sems.at[s]
        )

    @pl.when(g == 0)
    def _():
        spread[...] = jnp.zeros_like(spread)
        for f in range(5):
            prior[f] = halo[f, 0]
            wait[f] = jnp.zeros((rows, 128), jnp.float32)

    pl.when(g == 2)(lambda: first_copy().wait())
    pl.when(g > 2)(lambda: copy(g - 2).wait())

    def put(ref, at, value):
        if levels > 1:
            ref[pl.ds(at, tiles, stride=levels), :] = value
        else:
            ref[...] = value

    def one(l, _):
        for f in range(5):
            if n_edge == 1:
                put(spread.at[0, f], edge_at, edges[0][f, l])
            else:
                put(spread.at[0, f], levels - 1, edges[0][f, l])
                put(spread.at[1, f], 0, edges[1][f, l])
        for at in range(levels):
            put(below_ref, at, tail[l])
        wind = vw[l]
        base, fields = [], []
        for f in range(5):
            c = cot[f, l]
            w = wind * c
            a = c
            if levels > 1:
                up = jnp.where(k < levels - 1, pltpu.roll(w, rows - 1, 0), 0.0)
                a = a + (up - jnp.where(k > 0, pltpu.roll(w, 1, 0), 0.0))
            for n in range(n_edge):
                a = a + spread[n, f]
            if f == 3:
                theta = cot[2, l]
                below = below_ref[...] + theta
                for r in range(1, levels):
                    below = below + jnp.where(k < levels - r, pltpu.roll(theta, rows - r, 0), 0.0)
                a = a - COUPLE_B * below
            base.append(a)
            s = smooth[f, l]
            top = jnp.where(north, s, a[: 2 * levels])
            low = jnp.where(south, s, a[rows - 2 * levels :])
            fields.append(jnp.concatenate([top, a[2 * levels : rows - 2 * levels], low], 0))
        zonal = coupled(zc[l], fields, 0)
        merid = coupled(mc[l], fields, 1)
        for f in range(5):
            ready[slot, f, l] = wait[f] + zonal[f]
            left = pltpu.roll(merid[f], 1, 1)
            over = jnp.where(row < levels, 0.0, pltpu.roll(left, levels, 0))
            left = jnp.where(lane == 0, over, left)
            right = pltpu.roll(merid[f], 127, 1)
            over = jnp.where(row >= rows - levels, 0.0, pltpu.roll(right, rows - levels, 0))
            right = jnp.where(lane == 127, over, right)
            wait[f] = base[f] + (right - left) - prior[f]
            prior[f] = zonal[f]
        return 0

    lax.fori_loop(0, chunk, one, 0)
    pl.when(g == 0)(lambda: first_copy().start())
    pl.when(g > 0)(lambda: copy(g).start())

    @pl.when(g == steps - 1)
    def _():
        for f in range(5):
            final[f, 0] = wait[f] + halo[f, 1]
        end = pltpu.make_async_copy(final, out.at[:, pl.ds(steps * chunk - 1, 1)], last_sem)
        end.start()
        copy(g - 1).wait() if steps > 2 else first_copy().wait()
        copy(g).wait()
        end.wait()


def stencil(seat, cot, vw, zc, mc, smooth, halo, edges, levels):
    _, lon, rows, _ = cot.shape
    tiles = rows // levels
    chunk = chunk_of(lon)
    steps = lon // chunk
    field = lambda n: pl.BlockSpec((5, chunk, n, 128), lambda g, s: (0, g, 0, 0))
    plain = lambda n: pl.BlockSpec((chunk, n, 128), lambda g, s: (g, 0, 0))
    return pl.pallas_call(
        functools.partial(stencil_kernel, levels, steps, min(len(edges), 2)),
        out_shape=jax.ShapeDtypeStruct(cot.shape, jnp.float32),
        grid_spec=pltpu.PrefetchScalarGridSpec(
            num_scalar_prefetch=1,
            grid=(steps,),
            in_specs=[field(rows), plain(rows), plain(rows), plain(rows), field(2 * levels),
                      pl.BlockSpec((5, 2, rows, 128), lambda g, s: (0, 0, 0, 0))]
            + [pl.BlockSpec((6, chunk, tiles, 128), lambda g, s: (0, g, 0, 0))]
            if len(edges) == 1
            else [field(rows), plain(rows), plain(rows), plain(rows), field(2 * levels),
                  pl.BlockSpec((5, 2, rows, 128), lambda g, s: (0, 0, 0, 0)),
                  field(tiles), field(tiles), plain(tiles)],
            out_specs=pl.BlockSpec(memory_space=pl.ANY),
            scratch_shapes=[
                pltpu.VMEM((2, 5, chunk, rows, 128), jnp.float32),
                pltpu.VMEM((5, 1, rows, 128), jnp.float32),
                pltpu.VMEM((5, rows, 128), jnp.float32),
                pltpu.VMEM((5, rows, 128), jnp.float32),
                pltpu.VMEM((min(len(edges), 2), 5, rows, 128), jnp.float32),
                pltpu.VMEM((rows, 128), jnp.float32),
                pltpu.SemaphoreType.DMA((2,)),
                pltpu.SemaphoreType.DMA(()),
            ],
        ),
        compiler_params=pltpu.CompilerParams(vmem_limit_bytes=40 << 20),
        cost_estimate=pl.CostEstimate(
            flops=30 * 5 * lon * rows * 128, bytes_accessed=4 * 14 * lon * rows * 128, transcendentals=0
        ),
        name="stencil",
    )(seat, cot, vw, zc, mc, smooth, halo, *edges)


def swap_levels(first, last, total):
    count = lax.axis_size("lev")
    if count == 2:
        seat = lax.axis_index("lev")
        lead = jnp.concatenate([first, total[None]], 0)
        trail = jnp.concatenate([last, jnp.zeros_like(total)[None]], 0)
        got = lax.ppermute(jnp.where(seat == 0, trail, lead), "lev", [(0, 1), (1, 0)])
        return jnp.where(seat == 0, got[:5], 0.0), jnp.where(seat == 1, got[:5], 0.0), got[5]
    up = lax.ppermute(first, "lev", [(i + 1, i) for i in range(count - 1)])
    down = lax.ppermute(last, "lev", [(i, i + 1) for i in range(count - 1)])
    return up, down, later_sum(total)


def later_sum(local):
    count = lax.axis_size("lev")
    total = jnp.zeros_like(local)
    for r in range(1, count):
        total = total + lax.ppermute(local, "lev", [(i + r, i) for i in range(count - r)])
    return total


def ask_levels(cot, vw):
    return swap_levels(vw[0] * cot[:, 0], vw[-1] * cot[:, -1], cot[2].sum(0))


def adjoint_part(cot, vw, up, down, later):
    weighted = vw[None] * cot
    above = jnp.concatenate([weighted[:, 1:], up[:, None]], 1)
    under = jnp.concatenate([down[:, None], weighted[:, :-1]], 1)
    below = [later + cot[2, -1]]
    for k in range(cot.shape[1] - 2, -1, -1):
        below.insert(0, below[0] + cot[2, k])
    parts = cot + (above - under)
    return jnp.concatenate(
        [parts[:3], parts[3:4] - COUPLE_B * jnp.stack(below)[None], parts[4:]], 0
    )


def polar_cut(x):
    return jnp.concatenate([x[..., :POLAR], x[..., x.shape[-1] - POLAR :]], -1)


def plain_body(cotangent, zonal_coef, merid_coef, vertical_wind, cutoff):
    levels, lon_dev, lat = cotangent.shape[1:]
    peers = lax.axis_size("lon")
    count = lax.axis_size("lev")
    seat = lax.axis_index("lev").astype(jnp.int32)[None]
    cot, vw = to_rows(cotangent), to_rows(vertical_wind)
    polar_cot = jnp.swapaxes(polar_cut(cotangent), 2, 3)
    polar_vw = jnp.swapaxes(polar_cut(vertical_wind), 1, 2)
    polar_got = ask_levels(polar_cot, polar_vw)
    ends_cot, ends_vw = cotangent[:, :, :: lon_dev - 1], vertical_wind[:, :: lon_dev - 1]
    ends_got = ask_levels(ends_cot, ends_vw)

    sends = edges_of(seat, cot, vw, levels, count == 2)
    polar_got, ends_got, sends = lax.optimization_barrier((polar_got, ends_got, sends))
    if count == 2:
        edges = [lax.ppermute(sends[0], "lev", [(0, 1), (1, 0)])]
    else:
        edges = [
            lax.ppermute(sends[0], "lev", [(i + 1, i) for i in range(count - 1)]),
            lax.ppermute(sends[1], "lev", [(i, i + 1) for i in range(count - 1)]),
            later_sum(sends[2]),
        ]
    polar = adjoint_part(polar_cot, polar_vw, *polar_got)
    ends_adj = adjoint_part(ends_cot, ends_vw, *ends_got)

    rows = 2 * POLAR // peers
    grouped = polar.reshape(5 * levels, peers, rows, lon_dev)
    grouped = jnp.swapaxes(grouped, 0, 1).reshape(peers, 5 * levels * rows, lon_dev)

    pack = jnp.concatenate([ends_adj.reshape(5 * levels, 2, lat), zonal_coef[:, :: lon_dev - 1]], 0)
    up = [(i, (i + 1) % peers) for i in range(peers)]
    down = [(j, i) for i, j in up]
    beyond = jnp.stack([lax.ppermute(pack[:, 1], "lon", up), lax.ppermute(pack[:, 0], "lon", down)], 1)
    halo_adj = beyond[: 5 * levels].reshape(5, levels, 2, lat)
    halo_zc = beyond[5 * levels :]

    smoothed = polar_filter(grouped, cutoff, peers)
    smoothed = smoothed.reshape(2, peers // 2, 5, levels, rows, lon_dev + 2)
    smoothed = smoothed.transpose(2, 5, 0, 3, 1, 4).reshape(5, lon_dev + 2, 2, levels, POLAR)
    north, south = smoothed[:, :, 0], smoothed[:, :, 1]
    gap = ((0, 0), (0, 0), (0, 0))
    smooth = jnp.concatenate(
        [jnp.pad(north, (*gap, (0, 128 - POLAR))), jnp.pad(south, (*gap, (128 - POLAR, 0)))], 2
    )[:, 1 : lon_dev + 1]
    outer = [jnp.swapaxes(x[:, :: lon_dev + 1], 1, 2) for x in (north, south)]
    halo_f = jnp.concatenate([outer[0], halo_adj[..., POLAR : lat - POLAR], outer[1]], 3)
    halo = jnp.stack(coupled(halo_zc, [halo_f[f] for f in range(5)], 0))
    out = stencil(
        seat, cot, vw, to_rows(zonal_coef), to_rows(merid_coef), smooth, to_rows(halo), edges, levels
    )
    return from_rows(out, levels)


def lane_of(shape):
    return lax.broadcasted_iota(jnp.int32, shape, len(shape) - 1)


def pair_up(a, b, lane):
    inner = jnp.where(lane < 64, pltpu.roll(b, POLAR, 1), pltpu.roll(b, 128 - POLAR, 1))
    return jnp.where((lane >= POLAR) & (lane < 128 - POLAR), inner, a)


def second_of(pair, lane):
    return jnp.where(lane < 64, pltpu.roll(pair, 128 - POLAR, 1), pltpu.roll(pair, POLAR, 1))


def polar_level(levels, north, south, k, lane):
    lon, rows, _ = north.shape
    near = north.reshape(lon * rows, 128)[pl.ds(k, lon, stride=rows), :]
    far = south.reshape(lon * rows, 128)[pl.ds(levels + k, lon, stride=rows), :]
    return jnp.where(lane < 64, near, far)


def edge_block(levels, front, cot, vw, out):
    fields, chunk, rows, _ = cot.shape
    tiles = rows // levels
    flat_c = cot.reshape(fields * chunk * rows, 128)
    flat_v = vw.reshape(chunk * rows, 128)
    flat_t = cot.at[2].reshape(chunk * rows, 128)

    def product(k, sign):
        c = flat_c[pl.ds(k, fields * chunk * tiles, stride=levels), :]
        v = flat_v[pl.ds(k, chunk * tiles, stride=levels), :]
        c = c.reshape(fields, chunk, tiles, 128)
        out[:fields] = sign * (v.reshape(1, chunk, tiles, 128) * c)

    total = flat_t[pl.ds(0, chunk * tiles, stride=levels), :]
    for k in range(1, levels):
        total = total + flat_t[pl.ds(k, chunk * tiles, stride=levels), :]
    out[fields] = jnp.where(front, 0.0, total.reshape(chunk, tiles, 128))
    pl.when(front)(lambda: product(levels - 1, -1.0))
    pl.when(jnp.logical_not(front))(lambda: product(0, 1.0))


def open_kernel(levels, seat, cot, vw, sent, ends, local, cn, cs, vn, vs, ec, ev, below, sems):
    _, lon, rows, _ = cot.shape
    wide = 2 * levels
    lane = lane_of((lon, 128))
    front = seat[0] == 0
    near, far = pl.ds(0, wide), pl.ds(rows - wide, wide)
    jobs = [(vw.at[:, near], vn), (vw.at[:, far], vs)]
    order = (2, 0, 1, 3, 4)
    for f in order:
        jobs += [(cot.at[f, :, near], cn.at[f]), (cot.at[f, :, far], cs.at[f])]
    for n, e in enumerate((0, lon - 1)):
        jobs += [(cot.at[:, e], ec.at[:, n]), (vw.at[e], ev.at[n])]
    jobs = [pltpu.make_async_copy(a, b, sems.at[n]) for n, (a, b) in enumerate(jobs)]
    for job in jobs:
        job.start()
    jobs[0].wait()
    jobs[1].wait()
    v = [polar_level(levels, vn, vs, k, lane) for k in range(levels)]
    for n, f in enumerate(order):
        jobs[2 + 2 * n].wait()
        jobs[3 + 2 * n].wait()
        c = [polar_level(levels, cn.at[f], cs.at[f], k, lane) for k in range(levels)]
        w = [a * b for a, b in zip(v, c)]
        edge = jnp.where(front, -w[levels - 1], w[0])
        if f == 2:
            run = c[levels - 1]
            below[levels - 1] = run
            for k in range(levels - 2, -1, -1):
                run = run + c[k]
                below[k] = run
            total = jnp.where(front, 0.0, run)
            sent[2] = total
        if f == 4:
            sent[2] = pair_up(edge, sent[2], lane)
        elif f == 2:
            sent[1] = edge
        elif f % 2:
            sent[f // 2] = pair_up(sent[f // 2], edge, lane)
        else:
            sent[f // 2] = edge
        for k in range(0, levels, 2):
            pieces = []
            for at in (k, k + 1):
                a = c[at]
                if at < levels - 1:
                    a = a + w[at + 1]
                if at > 0:
                    a = a - w[at - 1]
                if f == 3:
                    a = a - COUPLE_B * below[at]
                pieces.append(a)
            local[f * levels // 2 + k // 2] = pair_up(pieces[0], pieces[1], lane)
    for job in jobs[12:]:
        job.wait()
    edge_block(levels, front, ec, ev, ends)


def opening(seat, cot, vw, levels):
    _, lon, rows, _ = cot.shape
    tiles, wide = rows // levels, 2 * levels
    f32 = jnp.float32
    place = pl.BlockSpec(memory_space=pl.ANY)
    vmem = pl.BlockSpec(memory_space=pltpu.VMEM)
    return pl.pallas_call(
        functools.partial(open_kernel, levels),
        out_shape=[
            jax.ShapeDtypeStruct((3, lon, 128), f32),
            jax.ShapeDtypeStruct((6, 2, tiles, 128), f32),
            jax.ShapeDtypeStruct((5 * levels // 2, lon, 128), f32),
        ],
        in_specs=[pl.BlockSpec(memory_space=pltpu.SMEM), place, place],
        out_specs=[vmem] * 3,
        scratch_shapes=[
            pltpu.VMEM((5, lon, wide, 128), f32), pltpu.VMEM((5, lon, wide, 128), f32),
            pltpu.VMEM((lon, wide, 128), f32), pltpu.VMEM((lon, wide, 128), f32),
            pltpu.VMEM((5, 2, rows, 128), f32), pltpu.VMEM((2, rows, 128), f32),
            pltpu.VMEM((levels, lon, 128), f32), pltpu.SemaphoreType.DMA((16,)),
        ],
        compiler_params=pltpu.CompilerParams(vmem_limit_bytes=SOME),
        cost_estimate=pl.CostEstimate(flops=9_000_000, bytes_accessed=10_000_000, transcendentals=0),
        name="opening",
    )(seat, cot, vw)


def edge_run_kernel(levels, start, chunk, count, seat, cot, vw, out, cbuf, vbuf, sems):
    def jobs(n):
        at = pl.ds(start + n * chunk, chunk)
        return (
            pltpu.make_async_copy(cot.at[:, at], cbuf.at[n], sems.at[n, 0]),
            pltpu.make_async_copy(vw.at[at], vbuf.at[n], sems.at[n, 1]),
        )

    for n in range(count):
        for job in jobs(n):
            job.start()
    for n in range(count):
        for job in jobs(n):
            job.wait()
        edge_block(
            levels, seat[0] == 0, cbuf.at[n], vbuf.at[n], out.at[:, pl.ds(n * chunk, chunk)]
        )


def edge_run(seat, cot, vw, levels, start, chunk, count):
    fields, lon, rows, _ = cot.shape
    tiles = rows // levels
    place = pl.BlockSpec(memory_space=pl.ANY)
    size = count * chunk
    return pl.pallas_call(
        functools.partial(edge_run_kernel, levels, start, chunk, count),
        out_shape=jax.ShapeDtypeStruct((fields + 1, size, tiles, 128), jnp.float32),
        in_specs=[pl.BlockSpec(memory_space=pltpu.SMEM), place, place],
        out_specs=pl.BlockSpec(memory_space=pltpu.VMEM),
        scratch_shapes=[
            pltpu.VMEM((count, fields, chunk, rows, 128), jnp.float32),
            pltpu.VMEM((count, chunk, rows, 128), jnp.float32),
            pltpu.SemaphoreType.DMA((count, 2)),
        ],
        compiler_params=pltpu.CompilerParams(vmem_limit_bytes=SOME),
        cost_estimate=pl.CostEstimate(
            flops=50_000 * size, bytes_accessed=120_000 * size, transcendentals=0
        ),
        name="edge_run",
    )(seat, cot, vw)


def slots_of(k, nq):
    north, south = range(nq // 2), range(nq // 2, nq)
    return (
        [(k, q) for q in north] + [(k + 1, q) for q in north]
        + [(k + 1, q) for q in south] + [(k, q) for q in south]
    )


def polar_kernel(
    peers, levels, late, chunk,
    cot, vw, zc, fwd, inv, local, got, ends, ct_ref, st_ref, mask_ref,
    smooth, left, right, *rest,
):
    late_out, rest = rest[: len(late)], rest[len(late) :]
    (fwd_ref, inv_ref, x_ref, held, made, back, z, zt, ec, ev, ez, es, flux, spread, below_ref, cbuf, vbuf, ebuf,
     own_sem, wave_sem, send_a, recv_a, send_b, recv_b, col_sem, halo_send, halo_recv, late_in, late_sem) = rest
    me = lax.axis_index("lon")
    front = lax.axis_index("lev") == 0
    _, lon, rows, _ = cot.shape
    wide = 2 * levels
    nq = peers // levels
    span = 2 * POLAR // nq
    cols = 5 * span
    half = cols // 2
    kpad = ct_ref.shape[2]
    lane = lane_of((lon, 128))
    barrier = pltpu.get_barrier_semaphore()

    def ahead(o):
        return lax.rem(me + o, peers)

    def behind(o):
        return lax.rem(me + peers - o, peers)

    def greet(o, _):
        pl.semaphore_signal(barrier, inc=1, device_id={"lon": ahead(o)}, device_id_type=MESH)
        return 0

    lax.fori_loop(1, peers, greet, 0)

    column_jobs = []
    for n, e in enumerate((0, lon - 1)):
        for m, (a, b) in enumerate(
            ((cot.at[:, e], ec.at[:, n]), (vw.at[e], ev.at[n]), (zc.at[e], ez.at[n]))
        ):
            column_jobs.append(pltpu.make_async_copy(a, b, col_sem.at[3 * n + m]))
    late_jobs, late_outs, n = [], [], 0
    for out, (start, size) in zip(late_out, late):
        for at in range(0, size, chunk):
            where = pl.ds(start + at, chunk)
            late_jobs.append((
                pltpu.make_async_copy(cot.at[:, where], cbuf.at[n], late_in.at[n, 0]),
                pltpu.make_async_copy(vw.at[where], vbuf.at[n], late_in.at[n, 1]),
            ))
            late_outs.append(
                pltpu.make_async_copy(ebuf.at[n], out.at[:, pl.ds(at, chunk)], late_sem.at[n])
            )
            n += 1
    wave_jobs = [
        pltpu.make_async_copy(fwd, fwd_ref, wave_sem.at[0]),
        pltpu.make_async_copy(inv, inv_ref, wave_sem.at[1]),
    ]
    for job in column_jobs + wave_jobs:
        job.start()
    for jobs in late_jobs:
        for job in jobs:
            job.start()

    z[...] = jnp.zeros_like(z)
    for f in range(5):
        pair = got[f // 2]
        edge = second_of(pair, lane) if f % 2 else pair
        tail = second_of(got[2], lane) if f == 3 else None
        for k in range(0, levels, 2):
            add = []
            for at in (k, k + 1):
                a = jnp.zeros((lon, 128), jnp.float32)
                if at == levels - 1:
                    a = a + jnp.where(front, edge, 0.0)
                if at == 0:
                    a = a + jnp.where(front, 0.0, edge)
                if f == 3:
                    a = a - COUPLE_B * tail
                add.append(a)
            z[:lon] = local[f * levels // 2 + k // 2] + pair_up(add[0], add[1], lane)
            zt[...] = z[...].T
            for n, (at, q) in enumerate(slots_of(k, nq)):
                d = at * nq + q
                x_ref[d, f * span : (f + 1) * span] = zt[n * span : (n + 1) * span, :128]
                for h in range(0, span, 8):
                    to = f * span + h
                    end = zt[n * span + h : n * span + h + 8, 128:]
                    if to < half:
                        x_ref[d, cols + to : cols + to + 8] = end
                    else:
                        to += cols - half
                        x_ref[d, to : to + 8] += pltpu.roll(end, 64, 1)

    def out_copy(d):
        return pltpu.make_async_remote_copy(
            src_ref=x_ref.at[d], dst_ref=held.at[me], send_sem=send_a.at[d],
            recv_sem=recv_a.at[me], device_id={"lon": d}, device_id_type=MESH,
        )

    def in_copy(s):
        return pltpu.make_async_remote_copy(
            src_ref=x_ref.at[s], dst_ref=held.at[s], send_sem=send_a.at[s],
            recv_sem=recv_a.at[s], device_id={"lon": s}, device_id_type=MESH,
        )

    def back_copy(d):
        return pltpu.make_async_remote_copy(
            src_ref=made.at[d], dst_ref=back.at[me], send_sem=send_b.at[d],
            recv_sem=recv_b.at[me], device_id={"lon": d}, device_id_type=MESH,
        )

    def home_copy(s):
        return pltpu.make_async_remote_copy(
            src_ref=made.at[s], dst_ref=back.at[s], send_sem=send_b.at[s],
            recv_sem=recv_b.at[s], device_id={"lon": s}, device_id_type=MESH,
        )

    pl.semaphore_wait(barrier, peers - 1)
    lax.fori_loop(1, peers, lambda o, c: (out_copy(ahead(o)).start(), c)[1], 0)
    own = pltpu.make_async_copy(x_ref.at[me], held.at[me], own_sem)
    own.start()

    for n, jobs in enumerate(late_jobs):
        for job in jobs:
            job.wait()
        edge_block(levels, front, cbuf.at[n], vbuf.at[n], ebuf.at[n])
        late_outs[n].start()

    for job in wave_jobs:
        job.wait()
    own.wait()
    zero = jnp.zeros((cols, kpad), jnp.float32)
    dot = functools.partial(jnp.dot, precision=HIGHEST, preferred_element_type=jnp.float32)

    def gather(s, carry):
        a, b = carry
        ends = held[s, cols:]
        ends = jnp.concatenate([ends[:, :64], ends[:, 64:]], 0)
        both = dot(held[s, :cols], fwd_ref[:128]) + dot(ends, fwd_ref[128:])
        c, v = both[:, :kpad], both[:, kpad:]
        ct, st = ct_ref[s], st_ref[s]
        return a + (ct * c - st * v), b + (st * c + ct * v)

    def arrive(o, carry):
        s = behind(o)
        in_copy(s).wait_recv()
        return gather(s, carry)

    a, b = lax.fori_loop(1, peers, arrive, gather(me, (zero, zero)))
    mask = jnp.concatenate([mask_ref[...]] * 5, 0)
    a = a * mask
    b = b * mask

    def turn(d):
        ct, st = ct_ref[d], st_ref[d]
        p, q = a * ct + b * st, b * ct - a * st
        y = dot(p, inv_ref[0]) + dot(q, inv_ref[1])
        made[d, :cols] = y[:, :128]
        made[d, cols:] = jnp.concatenate([y[:half, 128:], y[half:, 128:]], 1)

    def depart(o, _):
        turn(ahead(o))
        pl.when(o > 1)(lambda: back_copy(ahead(o - 1)).start())
        return 0

    lax.fori_loop(1, peers, depart, 0)
    turn(me)
    back_copy(ahead(peers - 1)).start()
    mine = pltpu.make_async_copy(made.at[me], back.at[me], own_sem)
    mine.start()
    for job in late_outs:
        job.wait()
    for job in column_jobs:
        job.wait()
    mine.wait()
    lax.fori_loop(1, peers, lambda o, c: (home_copy(behind(o)).wait_recv(), c)[1], 0)

    for f in range(5):
        flat = smooth.at[f].reshape(lon * wide, 128)
        for k in range(0, levels, 2):
            for n, (at, q) in enumerate(slots_of(k, nq)):
                d = at * nq + q
                zt[n * span : (n + 1) * span, :128] = back[d, f * span : (f + 1) * span]
                for h in range(0, span, 8):
                    to = f * span + h
                    if to < half:
                        end = back[d, cols + to : cols + to + 8]
                    else:
                        to += cols - half
                        end = pltpu.roll(back[d, to : to + 8], 64, 1)
                    zt[n * span + h : n * span + h + 8, 128:] = end
            z[...] = zt[...].T
            first = z[:lon]
            flat[pl.ds(k, lon, stride=wide), :] = first
            flat[pl.ds(levels + k, lon, stride=wide), :] = first
            flat[pl.ds(k + 1, lon, stride=wide), :] = pltpu.roll(first, 128 - POLAR, 1)
            flat[pl.ds(levels + k + 1, lon, stride=wide), :] = pltpu.roll(first, POLAR, 1)

    for f in range(5):
        for n, e in enumerate((0, lon - 1)):
            es[f, n] = smooth[f, e]
    spread[...] = jnp.zeros_like(spread)
    column = column_maker(levels, front, ec, ev, es, ends, spread, below_ref)
    for n in range(2):
        field = column(n)
        fields = [field(f)[1] for f in range(5)]
        for v in range(rows // 8):
            zonal = coupled(ez[n, 8 * v : 8 * v + 8], [fields[f][v] for f in range(5)], 0)
            for f in range(5):
                flux[n, f, 8 * v : 8 * v + 8] = zonal[f]
    to_left = pltpu.make_async_remote_copy(
        src_ref=flux.at[0], dst_ref=right, send_sem=halo_send.at[0], recv_sem=halo_recv.at[0],
        device_id={"lon": behind(1)}, device_id_type=MESH,
    )
    to_right = pltpu.make_async_remote_copy(
        src_ref=flux.at[1], dst_ref=left, send_sem=halo_send.at[1], recv_sem=halo_recv.at[1],
        device_id={"lon": ahead(1)}, device_id_type=MESH,
    )
    to_left.start()
    to_right.start()
    lax.fori_loop(1, peers, lambda o, c: (out_copy(ahead(o)).wait_send(), c)[1], 0)
    lax.fori_loop(1, peers, lambda o, c: (back_copy(ahead(o)).wait_send(), c)[1], 0)
    to_left.wait()
    to_right.wait()


def hold(a):
    return pltpu.with_memory_space_constraint(jnp.asarray(a), pltpu.HBM)


def polar_path(cot, vw, zc, local, got, ends, cutoff, levels, peers, late, chunk):
    _, lon, rows, _ = cot.shape
    tiles, wide = rows // levels, 2 * levels
    nq = peers // levels
    nlon = peers * lon
    span = cutoff.shape[0] // nq
    kpad = (KMAX + 1 + 127) // 128 * 128
    wave = np.arange(kpad)
    fwd = np.concatenate(angles(np.arange(lon)[:, None], wave[None, :], nlon), axis=1)
    inv = np.stack(angles(wave[:, None], np.arange(lon)[None, :], nlon))
    short = 192 - lon
    fwd = np.pad(fwd, ((0, short), (0, 0)))
    inv = np.pad(inv, ((0, 0), (0, 0), (0, short)))
    ct, st = angles(np.arange(peers)[:, None, None] * lon, wave[None, None, :], nlon)
    mine = lax.dynamic_slice_in_dim(cutoff, lax.axis_index("lon") % nq * span, span)
    weight = np.where(wave == 0, 1.0 / nlon, 2.0 / nlon).astype(np.float32)
    mask = jnp.where(jnp.asarray(wave, jnp.int32)[None, :] <= mine[:, None], weight[None, :], 0.0)
    vmem = pl.BlockSpec(memory_space=pltpu.VMEM)
    place = pl.BlockSpec(memory_space=pltpu.HBM)
    dma = pltpu.SemaphoreType.DMA
    f32 = jnp.float32
    shape = (peers, 5 * span + 5 * span // 2, 128)
    blocks = sum(size for _, size in late) // chunk
    return pl.pallas_call(
        functools.partial(polar_kernel, peers, levels, late, chunk),
        out_shape=[
            jax.ShapeDtypeStruct((5, lon, wide, 128), f32),
            jax.ShapeDtypeStruct((5, rows, 128), f32),
            jax.ShapeDtypeStruct((5, rows, 128), f32),
        ] + [jax.ShapeDtypeStruct((6, size, tiles, 128), f32) for _, size in late],
        in_specs=[place] * 5 + [vmem] * 6,
        out_specs=[vmem] * 3 + [place] * len(late),
        scratch_shapes=[
            pltpu.VMEM(fwd.shape, f32), pltpu.VMEM(inv.shape, f32),
            pltpu.VMEM(shape, f32), pltpu.VMEM(shape, f32), pltpu.VMEM(shape, f32),
            pltpu.VMEM(shape, f32), pltpu.VMEM((256, 128), f32), pltpu.VMEM((128, 256), f32),
            pltpu.VMEM((5, 2, rows, 128), f32), pltpu.VMEM((2, rows, 128), f32),
            pltpu.VMEM((2, rows, 128), f32), pltpu.VMEM((5, 2, wide, 128), f32),
            pltpu.VMEM((2, 5, rows, 128), f32), pltpu.VMEM((1, 5, rows, 128), f32),
            pltpu.VMEM((1, rows, 128), f32),
            pltpu.VMEM((blocks, 5, chunk, rows, 128), f32),
            pltpu.VMEM((blocks, chunk, rows, 128), f32),
            pltpu.VMEM((blocks, 6, chunk, tiles, 128), f32),
            dma(()), dma((2,)), dma((peers,)), dma((peers,)), dma((peers,)), dma((peers,)),
            dma((6,)), dma((2,)), dma((2,)), dma((blocks, 2)), dma((blocks,)),
        ],
        compiler_params=pltpu.CompilerParams(
            collective_id=1, has_side_effects=True, vmem_limit_bytes=30 << 20
        ),
        cost_estimate=pl.CostEstimate(flops=8_000_000_000, bytes_accessed=60_000_000, transcendentals=0),
        name="polar_path",
    )(cot, vw, zc, hold(fwd), hold(inv), local, got, ends, ct, st, mask)


def column_maker(levels, front, cot, vw, smooth, edges, spread, below_ref):
    _, _, rows, _ = cot.shape
    tiles = rows // levels
    parts = rows // 8
    edge_at = jnp.where(front, levels - 1, 0)
    row = lax.broadcasted_iota(jnp.int32, (8, 128), 0)
    lane = lane_of((8, 128))
    k = lax.rem(row, levels)
    north = (row < levels) & (lane < POLAR)
    south = (row >= levels) & (lane >= 128 - POLAR)
    at = [pl.ds(8 * v, 8) for v in range(parts)]

    def column(l, side=0):
        for f in range(5):
            spread[side, f, pl.ds(edge_at, tiles, stride=levels), :] = edges[f, l]
        for n in range(levels):
            below_ref[side, pl.ds(n, tiles, stride=levels), :] = edges[5, l]
        wind = [vw[l, a] for a in at]
        under = [jnp.where(k > 0, a, 0.0) for a in wind]
        over = [jnp.where(k < levels - 1, a, 0.0) for a in wind]

        def field(f):
            whole, inner = [], []
            for v in range(parts):
                c = cot[f, l, at[v]]
                a = c + (pltpu.roll(under[v] * c, 7, 0) - pltpu.roll(over[v] * c, 1, 0))
                a = a + spread[side, f, at[v]]
                if f == 3:
                    run, r = cot[2, l, at[v]], 1
                    while r < levels:
                        run = run + jnp.where(k < levels - r, pltpu.roll(run, 8 - r, 0), 0.0)
                        r *= 2
                    a = a - COUPLE_B * (run + below_ref[side, at[v]])
                whole.append(a)
                if v == 0:
                    a = jnp.where(north, smooth[f, l], a)
                if v == parts - 1:
                    a = jnp.where(south, smooth[f, l], a)
                inner.append(a)
            return whole, inner

        return field

    return column


def lat_change(levels, m):
    row = lax.broadcasted_iota(jnp.int32, (8, 128), 0)
    lane = lane_of((8, 128))
    top = row < levels
    turned = [pltpu.roll(a, levels, 0) for a in m]
    zero = jnp.zeros((8, 128), jnp.float32)
    tile = [jnp.where(top, a, b) for a, b in zip([zero] + turned, turned + [zero])]
    out = []
    for v, a in enumerate(m):
        near = pltpu.roll(jnp.where(lane == 127, tile[v], a), 1, 1)
        far = pltpu.roll(jnp.where(lane == 0, tile[v + 1], a), 127, 1)
        out.append(far - near)
    return out


def strip_kernel(levels, start, steps, first, last, seat, cot, vw, zc, mc, smooth, edges, *rest):
    rest = list(rest)
    if first:
        left = rest.pop(0)
    else:
        wait_in, prior_in, _ = rest.pop(0), rest.pop(0), rest.pop(0)
    if last:
        right = rest.pop(0)
    out, wait, prior, ready, spread, below_ref, sems = rest[:7]
    _, chunk, rows, _ = cot.shape
    parts = rows // 8
    g = pl.program_id(0)
    slot = lax.rem(g, 2)

    def first_copy():
        return pltpu.make_async_copy(
            ready.at[0, :, pl.ds(1, chunk - 1)], out.at[:, pl.ds(0, chunk - 1)], sems.at[0]
        )

    def copy(at):
        s = lax.rem(at, 2)
        return pltpu.make_async_copy(
            ready.at[s], out.at[:, pl.ds(start + at * chunk - 1, chunk)], sems.at[s]
        )

    def act(at, what):
        if first:
            pl.when(at == 0)(lambda: getattr(first_copy(), what)())
            pl.when(at > 0)(lambda: getattr(copy(at), what)())
        else:
            getattr(copy(at), what)()

    @pl.when(g == 0)
    def _():
        spread[...] = jnp.zeros_like(spread)
        if first:
            prior[...] = left[...]
            wait[...] = jnp.zeros_like(wait)
        else:
            prior[...] = prior_in[...]
            wait[...] = wait_in[...]

    pl.when(g >= 2)(lambda: act(g - 2, "wait"))
    column = column_maker(levels, seat[0] == 0, cot, vw, smooth, edges, spread, below_ref)
    at = [pl.ds(8 * v, 8) for v in range(parts)]

    def flux_of(l, side):
        field = column(l, side)
        zcs = [zc[l, a] for a in at]
        mcs = [mc[l, a] for a in at]
        whole3, f3 = field(3)
        half3 = [COUPLE_H * a for a in f3]
        parted, zonal = [None] * 5, [None] * 5

        def close(f, whole, inner, add_zonal=None, add_merid=None):
            z = [a * b for a, b in zip(zcs, inner)]
            m = [a * b for a, b in zip(mcs, inner)]
            if add_zonal is not None:
                z = [a + b for a, b in zip(z, add_zonal)]
            if add_merid is not None:
                m = [a + b for a, b in zip(m, add_merid)]
            zonal[f] = z
            parted[f] = [a + b for a, b in zip(whole, lat_change(levels, m))]

        whole, f0 = field(0)
        close(0, whole, f0, add_zonal=half3)
        whole, f1 = field(1)
        close(1, whole, f1, add_merid=half3)
        close(3, whole3, f3, [COUPLE_G * a for a in f0], [COUPLE_G * a for a in f1])
        for f in (2, 4):
            close(f, *field(f))
        return parted, zonal

    def one(l):
        parted, zonal = flux_of(l, 0)
        for f in range(5):
            for v in range(parts):
                ready[slot, f, l, at[v]] = wait[f, at[v]] + zonal[f][v]
                wait[f, at[v]] = parted[f][v] - prior[f, at[v]]
                prior[f, at[v]] = zonal[f][v]

    def two(n, _):
        l = 2 * n
        parted, zonal = flux_of(l, 0)
        for f in range(5):
            for v in range(parts):
                ready[slot, f, l, at[v]] = wait[f, at[v]] + zonal[f][v]
                parted[f][v] = parted[f][v] - prior[f, at[v]]
        later, after = flux_of(l + 1, 1)
        for f in range(5):
            for v in range(parts):
                ready[slot, f, l + 1, at[v]] = parted[f][v] + after[f][v]
                wait[f, at[v]] = later[f][v] - zonal[f][v]
                prior[f, at[v]] = after[f][v]
        return 0

    lax.fori_loop(0, chunk // 2, two, 0)
    if chunk % 2:
        one(chunk - 1)
    act(g, "start")

    @pl.when(g == steps - 1)
    def _():
        if last:
            final, last_sem = rest[7:]
            for f in range(5):
                final[f, 0] = wait[f] + right[f]
            end = pltpu.make_async_copy(
                final, out.at[:, pl.ds(start + steps * chunk - 1, 1)], last_sem
            )
            end.start()
        if steps > 1:
            act(g - 1, "wait")
        act(g, "wait")
        if last:
            end.wait()


def strip(seat, cot, vw, zc, mc, smooth, edges, state, right, levels, start, steps, chunk):
    _, lon, rows, _ = cot.shape
    tiles = rows // levels
    at = start // chunk
    first, last = len(state) == 1, right is not None
    field = lambda n: pl.BlockSpec((5, chunk, n, 128), lambda g, s: (0, at + g, 0, 0))
    plain = pl.BlockSpec((chunk, rows, 128), lambda g, s: (at + g, 0, 0))
    whole = pl.BlockSpec((5, rows, 128), lambda g, s: (0, 0, 0))
    place = pl.BlockSpec(memory_space=pl.ANY)
    in_specs = [field(rows), plain, plain, plain, field(2 * levels),
                pl.BlockSpec((6, chunk, tiles, 128), lambda g, s: (0, g, 0, 0))]
    in_specs += [whole] if first else [whole, whole, place]
    args = [seat, cot, vw, zc, mc, smooth, edges, *state]
    aliases = {} if first else {len(args) - 1: 0}
    if last:
        in_specs.append(whole)
        args.append(right)
    one = jax.ShapeDtypeStruct((5, rows, 128), jnp.float32)
    held = [pltpu.VMEM((5, rows, 128), jnp.float32)] * 2
    scratch = [
        pltpu.VMEM((2, 5, chunk, rows, 128), jnp.float32),
        pltpu.VMEM((2, 5, rows, 128), jnp.float32),
        pltpu.VMEM((2, rows, 128), jnp.float32),
        pltpu.SemaphoreType.DMA((2,)),
    ]
    if last:
        scratch = held + scratch + [
            pltpu.VMEM((5, 1, rows, 128), jnp.float32), pltpu.SemaphoreType.DMA(()),
        ]
    got = pl.pallas_call(
        functools.partial(strip_kernel, levels, start, steps, first, last),
        out_shape=[jax.ShapeDtypeStruct(cot.shape, jnp.float32)] + ([] if last else [one, one]),
        grid_spec=pltpu.PrefetchScalarGridSpec(
            num_scalar_prefetch=1,
            grid=(steps,),
            in_specs=in_specs,
            out_specs=[place] + ([] if last else [whole, whole]),
            scratch_shapes=scratch,
        ),
        input_output_aliases=aliases,
        compiler_params=pltpu.CompilerParams(vmem_limit_bytes=SOME),
        cost_estimate=pl.CostEstimate(
            flops=30 * 5 * steps * chunk * rows * 128,
            bytes_accessed=4 * 14 * steps * chunk * rows * 128,
            transcendentals=0,
        ),
        name="strip",
    )(*args)
    return got[0] if last else [got[1], got[2], got[0]]


def fast_body(cotangent, zonal_coef, merid_coef, vertical_wind, cutoff):
    levels, lon_dev, lat = cotangent.shape[1:]
    peers = lax.axis_size("lon")
    seat = lax.axis_index("lev").astype(jnp.int32)[None]
    cot, vw = to_rows(cotangent), to_rows(vertical_wind)
    zc, mc = to_rows(zonal_coef), to_rows(merid_coef)
    cot, vw, zc, mc = (hold(a) for a in (cot, vw, zc, mc))
    trade = lambda a: lax.ppermute(a, "lev", [(0, 1), (1, 0)])
    chunk = max(d for d in range(2, 13) if lon_dev % d == 0 and d not in (11, 12))
    blocks = lon_dev // chunk
    cuts = sorted({max(1, blocks // 3), max(1, 2 * blocks // 3), max(1, blocks - 1), blocks})
    parts = [(a * chunk, (b - a) * chunk) for a, b in zip([0] + cuts[:-1], cuts)]

    sent, ends, local = opening(seat, cot, vw, levels)
    polar_got, ends_got = trade(sent), trade(ends)
    token, _ = lax.optimization_barrier((seat, sent))
    edges = []
    for start, size in parts[:2]:
        part = edge_run(token, cot, vw, levels, start, chunk, size // chunk)
        edges.append(trade(part))
        token, _ = lax.optimization_barrier((token, part))
    polar_got, ends_got, token = lax.optimization_barrier((polar_got, ends_got, token))
    smooth, left, right, *later = polar_path(
        cot, vw, zc, local, polar_got, ends_got, cutoff, levels, peers, tuple(parts[2:]), chunk
    )
    edges += [trade(part) for part in later]
    state = [left]
    for n, (start, size) in enumerate(parts):
        end = right if n == len(parts) - 1 else None
        state = strip(
            seat, cot, vw, zc, mc, smooth, edges[n], state, end, levels, start, size // chunk, chunk
        )
    return from_rows(state, levels)


def body(cotangent, zonal_coef, merid_coef, vertical_wind, cutoff):
    levels, lon_dev, lat = cotangent.shape[1:]
    peers, count = lax.axis_size("lon"), lax.axis_size("lev")
    span = 2 * POLAR * levels // peers
    fast = (
        count == 2 and levels * 2 == 8 and peers % (2 * levels) == 0 and lat % 256 == 0
        and span % 16 == 0 and 128 < lon_dev <= 192 and cutoff.shape[0] == 2 * POLAR
    )
    return (fast_body if fast else plain_body)(
        cotangent, zonal_coef, merid_coef, vertical_wind, cutoff
    )


def solution(mesh):
    return jax.shard_map(
        body,
        mesh=mesh,
        in_specs=(
            P(None, "lev", "lon", None),
            P("lev", "lon", None),
            P("lev", "lon", None),
            P("lev", "lon", None),
            P(),
        ),
        out_specs=P(None, "lev", "lon", None),
        check_vma=False,
    )
```

```python
import functools
import math

import jax
import jax.numpy as jnp
import numpy as np
from jax import lax
from jax.experimental import pallas as pl
from jax.experimental.pallas import tpu as pltpu
from jax.sharding import PartitionSpec as P

POLAR = 32
KMAX = 360
COUPLE_G = 0.3
COUPLE_H = 0.3
COUPLE_B = 0.2
MESH = pl.DeviceIdType.MESH
HIGHEST = lax.Precision.HIGHEST
ROOM = 61 << 20
SOME = 36 << 20


def angles(left, right, period):
    phase = (left * right) % period * (2.0 * math.pi / period)
    return np.cos(phase).astype(np.float32), np.sin(phase).astype(np.float32)


def filter_kernel(
    peers, packed, x_ref, fwd_ref, inv_ref, ct_ref, st_ref, mask_ref, out_ref, held, made,
    own_sem, send_a, recv_a, send_b, recv_b,
):
    me = lax.axis_index("lon")
    kpad = ct_ref.shape[2]
    barrier = pltpu.get_barrier_semaphore()

    def greet(o, _):
        pl.semaphore_signal(
            barrier, inc=1, device_id={"lon": lax.rem(me + o, peers)}, device_id_type=MESH
        )
        return 0

    lax.fori_loop(1, peers, greet, 0)
    pl.semaphore_wait(barrier, peers - 1)

    def out_copy(o):
        d = lax.rem(me + o, peers)
        return pltpu.make_async_remote_copy(
            src_ref=x_ref.at[d], dst_ref=held.at[me], send_sem=send_a.at[d],
            recv_sem=recv_a.at[me], device_id={"lon": d}, device_id_type=MESH,
        )

    def in_copy(o):
        s = lax.rem(me + o, peers)
        return pltpu.make_async_remote_copy(
            src_ref=x_ref.at[s], dst_ref=held.at[s], send_sem=send_a.at[s],
            recv_sem=recv_a.at[s], device_id={"lon": s}, device_id_type=MESH,
        )

    def back_copy(o):
        d = lax.rem(me + o, peers)
        return pltpu.make_async_remote_copy(
            src_ref=made.at[d], dst_ref=out_ref.at[me], send_sem=send_b.at[d],
            recv_sem=recv_b.at[me], device_id={"lon": d}, device_id_type=MESH,
        )

    def home_copy(o):
        s = lax.rem(me + o, peers)
        return pltpu.make_async_remote_copy(
            src_ref=made.at[s], dst_ref=out_ref.at[s], send_sem=send_b.at[s],
            recv_sem=recv_b.at[s], device_id={"lon": s}, device_id_type=MESH,
        )

    lax.fori_loop(1, peers, lambda o, c: (out_copy(o).start(), c)[1], 0)
    own = pltpu.make_async_copy(x_ref.at[me], held.at[me], own_sem)
    own.start()
    own.wait()
    cols = mask_ref.shape[0]
    half = cols // 2
    zero = jnp.zeros((cols, kpad), jnp.float32)
    dot = functools.partial(jnp.dot, precision=HIGHEST, preferred_element_type=jnp.float32)

    def gather(s, carry):
        a, b = carry
        if packed:
            ends = held[s, cols:]
            ends = jnp.concatenate([ends[:, :64], ends[:, 64:]], 0)
            both = dot(held[s, :cols], fwd_ref[:128]) + dot(ends, fwd_ref[128:])
        else:
            both = dot(held[s], fwd_ref[...])
        c, v = both[:, :kpad], both[:, kpad:]
        ct, st = ct_ref[s], st_ref[s]
        return a + (ct * c - st * v), b + (st * c + ct * v)

    def arrive(o, carry):
        in_copy(o).wait_recv()
        return gather(lax.rem(me + o, peers), carry)

    a, b = lax.fori_loop(1, peers, arrive, gather(me, (zero, zero)))
    a = a * mask_ref[...]
    b = b * mask_ref[...]

    def spread(d):
        ct, st = ct_ref[d], st_ref[d]
        p, q = a * ct + b * st, b * ct - a * st
        if packed:
            y = dot(p, inv_ref[0]) + dot(q, inv_ref[1])
            made[d, :cols] = y[:, :128]
            made[d, cols:] = jnp.concatenate([y[:half, 128:], y[half:, 128:]], 1)
        else:
            made[d] = dot(p, inv_ref[0]) + dot(q, inv_ref[1])

    def depart(o, _):
        spread(lax.rem(me + o, peers))
        pl.when(o > 1)(lambda: back_copy(o - 1).start())
        return 0

    lax.fori_loop(1, peers, depart, 0)
    spread(me)
    back_copy(peers - 1).start()
    mine = pltpu.make_async_copy(made.at[me], out_ref.at[me], own_sem)
    mine.start()
    mine.wait()
    lax.fori_loop(1, peers, lambda o, c: (home_copy(o).wait_recv(), c)[1], 0)
    lax.fori_loop(1, peers, lambda o, c: (out_copy(o).wait_send(), c)[1], 0)
    lax.fori_loop(1, peers, lambda o, c: (back_copy(o).wait_send(), c)[1], 0)


def polar_filter(x, cutoff, peers):
    _, cols, lon_dev = x.shape
    nlon = peers * lon_dev
    rows = cutoff.shape[0] // peers
    kpad = (KMAX + 1 + 127) // 128 * 128
    wave = np.arange(kpad)
    fwd = np.concatenate(angles(np.arange(lon_dev)[:, None], wave[None, :], nlon), axis=1)
    inv = np.stack(angles(wave[:, None], np.arange(-1, lon_dev + 1)[None, :] % nlon, nlon))
    over, wider = lon_dev - 128, lon_dev + 2 - 128
    packed = over > 0 and wider <= 64 and cols % 16 == 0
    half = cols // 2
    if packed:
        fwd = np.pad(fwd, ((0, 64 - over), (0, 0)))
        inv = np.pad(inv, ((0, 0), (0, 0), (0, 64 - wider)))
        ends = jnp.pad(x[..., 128:], ((0, 0), (0, 0), (0, 64 - over)))
        x = jnp.concatenate([x[..., :128], jnp.concatenate([ends[:, :half], ends[:, half:]], 2)], 1)
        shape = (peers, cols + half, 128)
    else:
        shape = (peers, cols, lon_dev + 2)
    ct, st = angles(np.arange(peers)[:, None, None] * lon_dev, wave[None, None, :], nlon)
    mine = lax.dynamic_slice_in_dim(cutoff, lax.axis_index("lon") * rows, rows)
    weight = np.where(wave == 0, 1.0 / nlon, 2.0 / nlon).astype(np.float32)
    mask = jnp.where(jnp.asarray(wave, jnp.int32)[None, :] <= mine[:, None], weight[None, :], 0.0)
    mask = jnp.tile(mask, (cols // rows, 1))
    vmem = pl.BlockSpec(memory_space=pltpu.VMEM)
    dma = pltpu.SemaphoreType.DMA
    y = pl.pallas_call(
        functools.partial(filter_kernel, peers, packed),
        out_shape=jax.ShapeDtypeStruct(shape, jnp.float32),
        in_specs=[vmem] * 6,
        out_specs=vmem,
        scratch_shapes=[
            pltpu.VMEM(x.shape, jnp.float32),
            pltpu.VMEM(shape, jnp.float32),
            dma(()), dma((peers,)), dma((peers,)), dma((peers,)), dma((peers,)),
        ],
        compiler_params=pltpu.CompilerParams(
            collective_id=0, has_side_effects=True, vmem_limit_bytes=24 << 20
        ),
        cost_estimate=pl.CostEstimate(flops=8_000_000_000, bytes_accessed=60_000_000, transcendentals=0),
        name="polar_filter",
    )(x, fwd, inv, ct, st, mask)
    if not packed:
        return y
    ends = jnp.concatenate([y[:, cols:, :wider], y[:, cols:, 64 : 64 + wider]], 1)
    return jnp.concatenate([y[:, :cols], ends], 2)


def to_rows(x):
    *lead, levels, lon, lat = x.shape
    n = len(lead)
    x = x.reshape(*lead, levels, lon, lat // 128, 128)
    x = x.transpose(*range(n), n + 1, n + 2, n, n + 3)
    return x.reshape(*lead, lon, lat // 128 * levels, 128)


def from_rows(x, levels):
    *lead, lon, rows, _ = x.shape
    n = len(lead)
    x = x.reshape(*lead, lon, rows // levels, levels, 128)
    x = x.transpose(*range(n), n + 2, n, n + 1, n + 3)
    return x.reshape(*lead, levels, lon, rows // levels * 128)


def chunk_of(lon):
    return max(d for d in range(1, 21) if lon % d == 0)


def edge_kernel(levels, choose, seat, cot, vw, *outs):
    fields, chunk, rows, _ = cot.shape
    tiles = rows // levels
    flat_c = cot.reshape(fields * chunk * rows, 128)
    flat_v = vw.reshape(chunk * rows, 128)
    sends = outs[: 1 if choose else 2]

    def level(ref, count, k):
        return ref[pl.ds(k, count * tiles, stride=levels), :] if levels > 1 else ref[...]

    def product(k, sign, out):
        c = level(flat_c, fields * chunk, k).reshape(fields, chunk, tiles, 128)
        v = level(flat_v, chunk, k).reshape(1, chunk, tiles, 128)
        out[:fields] = sign * (v * c)

    flat_t = cot.at[2].reshape(chunk * rows, 128)
    total = level(flat_t, chunk, 0)
    for k in range(1, levels):
        total = total + level(flat_t, chunk, k)
    total = total.reshape(chunk, tiles, 128)
    if choose:
        sends[0][fields] = jnp.where(seat[0] == 0, 0.0, total)
        pl.when(seat[0] == 0)(lambda: product(levels - 1, -1.0, sends[0]))
        pl.when(seat[0] != 0)(lambda: product(0, 1.0, sends[0]))
    else:
        product(0, 1.0, sends[0])
        product(levels - 1, -1.0, sends[1])
        outs[2][...] = total


def edges_of(seat, cot, vw, levels, choose):
    fields, lon, rows, _ = cot.shape
    tiles = rows // levels
    chunk = chunk_of(lon)
    n = 1 if choose else 2
    wide = fields + 1 if choose else fields
    return pl.pallas_call(
        functools.partial(edge_kernel, levels, choose),
        out_shape=[jax.ShapeDtypeStruct((wide, lon, tiles, 128), jnp.float32)] * n
        + [jax.ShapeDtypeStruct((lon, tiles, 128), jnp.float32)] * (n - 1),
        grid_spec=pltpu.PrefetchScalarGridSpec(
            num_scalar_prefetch=1,
            grid=(lon // chunk,),
            in_specs=[
                pl.BlockSpec((fields, chunk, rows, 128), lambda g, s: (0, g, 0, 0)),
                pl.BlockSpec((chunk, rows, 128), lambda g, s: (g, 0, 0)),
            ],
            out_specs=[pl.BlockSpec((wide, chunk, tiles, 128), lambda g, s: (0, g, 0, 0))] * n
            + [pl.BlockSpec((chunk, tiles, 128), lambda g, s: (g, 0, 0))] * (n - 1),
        ),
        compiler_params=pltpu.CompilerParams(vmem_limit_bytes=24 << 20),
        cost_estimate=pl.CostEstimate(flops=10_000_000, bytes_accessed=22_000_000, transcendentals=0),
        name="edges",
    )(seat, cot, vw)


def coupled(coef, fields, first):
    flux = [coef * f for f in fields]
    flux[first] = flux[first] + COUPLE_H * fields[3]
    flux[3] = flux[3] + COUPLE_G * fields[first]
    return flux


def stencil_kernel(levels, steps, n_edge, seat, cot, vw, zc, mc, smooth, halo, *rest):
    edges = rest[:n_edge]
    tail = edges[0].at[5] if n_edge == 1 else rest[n_edge]
    rest = rest[1:] if n_edge > 1 else rest
    edge_at = (1 - seat[0]) * (levels - 1)
    out, ready, final, wait, prior, spread, below_ref, sems, last_sem = rest[n_edge:]
    _, chunk, rows, _ = cot.shape
    tiles = rows // levels
    g = pl.program_id(0)
    slot = lax.rem(g, 2)
    lane = lax.broadcasted_iota(jnp.int32, (rows, 128), 1)
    row = lax.broadcasted_iota(jnp.int32, (rows, 128), 0)
    k = lax.rem(row, levels)
    cap_lane = lax.broadcasted_iota(jnp.int32, (2 * levels, 128), 1)
    cap_row = lax.broadcasted_iota(jnp.int32, (2 * levels, 128), 0)
    north = (cap_row < levels) & (cap_lane < POLAR)
    south = (cap_row >= levels) & (cap_lane >= 128 - POLAR)

    def first_copy():
        return pltpu.make_async_copy(
            ready.at[0, :, pl.ds(1, chunk - 1)], out.at[:, pl.ds(0, chunk - 1)], sems.at[0]
        )

    def copy(at):
        s = lax.rem(at, 2)
        return pltpu.make_async_copy(
            ready.at[s], out.at[:, pl.ds(at * chunk - 1, chunk)], sems.at[s]
        )

    @pl.when(g == 0)
    def _():
        spread[...] = jnp.zeros_like(spread)
        for f in range(5):
            prior[f] = halo[f, 0]
            wait[f] = jnp.zeros((rows, 128), jnp.float32)

    pl.when(g == 2)(lambda: first_copy().wait())
    pl.when(g > 2)(lambda: copy(g - 2).wait())

    def put(ref, at, value):
        if levels > 1:
            ref[pl.ds(at, tiles, stride=levels), :] = value
        else:
            ref[...] = value

    def one(l, _):
        for f in range(5):
            if n_edge == 1:
                put(spread.at[0, f], edge_at, edges[0][f, l])
            else:
                put(spread.at[0, f], levels - 1, edges[0][f, l])
                put(spread.at[1, f], 0, edges[1][f, l])
        for at in range(levels):
            put(below_ref, at, tail[l])
        wind = vw[l]
        base, fields = [], []
        for f in range(5):
            c = cot[f, l]
            w = wind * c
            a = c
            if levels > 1:
                up = jnp.where(k < levels - 1, pltpu.roll(w, rows - 1, 0), 0.0)
                a = a + (up - jnp.where(k > 0, pltpu.roll(w, 1, 0), 0.0))
            for n in range(n_edge):
                a = a + spread[n, f]
            if f == 3:
                theta = cot[2, l]
                below = below_ref[...] + theta
                for r in range(1, levels):
                    below = below + jnp.where(k < levels - r, pltpu.roll(theta, rows - r, 0), 0.0)
                a = a - COUPLE_B * below
            base.append(a)
            s = smooth[f, l]
            top = jnp.where(north, s, a[: 2 * levels])
            low = jnp.where(south, s, a[rows - 2 * levels :])
            fields.append(jnp.concatenate([top, a[2 * levels : rows - 2 * levels], low], 0))
        zonal = coupled(zc[l], fields, 0)
        merid = coupled(mc[l], fields, 1)
        for f in range(5):
            ready[slot, f, l] = wait[f] + zonal[f]
            left = pltpu.roll(merid[f], 1, 1)
            over = jnp.where(row < levels, 0.0, pltpu.roll(left, levels, 0))
            left = jnp.where(lane == 0, over, left)
            right = pltpu.roll(merid[f], 127, 1)
            over = jnp.where(row >= rows - levels, 0.0, pltpu.roll(right, rows - levels, 0))
            right = jnp.where(lane == 127, over, right)
            wait[f] = base[f] + (right - left) - prior[f]
            prior[f] = zonal[f]
        return 0

    lax.fori_loop(0, chunk, one, 0)
    pl.when(g == 0)(lambda: first_copy().start())
    pl.when(g > 0)(lambda: copy(g).start())

    @pl.when(g == steps - 1)
    def _():
        for f in range(5):
            final[f, 0] = wait[f] + halo[f, 1]
        end = pltpu.make_async_copy(final, out.at[:, pl.ds(steps * chunk - 1, 1)], last_sem)
        end.start()
        copy(g - 1).wait() if steps > 2 else first_copy().wait()
        copy(g).wait()
        end.wait()


def stencil(seat, cot, vw, zc, mc, smooth, halo, edges, levels):
    _, lon, rows, _ = cot.shape
    tiles = rows // levels
    chunk = chunk_of(lon)
    steps = lon // chunk
    field = lambda n: pl.BlockSpec((5, chunk, n, 128), lambda g, s: (0, g, 0, 0))
    plain = lambda n: pl.BlockSpec((chunk, n, 128), lambda g, s: (g, 0, 0))
    return pl.pallas_call(
        functools.partial(stencil_kernel, levels, steps, min(len(edges), 2)),
        out_shape=jax.ShapeDtypeStruct(cot.shape, jnp.float32),
        grid_spec=pltpu.PrefetchScalarGridSpec(
            num_scalar_prefetch=1,
            grid=(steps,),
            in_specs=[field(rows), plain(rows), plain(rows), plain(rows), field(2 * levels),
                      pl.BlockSpec((5, 2, rows, 128), lambda g, s: (0, 0, 0, 0))]
            + [pl.BlockSpec((6, chunk, tiles, 128), lambda g, s: (0, g, 0, 0))]
            if len(edges) == 1
            else [field(rows), plain(rows), plain(rows), plain(rows), field(2 * levels),
                  pl.BlockSpec((5, 2, rows, 128), lambda g, s: (0, 0, 0, 0)),
                  field(tiles), field(tiles), plain(tiles)],
            out_specs=pl.BlockSpec(memory_space=pl.ANY),
            scratch_shapes=[
                pltpu.VMEM((2, 5, chunk, rows, 128), jnp.float32),
                pltpu.VMEM((5, 1, rows, 128), jnp.float32),
                pltpu.VMEM((5, rows, 128), jnp.float32),
                pltpu.VMEM((5, rows, 128), jnp.float32),
                pltpu.VMEM((min(len(edges), 2), 5, rows, 128), jnp.float32),
                pltpu.VMEM((rows, 128), jnp.float32),
                pltpu.SemaphoreType.DMA((2,)),
                pltpu.SemaphoreType.DMA(()),
            ],
        ),
        compiler_params=pltpu.CompilerParams(vmem_limit_bytes=40 << 20),
        cost_estimate=pl.CostEstimate(
            flops=30 * 5 * lon * rows * 128, bytes_accessed=4 * 14 * lon * rows * 128, transcendentals=0
        ),
        name="stencil",
    )(seat, cot, vw, zc, mc, smooth, halo, *edges)


def swap_levels(first, last, total):
    count = lax.axis_size("lev")
    if count == 2:
        seat = lax.axis_index("lev")
        lead = jnp.concatenate([first, total[None]], 0)
        trail = jnp.concatenate([last, jnp.zeros_like(total)[None]], 0)
        got = lax.ppermute(jnp.where(seat == 0, trail, lead), "lev", [(0, 1), (1, 0)])
        return jnp.where(seat == 0, got[:5], 0.0), jnp.where(seat == 1, got[:5], 0.0), got[5]
    up = lax.ppermute(first, "lev", [(i + 1, i) for i in range(count - 1)])
    down = lax.ppermute(last, "lev", [(i, i + 1) for i in range(count - 1)])
    return up, down, later_sum(total)


def later_sum(local):
    count = lax.axis_size("lev")
    total = jnp.zeros_like(local)
    for r in range(1, count):
        total = total + lax.ppermute(local, "lev", [(i + r, i) for i in range(count - r)])
    return total


def ask_levels(cot, vw):
    return swap_levels(vw[0] * cot[:, 0], vw[-1] * cot[:, -1], cot[2].sum(0))


def adjoint_part(cot, vw, up, down, later):
    weighted = vw[None] * cot
    above = jnp.concatenate([weighted[:, 1:], up[:, None]], 1)
    under = jnp.concatenate([down[:, None], weighted[:, :-1]], 1)
    below = [later + cot[2, -1]]
    for k in range(cot.shape[1] - 2, -1, -1):
        below.insert(0, below[0] + cot[2, k])
    parts = cot + (above - under)
    return jnp.concatenate(
        [parts[:3], parts[3:4] - COUPLE_B * jnp.stack(below)[None], parts[4:]], 0
    )


def polar_cut(x):
    return jnp.concatenate([x[..., :POLAR], x[..., x.shape[-1] - POLAR :]], -1)


def plain_body(cotangent, zonal_coef, merid_coef, vertical_wind, cutoff):
    levels, lon_dev, lat = cotangent.shape[1:]
    peers = lax.axis_size("lon")
    count = lax.axis_size("lev")
    seat = lax.axis_index("lev").astype(jnp.int32)[None]
    cot, vw = to_rows(cotangent), to_rows(vertical_wind)
    polar_cot = jnp.swapaxes(polar_cut(cotangent), 2, 3)
    polar_vw = jnp.swapaxes(polar_cut(vertical_wind), 1, 2)
    polar_got = ask_levels(polar_cot, polar_vw)
    ends_cot, ends_vw = cotangent[:, :, :: lon_dev - 1], vertical_wind[:, :: lon_dev - 1]
    ends_got = ask_levels(ends_cot, ends_vw)

    sends = edges_of(seat, cot, vw, levels, count == 2)
    polar_got, ends_got, sends = lax.optimization_barrier((polar_got, ends_got, sends))
    if count == 2:
        edges = [lax.ppermute(sends[0], "lev", [(0, 1), (1, 0)])]
    else:
        edges = [
            lax.ppermute(sends[0], "lev", [(i + 1, i) for i in range(count - 1)]),
            lax.ppermute(sends[1], "lev", [(i, i + 1) for i in range(count - 1)]),
            later_sum(sends[2]),
        ]
    polar = adjoint_part(polar_cot, polar_vw, *polar_got)
    ends_adj = adjoint_part(ends_cot, ends_vw, *ends_got)

    rows = 2 * POLAR // peers
    grouped = polar.reshape(5 * levels, peers, rows, lon_dev)
    grouped = jnp.swapaxes(grouped, 0, 1).reshape(peers, 5 * levels * rows, lon_dev)

    pack = jnp.concatenate([ends_adj.reshape(5 * levels, 2, lat), zonal_coef[:, :: lon_dev - 1]], 0)
    up = [(i, (i + 1) % peers) for i in range(peers)]
    down = [(j, i) for i, j in up]
    beyond = jnp.stack([lax.ppermute(pack[:, 1], "lon", up), lax.ppermute(pack[:, 0], "lon", down)], 1)
    halo_adj = beyond[: 5 * levels].reshape(5, levels, 2, lat)
    halo_zc = beyond[5 * levels :]

    smoothed = polar_filter(grouped, cutoff, peers)
    smoothed = smoothed.reshape(2, peers // 2, 5, levels, rows, lon_dev + 2)
    smoothed = smoothed.transpose(2, 5, 0, 3, 1, 4).reshape(5, lon_dev + 2, 2, levels, POLAR)
    north, south = smoothed[:, :, 0], smoothed[:, :, 1]
    gap = ((0, 0), (0, 0), (0, 0))
    smooth = jnp.concatenate(
        [jnp.pad(north, (*gap, (0, 128 - POLAR))), jnp.pad(south, (*gap, (128 - POLAR, 0)))], 2
    )[:, 1 : lon_dev + 1]
    outer = [jnp.swapaxes(x[:, :: lon_dev + 1], 1, 2) for x in (north, south)]
    halo_f = jnp.concatenate([outer[0], halo_adj[..., POLAR : lat - POLAR], outer[1]], 3)
    halo = jnp.stack(coupled(halo_zc, [halo_f[f] for f in range(5)], 0))
    out = stencil(
        seat, cot, vw, to_rows(zonal_coef), to_rows(merid_coef), smooth, to_rows(halo), edges, levels
    )
    return from_rows(out, levels)


def lane_of(shape):
    return lax.broadcasted_iota(jnp.int32, shape, len(shape) - 1)


def pair_up(a, b, lane):
    inner = jnp.where(lane < 64, pltpu.roll(b, POLAR, 1), pltpu.roll(b, 128 - POLAR, 1))
    return jnp.where((lane >= POLAR) & (lane < 128 - POLAR), inner, a)


def second_of(pair, lane):
    return jnp.where(lane < 64, pltpu.roll(pair, 128 - POLAR, 1), pltpu.roll(pair, POLAR, 1))


def polar_level(levels, north, south, k, lane):
    lon, rows, _ = north.shape
    near = north.reshape(lon * rows, 128)[pl.ds(k, lon, stride=rows), :]
    far = south.reshape(lon * rows, 128)[pl.ds(levels + k, lon, stride=rows), :]
    return jnp.where(lane < 64, near, far)


def edge_block(levels, front, cot, vw, out):
    fields, chunk, rows, _ = cot.shape
    tiles = rows // levels
    flat_c = cot.reshape(fields * chunk * rows, 128)
    flat_v = vw.reshape(chunk * rows, 128)
    flat_t = cot.at[2].reshape(chunk * rows, 128)

    def product(k, sign):
        c = flat_c[pl.ds(k, fields * chunk * tiles, stride=levels), :]
        v = flat_v[pl.ds(k, chunk * tiles, stride=levels), :]
        c = c.reshape(fields, chunk, tiles, 128)
        out[:fields] = sign * (v.reshape(1, chunk, tiles, 128) * c)

    total = flat_t[pl.ds(0, chunk * tiles, stride=levels), :]
    for k in range(1, levels):
        total = total + flat_t[pl.ds(k, chunk * tiles, stride=levels), :]
    out[fields] = jnp.where(front, 0.0, total.reshape(chunk, tiles, 128))
    pl.when(front)(lambda: product(levels - 1, -1.0))
    pl.when(jnp.logical_not(front))(lambda: product(0, 1.0))


def open_kernel(levels, seat, cot, vw, sent, ends, local, cn, cs, vn, vs, ec, ev, below, made, sems, out_sems):
    _, lon, rows, _ = cot.shape
    wide = 2 * levels
    lane = lane_of((lon, 128))
    front = seat[0] == 0
    near, far = pl.ds(0, wide), pl.ds(rows - wide, wide)
    jobs = [(vw.at[:, near], vn), (vw.at[:, far], vs)]
    order = (2, 0, 1, 3, 4)
    for f in order:
        jobs += [(cot.at[f, :, near], cn.at[f]), (cot.at[f, :, far], cs.at[f])]
    for n, e in enumerate((0, lon - 1)):
        jobs += [(cot.at[:, e], ec.at[:, n]), (vw.at[e], ev.at[n])]
    jobs = [pltpu.make_async_copy(a, b, sems.at[n]) for n, (a, b) in enumerate(jobs)]
    for job in jobs:
        job.start()
    jobs[0].wait()
    jobs[1].wait()
    v = [polar_level(levels, vn, vs, k, lane) for k in range(levels)]
    half, away = levels // 2, []
    for n, f in enumerate(order):
        jobs[2 + 2 * n].wait()
        jobs[3 + 2 * n].wait()
        c = [polar_level(levels, cn.at[f], cs.at[f], k, lane) for k in range(levels)]
        w = [a * b for a, b in zip(v, c)]
        edge = jnp.where(front, -w[levels - 1], w[0])
        if f == 2:
            run = c[levels - 1]
            below[levels - 1] = run
            for k in range(levels - 2, -1, -1):
                run = run + c[k]
                below[k] = run
            total = jnp.where(front, 0.0, run)
            sent[2] = total
        if f == 4:
            sent[2] = pair_up(edge, sent[2], lane)
        elif f == 2:
            sent[1] = edge
        elif f % 2:
            sent[f // 2] = pair_up(sent[f // 2], edge, lane)
        else:
            sent[f // 2] = edge
        for k in range(0, levels, 2):
            pieces = []
            for at in (k, k + 1):
                a = c[at]
                if at < levels - 1:
                    a = a + w[at + 1]
                if at > 0:
                    a = a - w[at - 1]
                if f == 3:
                    a = a - COUPLE_B * below[at]
                pieces.append(a)
            made[f * half + k // 2] = pair_up(pieces[0], pieces[1], lane)
        mine = pl.ds(f * half, half)
        away.append(pltpu.make_async_copy(made.at[mine], local.at[mine], out_sems.at[f]))
        away[-1].start()
    for job in jobs[12:]:
        job.wait()
    edge_block(levels, front, ec, ev, ends)
    for job in away:
        job.wait()


def opening(seat, cot, vw, levels):
    _, lon, rows, _ = cot.shape
    tiles, wide = rows // levels, 2 * levels
    f32 = jnp.float32
    place = pl.BlockSpec(memory_space=pltpu.HBM)
    vmem = pl.BlockSpec(memory_space=pltpu.VMEM)
    return pl.pallas_call(
        functools.partial(open_kernel, levels),
        out_shape=[
            jax.ShapeDtypeStruct((3, lon, 128), f32),
            jax.ShapeDtypeStruct((6, 2, tiles, 128), f32),
            jax.ShapeDtypeStruct((5 * levels // 2, lon, 128), f32),
        ],
        in_specs=[pl.BlockSpec(memory_space=pltpu.SMEM), place, place],
        out_specs=[vmem, vmem, place],
        scratch_shapes=[
            pltpu.VMEM((5, lon, wide, 128), f32), pltpu.VMEM((5, lon, wide, 128), f32),
            pltpu.VMEM((lon, wide, 128), f32), pltpu.VMEM((lon, wide, 128), f32),
            pltpu.VMEM((5, 2, rows, 128), f32), pltpu.VMEM((2, rows, 128), f32),
            pltpu.VMEM((levels, lon, 128), f32), pltpu.VMEM((5 * levels // 2, lon, 128), f32),
            pltpu.SemaphoreType.DMA((16,)), pltpu.SemaphoreType.DMA((5,)),
        ],
        compiler_params=pltpu.CompilerParams(vmem_limit_bytes=ROOM),
        cost_estimate=pl.CostEstimate(flops=9_000_000, bytes_accessed=10_000_000, transcendentals=0),
        name="opening",
    )(seat, cot, vw)


def edge_run_kernel(levels, start, chunk, count, seat, cot, vw, out, cbuf, vbuf, sems):
    def jobs(n):
        at = pl.ds(start + n * chunk, chunk)
        return (
            pltpu.make_async_copy(cot.at[:, at], cbuf.at[n], sems.at[n, 0]),
            pltpu.make_async_copy(vw.at[at], vbuf.at[n], sems.at[n, 1]),
        )

    for n in range(count):
        for job in jobs(n):
            job.start()
    for n in range(count):
        for job in jobs(n):
            job.wait()
        edge_block(
            levels, seat[0] == 0, cbuf.at[n], vbuf.at[n], out.at[:, pl.ds(n * chunk, chunk)]
        )


def edge_run(seat, cot, vw, levels, start, chunk, count):
    fields, lon, rows, _ = cot.shape
    tiles = rows // levels
    place = pl.BlockSpec(memory_space=pl.ANY)
    size = count * chunk
    return pl.pallas_call(
        functools.partial(edge_run_kernel, levels, start, chunk, count),
        out_shape=jax.ShapeDtypeStruct((fields + 1, size, tiles, 128), jnp.float32),
        in_specs=[pl.BlockSpec(memory_space=pltpu.SMEM), place, place],
        out_specs=pl.BlockSpec(memory_space=pltpu.VMEM),
        scratch_shapes=[
            pltpu.VMEM((count, fields, chunk, rows, 128), jnp.float32),
            pltpu.VMEM((count, chunk, rows, 128), jnp.float32),
            pltpu.SemaphoreType.DMA((count, 2)),
        ],
        compiler_params=pltpu.CompilerParams(vmem_limit_bytes=SOME),
        cost_estimate=pl.CostEstimate(
            flops=50_000 * size, bytes_accessed=120_000 * size, transcendentals=0
        ),
        name="edge_run",
    )(seat, cot, vw)


def slots_of(k, nq):
    north, south = range(nq // 2), range(nq // 2, nq)
    return (
        [(k, q) for q in north] + [(k + 1, q) for q in north]
        + [(k + 1, q) for q in south] + [(k, q) for q in south]
    )


def polar_kernel(
    peers, levels, late, chunk,
    cot, vw, zc, fwd, inv, ct, st, local, got, ends, mask_ref,
    smooth, flux_west, flux_east, *rest,
):
    late_out, rest = rest[: len(late)], rest[len(late) :]
    (fwd_ref, inv_ref, ct_ref, st_ref, mine_ref, x_ref, held, made, back, z, zt, ec, ev, ez, es, spread, below_ref, cbuf, vbuf, ebuf,
     own_sem, wave_sem, send_a, recv_a, send_b, recv_b, col_sem, late_in, late_sem) = rest
    me = lax.axis_index("lon")
    front = lax.axis_index("lev") == 0
    _, lon, rows, _ = cot.shape
    wide = 2 * levels
    nq = peers // levels
    span = 2 * POLAR // nq
    cols = 5 * span
    half = cols // 2
    kpad = ct_ref.shape[2]
    lane = lane_of((lon, 128))
    barrier = pltpu.get_barrier_semaphore()

    def ahead(o):
        return lax.rem(me + o, peers)

    def behind(o):
        return lax.rem(me + peers - o, peers)

    def greet(o, _):
        pl.semaphore_signal(barrier, inc=1, device_id={"lon": ahead(o)}, device_id_type=MESH)
        return 0

    own_part = pltpu.make_async_copy(local, mine_ref, wave_sem.at[4])
    own_part.start()
    lax.fori_loop(1, peers, greet, 0)

    column_jobs = []
    for n, e in enumerate((0, lon - 1)):
        for m, (a, b) in enumerate(
            ((cot.at[:, e], ec.at[:, n]), (vw.at[e], ev.at[n]), (zc.at[e], ez.at[n]))
        ):
            column_jobs.append(pltpu.make_async_copy(a, b, col_sem.at[3 * n + m]))
    late_jobs, late_outs, n = [], [], 0
    for out, (start, size) in zip(late_out, late):
        for at in range(0, size, chunk):
            where = pl.ds(start + at, chunk)
            late_jobs.append((
                pltpu.make_async_copy(cot.at[:, where], cbuf.at[n], late_in.at[n, 0]),
                pltpu.make_async_copy(vw.at[where], vbuf.at[n], late_in.at[n, 1]),
            ))
            late_outs.append(
                pltpu.make_async_copy(ebuf.at[n], out.at[:, pl.ds(at, chunk)], late_sem.at[n])
            )
            n += 1
    wave_jobs = [
        pltpu.make_async_copy(fwd, fwd_ref, wave_sem.at[0]),
        pltpu.make_async_copy(inv, inv_ref, wave_sem.at[1]),
        pltpu.make_async_copy(ct, ct_ref, wave_sem.at[2]),
        pltpu.make_async_copy(st, st_ref, wave_sem.at[3]),
    ]
    for job in column_jobs + wave_jobs:
        job.start()
    for jobs in late_jobs:
        for job in jobs:
            job.start()

    z[...] = jnp.zeros_like(z)
    own_part.wait()
    for f in range(5):
        pair = got[f // 2]
        edge = second_of(pair, lane) if f % 2 else pair
        tail = second_of(got[2], lane) if f == 3 else None
        for k in range(0, levels, 2):
            add = []
            for at in (k, k + 1):
                a = jnp.zeros((lon, 128), jnp.float32)
                if at == levels - 1:
                    a = a + jnp.where(front, edge, 0.0)
                if at == 0:
                    a = a + jnp.where(front, 0.0, edge)
                if f == 3:
                    a = a - COUPLE_B * tail
                add.append(a)
            z[:lon] = mine_ref[f * levels // 2 + k // 2] + pair_up(add[0], add[1], lane)
            zt[...] = z[...].T
            for n, (at, q) in enumerate(slots_of(k, nq)):
                d = at * nq + q
                x_ref[d, f * span : (f + 1) * span] = zt[n * span : (n + 1) * span, :128]
                for h in range(0, span, 8):
                    to = f * span + h
                    end = zt[n * span + h : n * span + h + 8, 128:]
                    if to < half:
                        x_ref[d, cols + to : cols + to + 8] = end
                    else:
                        to += cols - half
                        x_ref[d, to : to + 8] += pltpu.roll(end, 64, 1)

    def out_copy(d):
        return pltpu.make_async_remote_copy(
            src_ref=x_ref.at[d], dst_ref=held.at[me], send_sem=send_a.at[d],
            recv_sem=recv_a.at[me], device_id={"lon": d}, device_id_type=MESH,
        )

    def in_copy(s):
        return pltpu.make_async_remote_copy(
            src_ref=x_ref.at[s], dst_ref=held.at[s], send_sem=send_a.at[s],
            recv_sem=recv_a.at[s], device_id={"lon": s}, device_id_type=MESH,
        )

    def back_copy(d):
        return pltpu.make_async_remote_copy(
            src_ref=made.at[d], dst_ref=back.at[me], send_sem=send_b.at[d],
            recv_sem=recv_b.at[me], device_id={"lon": d}, device_id_type=MESH,
        )

    def home_copy(s):
        return pltpu.make_async_remote_copy(
            src_ref=made.at[s], dst_ref=back.at[s], send_sem=send_b.at[s],
            recv_sem=recv_b.at[s], device_id={"lon": s}, device_id_type=MESH,
        )

    pl.semaphore_wait(barrier, peers - 1)
    lax.fori_loop(1, peers, lambda o, c: (out_copy(ahead(o)).start(), c)[1], 0)
    own = pltpu.make_async_copy(x_ref.at[me], held.at[me], own_sem)
    own.start()

    for n, jobs in enumerate(late_jobs):
        for job in jobs:
            job.wait()
        edge_block(levels, front, cbuf.at[n], vbuf.at[n], ebuf.at[n])
        late_outs[n].start()

    for job in wave_jobs:
        job.wait()
    own.wait()
    zero = jnp.zeros((cols, kpad), jnp.float32)
    dot = functools.partial(jnp.dot, precision=HIGHEST, preferred_element_type=jnp.float32)

    def gather(s, carry):
        a, b = carry
        ends = held[s, cols:]
        ends = jnp.concatenate([ends[:, :64], ends[:, 64:]], 0)
        both = dot(held[s, :cols], fwd_ref[:128]) + dot(ends, fwd_ref[128:])
        c, v = both[:, :kpad], both[:, kpad:]
        cos, sin = ct_ref[s], st_ref[s]
        return a + (cos * c - sin * v), b + (sin * c + cos * v)

    def arrive(o, carry):
        s = behind(o)
        in_copy(s).wait_recv()
        return gather(s, carry)

    a, b = lax.fori_loop(1, peers, arrive, gather(me, (zero, zero)))
    mask = jnp.concatenate([mask_ref[...]] * 5, 0)
    a = a * mask
    b = b * mask

    def turn(d):
        cos, sin = ct_ref[d], st_ref[d]
        p, q = a * cos + b * sin, b * cos - a * sin
        y = dot(p, inv_ref[0]) + dot(q, inv_ref[1])
        made[d, :cols] = y[:, :128]
        made[d, cols:] = jnp.concatenate([y[:half, 128:], y[half:, 128:]], 1)

    far = peers - peers // 2

    def turn_of(n):
        return ahead(jnp.where(n < far, n + peers // 2, n - far + 1))

    def depart(n, _):
        turn(turn_of(n))
        pl.when(n > 0)(lambda: back_copy(turn_of(n - 1)).start())
        return 0

    lax.fori_loop(0, peers - 1, depart, 0)
    turn(me)
    back_copy(turn_of(peers - 2)).start()
    mine = pltpu.make_async_copy(made.at[me], back.at[me], own_sem)
    mine.start()
    for job in late_outs:
        job.wait()
    for job in column_jobs:
        job.wait()
    mine.wait()
    lax.fori_loop(1, peers, lambda o, c: (home_copy(behind(o)).wait_recv(), c)[1], 0)

    for f in range(5):
        flat = smooth.at[f].reshape(lon * wide, 128)
        for k in range(0, levels, 2):
            for n, (at, q) in enumerate(slots_of(k, nq)):
                d = at * nq + q
                zt[n * span : (n + 1) * span, :128] = back[d, f * span : (f + 1) * span]
                for h in range(0, span, 8):
                    to = f * span + h
                    if to < half:
                        end = back[d, cols + to : cols + to + 8]
                    else:
                        to += cols - half
                        end = pltpu.roll(back[d, to : to + 8], 64, 1)
                    zt[n * span + h : n * span + h + 8, 128:] = end
            z[...] = zt[...].T
            first = z[:lon]
            flat[pl.ds(k, lon, stride=wide), :] = first
            flat[pl.ds(levels + k, lon, stride=wide), :] = first
            flat[pl.ds(k + 1, lon, stride=wide), :] = pltpu.roll(first, 128 - POLAR, 1)
            flat[pl.ds(levels + k + 1, lon, stride=wide), :] = pltpu.roll(first, POLAR, 1)

    for f in range(5):
        for n, e in enumerate((0, lon - 1)):
            es[f, n] = smooth[f, e]
    spread[...] = jnp.zeros_like(spread)
    column = column_maker(levels, front, ec, ev, es, ends, spread, below_ref)
    for n in range(2):
        field = column(n)
        fields = [field(f)[1] for f in range(5)]
        for v in range(rows // 8):
            zonal = coupled(ez[n, 8 * v : 8 * v + 8], [fields[f][v] for f in range(5)], 0)
            for f in range(5):
                (flux_west, flux_east)[n][f, 8 * v : 8 * v + 8] = zonal[f]
    lax.fori_loop(1, peers, lambda o, c: (out_copy(ahead(o)).wait_send(), c)[1], 0)
    lax.fori_loop(1, peers, lambda o, c: (back_copy(ahead(o)).wait_send(), c)[1], 0)


def hold(a):
    return pltpu.with_memory_space_constraint(jnp.asarray(a), pltpu.HBM)


def polar_path(cot, vw, zc, local, got, ends, cutoff, levels, peers, late, chunk):
    _, lon, rows, _ = cot.shape
    tiles, wide = rows // levels, 2 * levels
    nq = peers // levels
    nlon = peers * lon
    span = cutoff.shape[0] // nq
    kpad = (KMAX + 1 + 127) // 128 * 128
    wave = np.arange(kpad)
    fwd = np.concatenate(angles(np.arange(lon)[:, None], wave[None, :], nlon), axis=1)
    inv = np.stack(angles(wave[:, None], np.arange(lon)[None, :], nlon))
    short = 192 - lon
    fwd = np.pad(fwd, ((0, short), (0, 0)))
    inv = np.pad(inv, ((0, 0), (0, 0), (0, short)))
    ct, st = angles(np.arange(peers)[:, None, None] * lon, wave[None, None, :], nlon)
    mine = lax.dynamic_slice_in_dim(cutoff, lax.axis_index("lon") % nq * span, span)
    weight = np.where(wave == 0, 1.0 / nlon, 2.0 / nlon).astype(np.float32)
    mask = jnp.where(jnp.asarray(wave, jnp.int32)[None, :] <= mine[:, None], weight[None, :], 0.0)
    vmem = pl.BlockSpec(memory_space=pltpu.VMEM)
    place = pl.BlockSpec(memory_space=pltpu.HBM)
    dma = pltpu.SemaphoreType.DMA
    f32 = jnp.float32
    shape = (peers, 5 * span + 5 * span // 2, 128)
    blocks = sum(size for _, size in late) // chunk
    return pl.pallas_call(
        functools.partial(polar_kernel, peers, levels, late, chunk),
        out_shape=[
            jax.ShapeDtypeStruct((5, lon, wide, 128), f32),
            jax.ShapeDtypeStruct((5, rows, 128), f32),
            jax.ShapeDtypeStruct((5, rows, 128), f32),
        ] + [jax.ShapeDtypeStruct((6, size, tiles, 128), f32) for _, size in late],
        in_specs=[place] * 8 + [vmem] * 3,
        out_specs=[vmem] * 3 + [place] * len(late),
        scratch_shapes=[
            pltpu.VMEM(fwd.shape, f32), pltpu.VMEM(inv.shape, f32),
            pltpu.VMEM(ct.shape, f32), pltpu.VMEM(st.shape, f32), pltpu.VMEM(local.shape, f32),
            pltpu.VMEM(shape, f32), pltpu.VMEM(shape, f32), pltpu.VMEM(shape, f32),
            pltpu.VMEM(shape, f32), pltpu.VMEM((256, 128), f32), pltpu.VMEM((128, 256), f32),
            pltpu.VMEM((5, 2, rows, 128), f32), pltpu.VMEM((2, rows, 128), f32),
            pltpu.VMEM((2, rows, 128), f32), pltpu.VMEM((5, 2, wide, 128), f32),
            pltpu.VMEM((1, 5, rows, 128), f32),
            pltpu.VMEM((1, rows, 128), f32),
            pltpu.VMEM((blocks, 5, chunk, rows, 128), f32),
            pltpu.VMEM((blocks, chunk, rows, 128), f32),
            pltpu.VMEM((blocks, 6, chunk, tiles, 128), f32),
            dma(()), dma((5,)), dma((peers,)), dma((peers,)), dma((peers,)), dma((peers,)),
            dma((6,)), dma((blocks, 2)), dma((blocks,)),
        ],
        compiler_params=pltpu.CompilerParams(
            collective_id=1, has_side_effects=True, vmem_limit_bytes=30 << 20
        ),
        cost_estimate=pl.CostEstimate(flops=8_000_000_000, bytes_accessed=60_000_000, transcendentals=0),
        name="polar_path",
    )(cot, vw, zc, *(hold(a) for a in (fwd, inv, ct, st)), local, got, ends, mask)


def column_maker(levels, front, cot, vw, smooth, edges, spread, below_ref):
    _, _, rows, _ = cot.shape
    tiles = rows // levels
    parts = rows // 8
    edge_at = jnp.where(front, levels - 1, 0)
    row = lax.broadcasted_iota(jnp.int32, (8, 128), 0)
    lane = lane_of((8, 128))
    k = lax.rem(row, levels)
    north = (row < levels) & (lane < POLAR)
    south = (row >= levels) & (lane >= 128 - POLAR)
    at = [pl.ds(8 * v, 8) for v in range(parts)]

    def column(l, side=0):
        for f in range(5):
            spread[side, f, pl.ds(edge_at, tiles, stride=levels), :] = edges[f, l]
        for n in range(levels):
            below_ref[side, pl.ds(n, tiles, stride=levels), :] = edges[5, l]
        wind = [vw[l, a] for a in at]
        under = [jnp.where(k > 0, a, 0.0) for a in wind]
        over = [jnp.where(k < levels - 1, a, 0.0) for a in wind]

        def field(f):
            whole, inner = [], []
            for v in range(parts):
                c = cot[f, l, at[v]]
                a = c + (pltpu.roll(under[v] * c, 7, 0) - pltpu.roll(over[v] * c, 1, 0))
                a = a + spread[side, f, at[v]]
                if f == 3:
                    run, r = cot[2, l, at[v]], 1
                    while r < levels:
                        run = run + jnp.where(k < levels - r, pltpu.roll(run, 8 - r, 0), 0.0)
                        r *= 2
                    a = a - COUPLE_B * (run + below_ref[side, at[v]])
                whole.append(a)
                if v == 0:
                    a = jnp.where(north, smooth[f, l], a)
                if v == parts - 1:
                    a = jnp.where(south, smooth[f, l], a)
                inner.append(a)
            return whole, inner

        return field

    return column


def lat_change(levels, m):
    row = lax.broadcasted_iota(jnp.int32, (8, 128), 0)
    lane = lane_of((8, 128))
    top = row < levels
    turned = [pltpu.roll(a, levels, 0) for a in m]
    zero = jnp.zeros((8, 128), jnp.float32)
    tile = [jnp.where(top, a, b) for a, b in zip([zero] + turned, turned + [zero])]
    out = []
    for v, a in enumerate(m):
        near = pltpu.roll(jnp.where(lane == 127, tile[v], a), 1, 1)
        far = pltpu.roll(jnp.where(lane == 0, tile[v + 1], a), 127, 1)
        out.append(far - near)
    return out


def strip_kernel(levels, start, steps, first, last, seat, cot, vw, zc, mc, smooth, edges, *rest):
    rest = list(rest)
    if not first:
        wait_in, prior_in, _ = rest.pop(0), rest.pop(0), rest.pop(0)
    if last:
        left, right, column_in = rest.pop(0), rest.pop(0), rest.pop(0)
    if first:
        column_out = rest.pop(1)
    out, wait, prior, ready, spread, below_ref, sems = rest[:7]
    _, chunk, rows, _ = cot.shape
    parts = rows // 8
    g = pl.program_id(0)
    slot = lax.rem(g, 2)

    def first_copy():
        return pltpu.make_async_copy(
            ready.at[0, :, pl.ds(2, chunk - 2)], out.at[:, pl.ds(1, chunk - 2)], sems.at[0]
        )

    def copy(at):
        s = lax.rem(at, 2)
        return pltpu.make_async_copy(
            ready.at[s], out.at[:, pl.ds(start + at * chunk - 1, chunk)], sems.at[s]
        )

    def act(at, what):
        if first:
            pl.when(at == 0)(lambda: getattr(first_copy(), what)())
            pl.when(at > 0)(lambda: getattr(copy(at), what)())
        else:
            getattr(copy(at), what)()

    @pl.when(g == 0)
    def _():
        spread[...] = jnp.zeros_like(spread)
        if first:
            prior[...] = jnp.zeros_like(prior)
            wait[...] = jnp.zeros_like(wait)
        else:
            prior[...] = prior_in[...]
            wait[...] = wait_in[...]

    pl.when(g >= 2)(lambda: act(g - 2, "wait"))
    column = column_maker(levels, seat[0] == 0, cot, vw, smooth, edges, spread, below_ref)
    at = [pl.ds(8 * v, 8) for v in range(parts)]

    def flux_of(l, side):
        field = column(l, side)
        zcs = [zc[l, a] for a in at]
        mcs = [mc[l, a] for a in at]
        whole3, f3 = field(3)
        half3 = [COUPLE_H * a for a in f3]
        parted, zonal = [None] * 5, [None] * 5

        def close(f, whole, inner, add_zonal=None, add_merid=None):
            z = [a * b for a, b in zip(zcs, inner)]
            m = [a * b for a, b in zip(mcs, inner)]
            if add_zonal is not None:
                z = [a + b for a, b in zip(z, add_zonal)]
            if add_merid is not None:
                m = [a + b for a, b in zip(m, add_merid)]
            zonal[f] = z
            parted[f] = [a + b for a, b in zip(whole, lat_change(levels, m))]

        whole, f0 = field(0)
        close(0, whole, f0, add_zonal=half3)
        whole, f1 = field(1)
        close(1, whole, f1, add_merid=half3)
        close(3, whole3, f3, [COUPLE_G * a for a in f0], [COUPLE_G * a for a in f1])
        for f in (2, 4):
            close(f, *field(f))
        return parted, zonal

    def one(l):
        parted, zonal = flux_of(l, 0)
        for f in range(5):
            for v in range(parts):
                ready[slot, f, l, at[v]] = wait[f, at[v]] + zonal[f][v]
                wait[f, at[v]] = parted[f][v] - prior[f, at[v]]
                prior[f, at[v]] = zonal[f][v]

    def two(n, _):
        l = 2 * n
        parted, zonal = flux_of(l, 0)
        for f in range(5):
            for v in range(parts):
                ready[slot, f, l, at[v]] = wait[f, at[v]] + zonal[f][v]
                parted[f][v] = parted[f][v] - prior[f, at[v]]
        later, after = flux_of(l + 1, 1)
        for f in range(5):
            for v in range(parts):
                ready[slot, f, l + 1, at[v]] = parted[f][v] + after[f][v]
                wait[f, at[v]] = later[f][v] - zonal[f][v]
                prior[f, at[v]] = after[f][v]
        return 0

    lax.fori_loop(0, chunk // 2, two, 0)
    if chunk % 2:
        one(chunk - 1)
    act(g, "start")
    if first:

        @pl.when(g == 0)
        def _():
            for f in range(5):
                column_out[f] = ready[0, f, 1]

    @pl.when(g == steps - 1)
    def _():
        if last:
            final, last_sem = rest[7:]
            for f in range(5):
                final[0, f, 0] = column_in[f] - left[f]
                final[1, f, 0] = wait[f] + right[f]
            ends = [
                pltpu.make_async_copy(final.at[n], out.at[:, pl.ds(e, 1)], last_sem.at[n])
                for n, e in enumerate((0, start + steps * chunk - 1))
            ]
            for end in ends:
                end.start()
        if steps > 1:
            act(g - 1, "wait")
        act(g, "wait")
        if last:
            for end in ends:
                end.wait()


def strip(seat, cot, vw, zc, mc, smooth, edges, state, borders, levels, start, steps, chunk):
    _, lon, rows, _ = cot.shape
    tiles = rows // levels
    at = start // chunk
    first, last = not state, borders is not None
    field = lambda n: pl.BlockSpec((5, chunk, n, 128), lambda g, s: (0, at + g, 0, 0))
    plain = pl.BlockSpec((chunk, rows, 128), lambda g, s: (at + g, 0, 0))
    whole = pl.BlockSpec((5, rows, 128), lambda g, s: (0, 0, 0))
    place = pl.BlockSpec(memory_space=pl.ANY)
    in_specs = [field(rows), plain, plain, plain, field(2 * levels),
                pl.BlockSpec((6, chunk, tiles, 128), lambda g, s: (0, g, 0, 0))]
    in_specs += [] if first else [whole, whole, place]
    args = [seat, cot, vw, zc, mc, smooth, edges, *state]
    aliases = {} if first else {len(args) - 1: 0}
    if last:
        in_specs += [whole] * 3
        args += borders
    one = jax.ShapeDtypeStruct((5, rows, 128), jnp.float32)
    held = [pltpu.VMEM((5, rows, 128), jnp.float32)] * 2
    scratch = [
        pltpu.VMEM((2, 5, chunk, rows, 128), jnp.float32),
        pltpu.VMEM((2, 5, rows, 128), jnp.float32),
        pltpu.VMEM((2, rows, 128), jnp.float32),
        pltpu.SemaphoreType.DMA((2,)),
    ]
    if last:
        scratch = held + scratch + [
            pltpu.VMEM((2, 5, 1, rows, 128), jnp.float32), pltpu.SemaphoreType.DMA((2,)),
        ]
    extra = 0 if last else 3 if first else 2
    got = pl.pallas_call(
        functools.partial(strip_kernel, levels, start, steps, first, last),
        out_shape=[jax.ShapeDtypeStruct(cot.shape, jnp.float32)] + [one] * extra,
        grid_spec=pltpu.PrefetchScalarGridSpec(
            num_scalar_prefetch=1,
            grid=(steps,),
            in_specs=in_specs,
            out_specs=[place] + [whole] * extra,
            scratch_shapes=scratch,
        ),
        input_output_aliases=aliases,
        compiler_params=pltpu.CompilerParams(vmem_limit_bytes=SOME),
        cost_estimate=pl.CostEstimate(
            flops=30 * 5 * steps * chunk * rows * 128,
            bytes_accessed=4 * 14 * steps * chunk * rows * 128,
            transcendentals=0,
        ),
        name="strip",
    )(*args)
    return got[0] if last else [*got[-2:], got[0], *got[1:-2]]


def fast_body(cotangent, zonal_coef, merid_coef, vertical_wind, cutoff):
    levels, lon_dev, lat = cotangent.shape[1:]
    peers = lax.axis_size("lon")
    seat = lax.axis_index("lev").astype(jnp.int32)[None]
    cot, vw = to_rows(cotangent), to_rows(vertical_wind)
    zc, mc = to_rows(zonal_coef), to_rows(merid_coef)
    cot, vw, zc, mc = (hold(a) for a in (cot, vw, zc, mc))
    trade = lambda a: lax.ppermute(a, "lev", [(0, 1), (1, 0)])
    chunk = max(d for d in range(2, 13) if lon_dev % d == 0 and d not in (11, 12))
    blocks = lon_dev // chunk
    cuts = sorted({max(1, blocks * n // 18) for n in (6, 12, 16, 17)} | {blocks})
    parts = [(a * chunk, (b - a) * chunk) for a, b in zip([0] + cuts[:-1], cuts)]

    sent, ends, local = opening(seat, cot, vw, levels)
    local = hold(local)
    polar_got, ends_got = trade(sent), trade(ends)
    token, _ = lax.optimization_barrier((seat, sent))
    edges = []
    for start, size in parts[:2]:
        part = edge_run(token, cot, vw, levels, start, chunk, size // chunk)
        edges.append(trade(part))
        token, _ = lax.optimization_barrier((token, part))
    polar_got, ends_got, token = lax.optimization_barrier((polar_got, ends_got, token))
    smooth, west, east, *later = polar_path(
        cot, vw, zc, local, polar_got, ends_got, cutoff, levels, peers, tuple(parts[2:]), chunk
    )
    edges += [trade(part) for part in later]
    state, borders, kept = [], None, None
    up = [(i, (i + 1) % peers) for i in range(peers)]
    for n, (start, size) in enumerate(parts):
        if n == len(parts) - 1:
            borders = [left, right, kept]
        state = strip(
            seat, cot, vw, zc, mc, smooth, edges[n], state, borders, levels, start, size // chunk, chunk
        )
        if n == 0:
            kept = state.pop()
            west, east, state[0] = lax.optimization_barrier((west, east, state[0]))
            left = lax.ppermute(east, "lon", up)
            right = lax.ppermute(west, "lon", [(j, i) for i, j in up])
    return from_rows(state, levels)


def body(cotangent, zonal_coef, merid_coef, vertical_wind, cutoff):
    levels, lon_dev, lat = cotangent.shape[1:]
    peers, count = lax.axis_size("lon"), lax.axis_size("lev")
    span = 2 * POLAR * levels // peers
    fast = (
        count == 2 and levels * 2 == 8 and peers % (2 * levels) == 0 and lat % 256 == 0
        and span % 16 == 0 and 128 < lon_dev <= 192 and cutoff.shape[0] == 2 * POLAR
    )
    return (fast_body if fast else plain_body)(
        cotangent, zonal_coef, merid_coef, vertical_wind, cutoff
    )


def solution(mesh):
    return jax.shard_map(
        body,
        mesh=mesh,
        in_specs=(
            P(None, "lev", "lon", None),
            P("lev", "lon", None),
            P("lev", "lon", None),
            P("lev", "lon", None),
            P(),
        ),
        out_specs=P(None, "lev", "lon", None),
        check_vma=False,
    )
```

```python
import functools
import math

import jax
import jax.numpy as jnp
import numpy as np
from jax import lax
from jax.experimental import pallas as pl
from jax.experimental.pallas import tpu as pltpu
from jax.sharding import PartitionSpec as P


POLAR = 32
KMAX = 360
COUPLE_G = 0.3
COUPLE_H = 0.3
COUPLE_B = 0.2
MESH = pl.DeviceIdType.MESH
HIGHEST = lax.Precision.HIGHEST
ROOM = 61 << 20
SOME = 36 << 20


def angles(left, right, period):
    phase = (left * right) % period * (2.0 * math.pi / period)
    return np.cos(phase).astype(np.float32), np.sin(phase).astype(np.float32)


def filter_kernel(
    peers, packed, x_ref, fwd_ref, inv_ref, ct_ref, st_ref, mask_ref, out_ref, held, made,
    own_sem, send_a, recv_a, send_b, recv_b,
):
    me = lax.axis_index("lon")
    kpad = ct_ref.shape[2]
    barrier = pltpu.get_barrier_semaphore()

    def greet(o, _):
        pl.semaphore_signal(
            barrier, inc=1, device_id={"lon": lax.rem(me + o, peers)}, device_id_type=MESH
        )
        return 0

    lax.fori_loop(1, peers, greet, 0)
    pl.semaphore_wait(barrier, peers - 1)

    def out_copy(o):
        d = lax.rem(me + o, peers)
        return pltpu.make_async_remote_copy(
            src_ref=x_ref.at[d], dst_ref=held.at[me], send_sem=send_a.at[d],
            recv_sem=recv_a.at[me], device_id={"lon": d}, device_id_type=MESH,
        )

    def in_copy(o):
        s = lax.rem(me + o, peers)
        return pltpu.make_async_remote_copy(
            src_ref=x_ref.at[s], dst_ref=held.at[s], send_sem=send_a.at[s],
            recv_sem=recv_a.at[s], device_id={"lon": s}, device_id_type=MESH,
        )

    def back_copy(o):
        d = lax.rem(me + o, peers)
        return pltpu.make_async_remote_copy(
            src_ref=made.at[d], dst_ref=out_ref.at[me], send_sem=send_b.at[d],
            recv_sem=recv_b.at[me], device_id={"lon": d}, device_id_type=MESH,
        )

    def home_copy(o):
        s = lax.rem(me + o, peers)
        return pltpu.make_async_remote_copy(
            src_ref=made.at[s], dst_ref=out_ref.at[s], send_sem=send_b.at[s],
            recv_sem=recv_b.at[s], device_id={"lon": s}, device_id_type=MESH,
        )

    lax.fori_loop(1, peers, lambda o, c: (out_copy(o).start(), c)[1], 0)
    own = pltpu.make_async_copy(x_ref.at[me], held.at[me], own_sem)
    own.start()
    own.wait()
    cols = mask_ref.shape[0]
    half = cols // 2
    zero = jnp.zeros((cols, kpad), jnp.float32)
    dot = functools.partial(jnp.dot, precision=HIGHEST, preferred_element_type=jnp.float32)

    def gather(s, carry):
        a, b = carry
        if packed:
            ends = held[s, cols:]
            ends = jnp.concatenate([ends[:, :64], ends[:, 64:]], 0)
            both = dot(held[s, :cols], fwd_ref[:128]) + dot(ends, fwd_ref[128:])
        else:
            both = dot(held[s], fwd_ref[...])
        c, v = both[:, :kpad], both[:, kpad:]
        ct, st = ct_ref[s], st_ref[s]
        return a + (ct * c - st * v), b + (st * c + ct * v)

    def arrive(o, carry):
        in_copy(o).wait_recv()
        return gather(lax.rem(me + o, peers), carry)

    a, b = lax.fori_loop(1, peers, arrive, gather(me, (zero, zero)))
    a = a * mask_ref[...]
    b = b * mask_ref[...]

    def spread(d):
        ct, st = ct_ref[d], st_ref[d]
        p, q = a * ct + b * st, b * ct - a * st
        if packed:
            y = dot(p, inv_ref[0]) + dot(q, inv_ref[1])
            made[d, :cols] = y[:, :128]
            made[d, cols:] = jnp.concatenate([y[:half, 128:], y[half:, 128:]], 1)
        else:
            made[d] = dot(p, inv_ref[0]) + dot(q, inv_ref[1])

    def depart(o, _):
        spread(lax.rem(me + o, peers))
        pl.when(o > 1)(lambda: back_copy(o - 1).start())
        return 0

    lax.fori_loop(1, peers, depart, 0)
    spread(me)
    back_copy(peers - 1).start()
    mine = pltpu.make_async_copy(made.at[me], out_ref.at[me], own_sem)
    mine.start()
    mine.wait()
    lax.fori_loop(1, peers, lambda o, c: (home_copy(o).wait_recv(), c)[1], 0)
    lax.fori_loop(1, peers, lambda o, c: (out_copy(o).wait_send(), c)[1], 0)
    lax.fori_loop(1, peers, lambda o, c: (back_copy(o).wait_send(), c)[1], 0)


def polar_filter(x, cutoff, peers):
    _, cols, lon_dev = x.shape
    nlon = peers * lon_dev
    rows = cutoff.shape[0] // peers
    kpad = (KMAX + 1 + 127) // 128 * 128
    wave = np.arange(kpad)
    fwd = np.concatenate(angles(np.arange(lon_dev)[:, None], wave[None, :], nlon), axis=1)
    inv = np.stack(angles(wave[:, None], np.arange(-1, lon_dev + 1)[None, :] % nlon, nlon))
    over, wider = lon_dev - 128, lon_dev + 2 - 128
    packed = over > 0 and wider <= 64 and cols % 16 == 0
    half = cols // 2
    if packed:
        fwd = np.pad(fwd, ((0, 64 - over), (0, 0)))
        inv = np.pad(inv, ((0, 0), (0, 0), (0, 64 - wider)))
        ends = jnp.pad(x[..., 128:], ((0, 0), (0, 0), (0, 64 - over)))
        x = jnp.concatenate([x[..., :128], jnp.concatenate([ends[:, :half], ends[:, half:]], 2)], 1)
        shape = (peers, cols + half, 128)
    else:
        shape = (peers, cols, lon_dev + 2)
    ct, st = angles(np.arange(peers)[:, None, None] * lon_dev, wave[None, None, :], nlon)
    mine = lax.dynamic_slice_in_dim(cutoff, lax.axis_index("lon") * rows, rows)
    weight = np.where(wave == 0, 1.0 / nlon, 2.0 / nlon).astype(np.float32)
    mask = jnp.where(jnp.asarray(wave, jnp.int32)[None, :] <= mine[:, None], weight[None, :], 0.0)
    mask = jnp.tile(mask, (cols // rows, 1))
    vmem = pl.BlockSpec(memory_space=pltpu.VMEM)
    dma = pltpu.SemaphoreType.DMA
    y = pl.pallas_call(
        functools.partial(filter_kernel, peers, packed),
        out_shape=jax.ShapeDtypeStruct(shape, jnp.float32),
        in_specs=[vmem] * 6,
        out_specs=vmem,
        scratch_shapes=[
            pltpu.VMEM(x.shape, jnp.float32),
            pltpu.VMEM(shape, jnp.float32),
            dma(()), dma((peers,)), dma((peers,)), dma((peers,)), dma((peers,)),
        ],
        compiler_params=pltpu.CompilerParams(
            collective_id=0, has_side_effects=True, vmem_limit_bytes=24 << 20
        ),
        cost_estimate=pl.CostEstimate(flops=8_000_000_000, bytes_accessed=60_000_000, transcendentals=0),
        name="polar_filter",
    )(x, fwd, inv, ct, st, mask)
    if not packed:
        return y
    ends = jnp.concatenate([y[:, cols:, :wider], y[:, cols:, 64 : 64 + wider]], 1)
    return jnp.concatenate([y[:, :cols], ends], 2)


def to_rows(x):
    *lead, levels, lon, lat = x.shape
    n = len(lead)
    x = x.reshape(*lead, levels, lon, lat // 128, 128)
    x = x.transpose(*range(n), n + 1, n + 2, n, n + 3)
    return x.reshape(*lead, lon, lat // 128 * levels, 128)


def from_rows(x, levels):
    *lead, lon, rows, _ = x.shape
    n = len(lead)
    x = x.reshape(*lead, lon, rows // levels, levels, 128)
    x = x.transpose(*range(n), n + 2, n, n + 1, n + 3)
    return x.reshape(*lead, levels, lon, rows // levels * 128)


def chunk_of(lon):
    return max(d for d in range(1, 21) if lon % d == 0)


def edge_kernel(levels, choose, seat, cot, vw, *outs):
    fields, chunk, rows, _ = cot.shape
    tiles = rows // levels
    flat_c = cot.reshape(fields * chunk * rows, 128)
    flat_v = vw.reshape(chunk * rows, 128)
    sends = outs[: 1 if choose else 2]

    def level(ref, count, k):
        return ref[pl.ds(k, count * tiles, stride=levels), :] if levels > 1 else ref[...]

    def product(k, sign, out):
        c = level(flat_c, fields * chunk, k).reshape(fields, chunk, tiles, 128)
        v = level(flat_v, chunk, k).reshape(1, chunk, tiles, 128)
        out[:fields] = sign * (v * c)

    flat_t = cot.at[2].reshape(chunk * rows, 128)
    total = level(flat_t, chunk, 0)
    for k in range(1, levels):
        total = total + level(flat_t, chunk, k)
    total = total.reshape(chunk, tiles, 128)
    if choose:
        sends[0][fields] = jnp.where(seat[0] == 0, 0.0, total)
        pl.when(seat[0] == 0)(lambda: product(levels - 1, -1.0, sends[0]))
        pl.when(seat[0] != 0)(lambda: product(0, 1.0, sends[0]))
    else:
        product(0, 1.0, sends[0])
        product(levels - 1, -1.0, sends[1])
        outs[2][...] = total


def edges_of(seat, cot, vw, levels, choose):
    fields, lon, rows, _ = cot.shape
    tiles = rows // levels
    chunk = chunk_of(lon)
    n = 1 if choose else 2
    wide = fields + 1 if choose else fields
    return pl.pallas_call(
        functools.partial(edge_kernel, levels, choose),
        out_shape=[jax.ShapeDtypeStruct((wide, lon, tiles, 128), jnp.float32)] * n
        + [jax.ShapeDtypeStruct((lon, tiles, 128), jnp.float32)] * (n - 1),
        grid_spec=pltpu.PrefetchScalarGridSpec(
            num_scalar_prefetch=1,
            grid=(lon // chunk,),
            in_specs=[
                pl.BlockSpec((fields, chunk, rows, 128), lambda g, s: (0, g, 0, 0)),
                pl.BlockSpec((chunk, rows, 128), lambda g, s: (g, 0, 0)),
            ],
            out_specs=[pl.BlockSpec((wide, chunk, tiles, 128), lambda g, s: (0, g, 0, 0))] * n
            + [pl.BlockSpec((chunk, tiles, 128), lambda g, s: (g, 0, 0))] * (n - 1),
        ),
        compiler_params=pltpu.CompilerParams(vmem_limit_bytes=24 << 20),
        cost_estimate=pl.CostEstimate(flops=10_000_000, bytes_accessed=22_000_000, transcendentals=0),
        name="edges",
    )(seat, cot, vw)


def coupled(coef, fields, first):
    flux = [coef * f for f in fields]
    flux[first] = flux[first] + COUPLE_H * fields[3]
    flux[3] = flux[3] + COUPLE_G * fields[first]
    return flux


def stencil_kernel(levels, steps, n_edge, seat, cot, vw, zc, mc, smooth, halo, *rest):
    edges = rest[:n_edge]
    tail = edges[0].at[5] if n_edge == 1 else rest[n_edge]
    rest = rest[1:] if n_edge > 1 else rest
    edge_at = (1 - seat[0]) * (levels - 1)
    out, ready, final, wait, prior, spread, below_ref, sems, last_sem = rest[n_edge:]
    _, chunk, rows, _ = cot.shape
    tiles = rows // levels
    g = pl.program_id(0)
    slot = lax.rem(g, 2)
    lane = lax.broadcasted_iota(jnp.int32, (rows, 128), 1)
    row = lax.broadcasted_iota(jnp.int32, (rows, 128), 0)
    k = lax.rem(row, levels)
    cap_lane = lax.broadcasted_iota(jnp.int32, (2 * levels, 128), 1)
    cap_row = lax.broadcasted_iota(jnp.int32, (2 * levels, 128), 0)
    north = (cap_row < levels) & (cap_lane < POLAR)
    south = (cap_row >= levels) & (cap_lane >= 128 - POLAR)

    def first_copy():
        return pltpu.make_async_copy(
            ready.at[0, :, pl.ds(1, chunk - 1)], out.at[:, pl.ds(0, chunk - 1)], sems.at[0]
        )

    def copy(at):
        s = lax.rem(at, 2)
        return pltpu.make_async_copy(
            ready.at[s], out.at[:, pl.ds(at * chunk - 1, chunk)], sems.at[s]
        )

    @pl.when(g == 0)
    def _():
        spread[...] = jnp.zeros_like(spread)
        for f in range(5):
            prior[f] = halo[f, 0]
            wait[f] = jnp.zeros((rows, 128), jnp.float32)

    pl.when(g == 2)(lambda: first_copy().wait())
    pl.when(g > 2)(lambda: copy(g - 2).wait())

    def put(ref, at, value):
        if levels > 1:
            ref[pl.ds(at, tiles, stride=levels), :] = value
        else:
            ref[...] = value

    def one(l, _):
        for f in range(5):
            if n_edge == 1:
                put(spread.at[0, f], edge_at, edges[0][f, l])
            else:
                put(spread.at[0, f], levels - 1, edges[0][f, l])
                put(spread.at[1, f], 0, edges[1][f, l])
        for at in range(levels):
            put(below_ref, at, tail[l])
        wind = vw[l]
        base, fields = [], []
        for f in range(5):
            c = cot[f, l]
            w = wind * c
            a = c
            if levels > 1:
                up = jnp.where(k < levels - 1, pltpu.roll(w, rows - 1, 0), 0.0)
                a = a + (up - jnp.where(k > 0, pltpu.roll(w, 1, 0), 0.0))
            for n in range(n_edge):
                a = a + spread[n, f]
            if f == 3:
                theta = cot[2, l]
                below = below_ref[...] + theta
                for r in range(1, levels):
                    below = below + jnp.where(k < levels - r, pltpu.roll(theta, rows - r, 0), 0.0)
                a = a - COUPLE_B * below
            base.append(a)
            s = smooth[f, l]
            top = jnp.where(north, s, a[: 2 * levels])
            low = jnp.where(south, s, a[rows - 2 * levels :])
            fields.append(jnp.concatenate([top, a[2 * levels : rows - 2 * levels], low], 0))
        zonal = coupled(zc[l], fields, 0)
        merid = coupled(mc[l], fields, 1)
        for f in range(5):
            ready[slot, f, l] = wait[f] + zonal[f]
            left = pltpu.roll(merid[f], 1, 1)
            over = jnp.where(row < levels, 0.0, pltpu.roll(left, levels, 0))
            left = jnp.where(lane == 0, over, left)
            right = pltpu.roll(merid[f], 127, 1)
            over = jnp.where(row >= rows - levels, 0.0, pltpu.roll(right, rows - levels, 0))
            right = jnp.where(lane == 127, over, right)
            wait[f] = base[f] + (right - left) - prior[f]
            prior[f] = zonal[f]
        return 0

    lax.fori_loop(0, chunk, one, 0)
    pl.when(g == 0)(lambda: first_copy().start())
    pl.when(g > 0)(lambda: copy(g).start())

    @pl.when(g == steps - 1)
    def _():
        for f in range(5):
            final[f, 0] = wait[f] + halo[f, 1]
        end = pltpu.make_async_copy(final, out.at[:, pl.ds(steps * chunk - 1, 1)], last_sem)
        end.start()
        copy(g - 1).wait() if steps > 2 else first_copy().wait()
        copy(g).wait()
        end.wait()


def stencil(seat, cot, vw, zc, mc, smooth, halo, edges, levels):
    _, lon, rows, _ = cot.shape
    tiles = rows // levels
    chunk = chunk_of(lon)
    steps = lon // chunk
    field = lambda n: pl.BlockSpec((5, chunk, n, 128), lambda g, s: (0, g, 0, 0))
    plain = lambda n: pl.BlockSpec((chunk, n, 128), lambda g, s: (g, 0, 0))
    return pl.pallas_call(
        functools.partial(stencil_kernel, levels, steps, min(len(edges), 2)),
        out_shape=jax.ShapeDtypeStruct(cot.shape, jnp.float32),
        grid_spec=pltpu.PrefetchScalarGridSpec(
            num_scalar_prefetch=1,
            grid=(steps,),
            in_specs=[field(rows), plain(rows), plain(rows), plain(rows), field(2 * levels),
                      pl.BlockSpec((5, 2, rows, 128), lambda g, s: (0, 0, 0, 0))]
            + [pl.BlockSpec((6, chunk, tiles, 128), lambda g, s: (0, g, 0, 0))]
            if len(edges) == 1
            else [field(rows), plain(rows), plain(rows), plain(rows), field(2 * levels),
                  pl.BlockSpec((5, 2, rows, 128), lambda g, s: (0, 0, 0, 0)),
                  field(tiles), field(tiles), plain(tiles)],
            out_specs=pl.BlockSpec(memory_space=pl.ANY),
            scratch_shapes=[
                pltpu.VMEM((2, 5, chunk, rows, 128), jnp.float32),
                pltpu.VMEM((5, 1, rows, 128), jnp.float32),
                pltpu.VMEM((5, rows, 128), jnp.float32),
                pltpu.VMEM((5, rows, 128), jnp.float32),
                pltpu.VMEM((min(len(edges), 2), 5, rows, 128), jnp.float32),
                pltpu.VMEM((rows, 128), jnp.float32),
                pltpu.SemaphoreType.DMA((2,)),
                pltpu.SemaphoreType.DMA(()),
            ],
        ),
        compiler_params=pltpu.CompilerParams(vmem_limit_bytes=40 << 20),
        cost_estimate=pl.CostEstimate(
            flops=30 * 5 * lon * rows * 128, bytes_accessed=4 * 14 * lon * rows * 128, transcendentals=0
        ),
        name="stencil",
    )(seat, cot, vw, zc, mc, smooth, halo, *edges)


def swap_levels(first, last, total):
    count = lax.axis_size("lev")
    if count == 2:
        seat = lax.axis_index("lev")
        lead = jnp.concatenate([first, total[None]], 0)
        trail = jnp.concatenate([last, jnp.zeros_like(total)[None]], 0)
        got = lax.ppermute(jnp.where(seat == 0, trail, lead), "lev", [(0, 1), (1, 0)])
        return jnp.where(seat == 0, got[:5], 0.0), jnp.where(seat == 1, got[:5], 0.0), got[5]
    up = lax.ppermute(first, "lev", [(i + 1, i) for i in range(count - 1)])
    down = lax.ppermute(last, "lev", [(i, i + 1) for i in range(count - 1)])
    return up, down, later_sum(total)


def later_sum(local):
    count = lax.axis_size("lev")
    total = jnp.zeros_like(local)
    for r in range(1, count):
        total = total + lax.ppermute(local, "lev", [(i + r, i) for i in range(count - r)])
    return total


def ask_levels(cot, vw):
    return swap_levels(vw[0] * cot[:, 0], vw[-1] * cot[:, -1], cot[2].sum(0))


def adjoint_part(cot, vw, up, down, later):
    weighted = vw[None] * cot
    above = jnp.concatenate([weighted[:, 1:], up[:, None]], 1)
    under = jnp.concatenate([down[:, None], weighted[:, :-1]], 1)
    below = [later + cot[2, -1]]
    for k in range(cot.shape[1] - 2, -1, -1):
        below.insert(0, below[0] + cot[2, k])
    parts = cot + (above - under)
    return jnp.concatenate(
        [parts[:3], parts[3:4] - COUPLE_B * jnp.stack(below)[None], parts[4:]], 0
    )


def polar_cut(x):
    return jnp.concatenate([x[..., :POLAR], x[..., x.shape[-1] - POLAR :]], -1)


def plain_body(cotangent, zonal_coef, merid_coef, vertical_wind, cutoff):
    levels, lon_dev, lat = cotangent.shape[1:]
    peers = lax.axis_size("lon")
    count = lax.axis_size("lev")
    seat = lax.axis_index("lev").astype(jnp.int32)[None]
    cot, vw = to_rows(cotangent), to_rows(vertical_wind)
    polar_cot = jnp.swapaxes(polar_cut(cotangent), 2, 3)
    polar_vw = jnp.swapaxes(polar_cut(vertical_wind), 1, 2)
    polar_got = ask_levels(polar_cot, polar_vw)
    ends_cot, ends_vw = cotangent[:, :, :: lon_dev - 1], vertical_wind[:, :: lon_dev - 1]
    ends_got = ask_levels(ends_cot, ends_vw)

    sends = edges_of(seat, cot, vw, levels, count == 2)
    polar_got, ends_got, sends = lax.optimization_barrier((polar_got, ends_got, sends))
    if count == 2:
        edges = [lax.ppermute(sends[0], "lev", [(0, 1), (1, 0)])]
    else:
        edges = [
            lax.ppermute(sends[0], "lev", [(i + 1, i) for i in range(count - 1)]),
            lax.ppermute(sends[1], "lev", [(i, i + 1) for i in range(count - 1)]),
            later_sum(sends[2]),
        ]
    polar = adjoint_part(polar_cot, polar_vw, *polar_got)
    ends_adj = adjoint_part(ends_cot, ends_vw, *ends_got)

    rows = 2 * POLAR // peers
    grouped = polar.reshape(5 * levels, peers, rows, lon_dev)
    grouped = jnp.swapaxes(grouped, 0, 1).reshape(peers, 5 * levels * rows, lon_dev)

    pack = jnp.concatenate([ends_adj.reshape(5 * levels, 2, lat), zonal_coef[:, :: lon_dev - 1]], 0)
    up = [(i, (i + 1) % peers) for i in range(peers)]
    down = [(j, i) for i, j in up]
    beyond = jnp.stack([lax.ppermute(pack[:, 1], "lon", up), lax.ppermute(pack[:, 0], "lon", down)], 1)
    halo_adj = beyond[: 5 * levels].reshape(5, levels, 2, lat)
    halo_zc = beyond[5 * levels :]

    smoothed = polar_filter(grouped, cutoff, peers)
    smoothed = smoothed.reshape(2, peers // 2, 5, levels, rows, lon_dev + 2)
    smoothed = smoothed.transpose(2, 5, 0, 3, 1, 4).reshape(5, lon_dev + 2, 2, levels, POLAR)
    north, south = smoothed[:, :, 0], smoothed[:, :, 1]
    gap = ((0, 0), (0, 0), (0, 0))
    smooth = jnp.concatenate(
        [jnp.pad(north, (*gap, (0, 128 - POLAR))), jnp.pad(south, (*gap, (128 - POLAR, 0)))], 2
    )[:, 1 : lon_dev + 1]
    outer = [jnp.swapaxes(x[:, :: lon_dev + 1], 1, 2) for x in (north, south)]
    halo_f = jnp.concatenate([outer[0], halo_adj[..., POLAR : lat - POLAR], outer[1]], 3)
    halo = jnp.stack(coupled(halo_zc, [halo_f[f] for f in range(5)], 0))
    out = stencil(
        seat, cot, vw, to_rows(zonal_coef), to_rows(merid_coef), smooth, to_rows(halo), edges, levels
    )
    return from_rows(out, levels)


def lane_of(shape):
    return lax.broadcasted_iota(jnp.int32, shape, len(shape) - 1)


def pair_up(a, b, lane):
    inner = jnp.where(lane < 64, pltpu.roll(b, POLAR, 1), pltpu.roll(b, 128 - POLAR, 1))
    return jnp.where((lane >= POLAR) & (lane < 128 - POLAR), inner, a)


def second_of(pair, lane):
    return jnp.where(lane < 64, pltpu.roll(pair, 128 - POLAR, 1), pltpu.roll(pair, POLAR, 1))


def polar_level(levels, north, south, k, lane):
    lon, rows, _ = north.shape
    near = north.reshape(lon * rows, 128)[pl.ds(k, lon, stride=rows), :]
    far = south.reshape(lon * rows, 128)[pl.ds(levels + k, lon, stride=rows), :]
    return jnp.where(lane < 64, near, far)


def edge_block(levels, front, cot, vw, out):
    fields, chunk, rows, _ = cot.shape
    tiles = rows // levels
    flat_c = cot.reshape(fields * chunk * rows, 128)
    flat_v = vw.reshape(chunk * rows, 128)
    flat_t = cot.at[2].reshape(chunk * rows, 128)

    def product(k, sign):
        c = flat_c[pl.ds(k, fields * chunk * tiles, stride=levels), :]
        v = flat_v[pl.ds(k, chunk * tiles, stride=levels), :]
        c = c.reshape(fields, chunk, tiles, 128)
        out[:fields] = sign * (v.reshape(1, chunk, tiles, 128) * c)

    total = flat_t[pl.ds(0, chunk * tiles, stride=levels), :]
    for k in range(1, levels):
        total = total + flat_t[pl.ds(k, chunk * tiles, stride=levels), :]
    out[fields] = jnp.where(front, 0.0, total.reshape(chunk, tiles, 128))
    pl.when(front)(lambda: product(levels - 1, -1.0))
    pl.when(jnp.logical_not(front))(lambda: product(0, 1.0))


def edge_pack(levels, front, cot, vw, out):
    _, chunk, rows, _ = cot.shape
    tiles = rows // levels
    lane = lane_of((chunk, 128))
    k = jnp.where(front, levels - 1, 0)
    sign = jnp.where(front, -1.0, 1.0)
    flat_v = vw.reshape(chunk * rows, 128)
    wind = [sign * flat_v[pl.ds(t * levels + k, chunk, stride=rows), :] for t in range(tiles)]
    spare = []
    for f in range(6):
        flat = cot.at[min(f, 4) if f < 5 else 2].reshape(chunk * rows, 128)
        w = []
        for t in range(tiles):
            if f < 5:
                w.append(wind[t] * flat[pl.ds(t * levels + k, chunk, stride=rows), :])
            else:
                total = flat[pl.ds(t * levels, chunk, stride=rows), :]
                for n in range(1, levels):
                    total = total + flat[pl.ds(t * levels + n, chunk, stride=rows), :]
                w.append(jnp.where(front, 0.0, total))
        at = f * (tiles - 1)
        out[at] = jnp.where(lane < POLAR, w[-1], w[0])
        for t in range(1, tiles - 1):
            out[at + t] = w[t]
        spare.append(w[-1])
        if f % 2:
            inner = (lane >= POLAR) & (lane < 128 - POLAR)
            out[6 * (tiles - 1) + f // 2] = jnp.where(inner, spare[f - 1], pltpu.roll(spare[f], 64, 1))


def edge_unpack(tiles, edges, polar, full):
    chunk = edges.shape[1]
    lane = lane_of((chunk, 128))
    for f in range(6):
        at = f * (tiles - 1)
        mixed, rest, near = edges[at], edges[6 * (tiles - 1) + f // 2], polar[f]
        if f % 2:
            rest = pltpu.roll(rest, 64, 1)
        full[f * tiles] = jnp.where(lane < POLAR, near, mixed)
        for t in range(1, tiles - 1):
            full[f * tiles + t] = edges[at + t]
        last = jnp.where(lane < 128 - POLAR, rest, near)
        full[f * tiles + tiles - 1] = jnp.where(lane < POLAR, mixed, last)


def open_kernel(levels, seat, cot, vw, sent, ends, local, cn, cs, vn, vs, ec, ev, below, made, sems, out_sems):
    _, lon, rows, _ = cot.shape
    wide = 2 * levels
    lane = lane_of((lon, 128))
    front = seat[0] == 0
    near, far = pl.ds(0, wide), pl.ds(rows - wide, wide)
    jobs = [(vw.at[:, near], vn), (vw.at[:, far], vs)]
    order = (2, 0, 1, 3, 4)
    for f in order:
        jobs += [(cot.at[f, :, near], cn.at[f]), (cot.at[f, :, far], cs.at[f])]
    for n, e in enumerate((0, lon - 1)):
        jobs += [(cot.at[:, e], ec.at[:, n]), (vw.at[e], ev.at[n])]
    jobs = [pltpu.make_async_copy(a, b, sems.at[n]) for n, (a, b) in enumerate(jobs)]
    for job in jobs:
        job.start()
    jobs[0].wait()
    jobs[1].wait()
    v = [polar_level(levels, vn, vs, k, lane) for k in range(levels)]
    half, away = levels // 2, []
    for n, f in enumerate(order):
        jobs[2 + 2 * n].wait()
        jobs[3 + 2 * n].wait()
        c = [polar_level(levels, cn.at[f], cs.at[f], k, lane) for k in range(levels)]
        w = [a * b for a, b in zip(v, c)]
        edge = jnp.where(front, -w[levels - 1], w[0])
        if f == 2:
            run = c[levels - 1]
            below[levels - 1] = run
            for k in range(levels - 2, -1, -1):
                run = run + c[k]
                below[k] = run
            total = jnp.where(front, 0.0, run)
            sent[2] = total
        if f == 4:
            sent[2] = pair_up(edge, sent[2], lane)
        elif f == 2:
            sent[1] = edge
        elif f % 2:
            sent[f // 2] = pair_up(sent[f // 2], edge, lane)
        else:
            sent[f // 2] = edge
        for k in range(0, levels, 2):
            pieces = []
            for at in (k, k + 1):
                a = c[at]
                if at < levels - 1:
                    a = a + w[at + 1]
                if at > 0:
                    a = a - w[at - 1]
                if f == 3:
                    a = a - COUPLE_B * below[at]
                pieces.append(a)
            made[f * half + k // 2] = pair_up(pieces[0], pieces[1], lane)
        mine = pl.ds(f * half, half)
        away.append(pltpu.make_async_copy(made.at[mine], local.at[mine], out_sems.at[f]))
        away[-1].start()
    for job in jobs[12:]:
        job.wait()
    edge_block(levels, front, ec, ev, ends)
    for job in away:
        job.wait()


def opening(seat, cot, vw, levels):
    _, lon, rows, _ = cot.shape
    tiles, wide = rows // levels, 2 * levels
    f32 = jnp.float32
    place = pl.BlockSpec(memory_space=pltpu.HBM)
    vmem = pl.BlockSpec(memory_space=pltpu.VMEM)
    return pl.pallas_call(
        functools.partial(open_kernel, levels),
        out_shape=[
            jax.ShapeDtypeStruct((3, lon, 128), f32),
            jax.ShapeDtypeStruct((6, 2, tiles, 128), f32),
            pltpu.HBM((5 * levels // 2, lon, 128), f32),
        ],
        in_specs=[pl.BlockSpec(memory_space=pltpu.SMEM), place, place],
        out_specs=[vmem, vmem, place],
        scratch_shapes=[
            pltpu.VMEM((5, lon, wide, 128), f32), pltpu.VMEM((5, lon, wide, 128), f32),
            pltpu.VMEM((lon, wide, 128), f32), pltpu.VMEM((lon, wide, 128), f32),
            pltpu.VMEM((5, 2, rows, 128), f32), pltpu.VMEM((2, rows, 128), f32),
            pltpu.VMEM((levels, lon, 128), f32), pltpu.VMEM((5 * levels // 2, lon, 128), f32),
            pltpu.SemaphoreType.DMA((16,)), pltpu.SemaphoreType.DMA((5,)),
        ],
        compiler_params=pltpu.CompilerParams(vmem_limit_bytes=ROOM),
        cost_estimate=pl.CostEstimate(flops=9_000_000, bytes_accessed=10_000_000, transcendentals=0),
        name="opening",
    )(seat, cot, vw)


def edge_run_kernel(levels, start, chunk, count, seat, cot, vw, out, cbuf, vbuf, sems):
    def jobs(n):
        at = pl.ds(start + n * chunk, chunk)
        return (
            pltpu.make_async_copy(cot.at[:, at], cbuf.at[n], sems.at[n, 0]),
            pltpu.make_async_copy(vw.at[at], vbuf.at[n], sems.at[n, 1]),
        )

    for n in range(count):
        for job in jobs(n):
            job.start()
    for n in range(count):
        for job in jobs(n):
            job.wait()
        edge_pack(
            levels, seat[0] == 0, cbuf.at[n], vbuf.at[n], out.at[:, pl.ds(n * chunk, chunk)]
        )


def packed_rows(tiles):
    return 6 * (tiles - 1) + 3


def edge_run(seat, cot, vw, levels, start, chunk, count):
    fields, _, rows, _ = cot.shape
    tiles = rows // levels
    place = pl.BlockSpec(memory_space=pl.ANY)
    size = count * chunk
    return pl.pallas_call(
        functools.partial(edge_run_kernel, levels, start, chunk, count),
        out_shape=jax.ShapeDtypeStruct((packed_rows(tiles), size, 128), jnp.float32),
        in_specs=[pl.BlockSpec(memory_space=pltpu.SMEM), place, place],
        out_specs=pl.BlockSpec(memory_space=pltpu.VMEM),
        scratch_shapes=[
            pltpu.VMEM((count, fields, chunk, rows, 128), jnp.float32),
            pltpu.VMEM((count, chunk, rows, 128), jnp.float32),
            pltpu.SemaphoreType.DMA((count, 2)),
        ],
        compiler_params=pltpu.CompilerParams(vmem_limit_bytes=SOME),
        cost_estimate=pl.CostEstimate(
            flops=50_000 * size, bytes_accessed=120_000 * size, transcendentals=0
        ),
        name="edge_run",
    )(seat, cot, vw)


def slots_of(k, nq):
    north, south = range(nq // 2), range(nq // 2, nq)
    return (
        [(k, q) for q in north] + [(k + 1, q) for q in north]
        + [(k + 1, q) for q in south] + [(k, q) for q in south]
    )


def polar_kernel(
    peers, levels, late,
    cot, vw, zc, fwd, inv, ct, st, local, got, ends, mask_ref,
    smooth, flux_west, flux_east, polar, *rest,
):
    late_out, rest = rest[: len(late)], rest[len(late) :]
    count = len(late)
    cbufs, vbufs, ebufs = rest[:count], rest[count : 2 * count], rest[2 * count : 3 * count]
    (fwd_ref, inv_ref, ct_ref, st_ref, mine_ref, x_ref, held, made, back, z, zt, ec, ev, ez, es, spread, below_ref,
     own_sem, wave_sem, send_a, recv_a, send_b, recv_b, col_sem, late_in, late_sem) = rest[3 * count :]
    me = lax.axis_index("lon")
    front = lax.axis_index("lev") == 0
    _, lon, rows, _ = cot.shape
    wide = 2 * levels
    nq = peers // levels
    span = 2 * POLAR // nq
    cols = 5 * span
    half = cols // 2
    kpad = ct_ref.shape[2]
    lane = lane_of((lon, 128))
    barrier = pltpu.get_barrier_semaphore()

    def ahead(o):
        return lax.rem(me + o, peers)

    def behind(o):
        return lax.rem(me + peers - o, peers)

    def greet(o, _):
        pl.semaphore_signal(barrier, inc=1, device_id={"lon": ahead(o)}, device_id_type=MESH)
        return 0

    own_part = pltpu.make_async_copy(local, mine_ref, wave_sem.at[4])
    own_part.start()
    lax.fori_loop(1, peers, greet, 0)

    column_jobs = []
    for n, e in enumerate((0, lon - 1)):
        for m, (a, b) in enumerate(
            ((cot.at[:, e], ec.at[:, n]), (vw.at[e], ev.at[n]), (zc.at[e], ez.at[n]))
        ):
            column_jobs.append(pltpu.make_async_copy(a, b, col_sem.at[3 * n + m]))
    late_jobs, late_outs = [], []
    for n, (out, (start, size, _)) in enumerate(zip(late_out, late)):
        where = pl.ds(start, size)
        late_jobs.append((
            pltpu.make_async_copy(cot.at[:, where], cbufs[n], late_in.at[n, 0]),
            pltpu.make_async_copy(vw.at[where], vbufs[n], late_in.at[n, 1]),
        ))
        late_outs.append(pltpu.make_async_copy(ebufs[n], out, late_sem.at[n]))
    wave_jobs = [
        pltpu.make_async_copy(fwd, fwd_ref, wave_sem.at[0]),
        pltpu.make_async_copy(inv, inv_ref, wave_sem.at[1]),
        pltpu.make_async_copy(ct, ct_ref, wave_sem.at[2]),
        pltpu.make_async_copy(st, st_ref, wave_sem.at[3]),
    ]
    for job in column_jobs + wave_jobs:
        job.start()
    for jobs in late_jobs:
        for job in jobs:
            job.start()

    z[...] = jnp.zeros_like(z)
    own_part.wait()
    for f in range(5):
        pair = got[f // 2]
        edge = second_of(pair, lane) if f % 2 else pair
        tail = second_of(got[2], lane) if f == 3 else None
        for k in range(0, levels, 2):
            add = []
            for at in (k, k + 1):
                a = jnp.zeros((lon, 128), jnp.float32)
                if at == levels - 1:
                    a = a + jnp.where(front, edge, 0.0)
                if at == 0:
                    a = a + jnp.where(front, 0.0, edge)
                if f == 3:
                    a = a - COUPLE_B * tail
                add.append(a)
            z[:lon] = mine_ref[f * levels // 2 + k // 2] + pair_up(add[0], add[1], lane)
            zt[...] = z[...].T
            for n, (at, q) in enumerate(slots_of(k, nq)):
                d = at * nq + q
                x_ref[d, f * span : (f + 1) * span] = zt[n * span : (n + 1) * span, :128]
                for h in range(0, span, 8):
                    to = f * span + h
                    end = zt[n * span + h : n * span + h + 8, 128:]
                    if to < half:
                        x_ref[d, cols + to : cols + to + 8] = end
                    else:
                        to += cols - half
                        x_ref[d, to : to + 8] += pltpu.roll(end, 64, 1)

    def out_copy(d):
        return pltpu.make_async_remote_copy(
            src_ref=x_ref.at[d], dst_ref=held.at[me], send_sem=send_a.at[d],
            recv_sem=recv_a.at[me], device_id={"lon": d}, device_id_type=MESH,
        )

    def in_copy(s):
        return pltpu.make_async_remote_copy(
            src_ref=x_ref.at[s], dst_ref=held.at[s], send_sem=send_a.at[s],
            recv_sem=recv_a.at[s], device_id={"lon": s}, device_id_type=MESH,
        )

    def back_copy(d):
        return pltpu.make_async_remote_copy(
            src_ref=made.at[d], dst_ref=back.at[me], send_sem=send_b.at[d],
            recv_sem=recv_b.at[me], device_id={"lon": d}, device_id_type=MESH,
        )

    def home_copy(s):
        return pltpu.make_async_remote_copy(
            src_ref=made.at[s], dst_ref=back.at[s], send_sem=send_b.at[s],
            recv_sem=recv_b.at[s], device_id={"lon": s}, device_id_type=MESH,
        )

    pl.semaphore_wait(barrier, peers - 1)
    lax.fori_loop(1, peers, lambda o, c: (out_copy(ahead(o)).start(), c)[1], 0)
    own = pltpu.make_async_copy(x_ref.at[me], held.at[me], own_sem)
    own.start()

    for n, jobs in enumerate(late_jobs):
        for job in jobs:
            job.wait()
        (edge_pack if late[n][2] else edge_block)(levels, front, cbufs[n], vbufs[n], ebufs[n])
        late_outs[n].start()

    for job in wave_jobs:
        job.wait()
    for f in range(6):
        polar[f] = second_of(got[f // 2], lane) if f % 2 else got[f // 2]
    own.wait()
    zero = jnp.zeros((cols, kpad), jnp.float32)
    dot = functools.partial(jnp.dot, precision=HIGHEST, preferred_element_type=jnp.float32)

    def gather(s, carry):
        a, b = carry
        ends = held[s, cols:]
        ends = jnp.concatenate([ends[:, :64], ends[:, 64:]], 0)
        both = dot(held[s, :cols], fwd_ref[:128]) + dot(ends, fwd_ref[128:])
        c, v = both[:, :kpad], both[:, kpad:]
        cos, sin = ct_ref[s], st_ref[s]
        return a + (cos * c - sin * v), b + (sin * c + cos * v)

    def arrive(o, carry):
        s = behind(o)
        in_copy(s).wait_recv()
        return gather(s, carry)

    a, b = lax.fori_loop(1, peers, arrive, gather(me, (zero, zero)))
    mask = jnp.concatenate([mask_ref[...]] * 5, 0)
    a = a * mask
    b = b * mask

    def turn(d):
        cos, sin = ct_ref[d], st_ref[d]
        p, q = a * cos + b * sin, b * cos - a * sin
        y = dot(p, inv_ref[0]) + dot(q, inv_ref[1])
        made[d, :cols] = y[:, :128]
        made[d, cols:] = jnp.concatenate([y[:half, 128:], y[half:, 128:]], 1)

    far = peers - peers // 2

    def turn_of(n):
        return ahead(jnp.where(n < far, n + peers // 2, n - far + 1))

    def depart(n, _):
        turn(turn_of(n))
        pl.when(n > 0)(lambda: back_copy(turn_of(n - 1)).start())
        return 0

    lax.fori_loop(0, peers - 1, depart, 0)
    turn(me)
    back_copy(turn_of(peers - 2)).start()
    mine = pltpu.make_async_copy(made.at[me], back.at[me], own_sem)
    mine.start()
    for job in late_outs:
        job.wait()
    for job in column_jobs:
        job.wait()
    mine.wait()
    lax.fori_loop(1, peers, lambda o, c: (home_copy(behind(o)).wait_recv(), c)[1], 0)

    for f in range(5):
        flat = smooth.at[f].reshape(lon * wide, 128)
        for k in range(0, levels, 2):
            for n, (at, q) in enumerate(slots_of(k, nq)):
                d = at * nq + q
                zt[n * span : (n + 1) * span, :128] = back[d, f * span : (f + 1) * span]
                for h in range(0, span, 8):
                    to = f * span + h
                    if to < half:
                        end = back[d, cols + to : cols + to + 8]
                    else:
                        to += cols - half
                        end = pltpu.roll(back[d, to : to + 8], 64, 1)
                    zt[n * span + h : n * span + h + 8, 128:] = end
            z[...] = zt[...].T
            first = z[:lon]
            flat[pl.ds(k, lon, stride=wide), :] = first
            flat[pl.ds(levels + k, lon, stride=wide), :] = first
            flat[pl.ds(k + 1, lon, stride=wide), :] = pltpu.roll(first, 128 - POLAR, 1)
            flat[pl.ds(levels + k + 1, lon, stride=wide), :] = pltpu.roll(first, POLAR, 1)

    for f in range(5):
        for n, e in enumerate((0, lon - 1)):
            es[f, n] = smooth[f, e]
    spread[...] = jnp.zeros_like(spread)
    column = column_maker(levels, front, ec, ev, es, lambda f, l: ends[f, l], spread, below_ref)
    for n in range(2):
        field = column(n)
        fields = [field(f)[1] for f in range(5)]
        for v in range(rows // 8):
            zonal = coupled(ez[n, 8 * v : 8 * v + 8], [fields[f][v] for f in range(5)], 0)
            for f in range(5):
                (flux_west, flux_east)[n][f, 8 * v : 8 * v + 8] = zonal[f]
    lax.fori_loop(1, peers, lambda o, c: (out_copy(ahead(o)).wait_send(), c)[1], 0)
    lax.fori_loop(1, peers, lambda o, c: (back_copy(ahead(o)).wait_send(), c)[1], 0)


def hold(a):
    return pltpu.with_memory_space_constraint(jnp.asarray(a), pltpu.HBM)


def polar_path(cot, vw, zc, local, got, ends, cutoff, levels, peers, late):
    _, lon, rows, _ = cot.shape
    tiles, wide = rows // levels, 2 * levels
    nq = peers // levels
    nlon = peers * lon
    span = cutoff.shape[0] // nq
    kpad = (KMAX + 1 + 127) // 128 * 128
    wave = np.arange(kpad)
    fwd = np.concatenate(angles(np.arange(lon)[:, None], wave[None, :], nlon), axis=1)
    inv = np.stack(angles(wave[:, None], np.arange(lon)[None, :], nlon))
    short = 192 - lon
    fwd = np.pad(fwd, ((0, short), (0, 0)))
    inv = np.pad(inv, ((0, 0), (0, 0), (0, short)))
    ct, st = angles(np.arange(peers)[:, None, None] * lon, wave[None, None, :], nlon)
    mine = lax.dynamic_slice_in_dim(cutoff, lax.axis_index("lon") % nq * span, span)
    weight = np.where(wave == 0, 1.0 / nlon, 2.0 / nlon).astype(np.float32)
    mask = jnp.where(jnp.asarray(wave, jnp.int32)[None, :] <= mine[:, None], weight[None, :], 0.0)
    vmem = pl.BlockSpec(memory_space=pltpu.VMEM)
    place = pl.BlockSpec(memory_space=pltpu.HBM)
    dma = pltpu.SemaphoreType.DMA
    f32 = jnp.float32
    shape = (peers, 5 * span + 5 * span // 2, 128)
    count = len(late)
    away = [
        (packed_rows(tiles), size, 128) if packed else (6, size, tiles, 128) for _, size, packed in late
    ]
    return pl.pallas_call(
        functools.partial(polar_kernel, peers, levels, late),
        out_shape=[
            jax.ShapeDtypeStruct((5, lon, wide, 128), f32),
            jax.ShapeDtypeStruct((5, rows, 128), f32),
            jax.ShapeDtypeStruct((5, rows, 128), f32),
            jax.ShapeDtypeStruct((6, lon, 128), f32),
        ] + [jax.ShapeDtypeStruct(a, f32) for a in away],
        in_specs=[place] * 8 + [vmem] * 3,
        out_specs=[vmem] * 4 + [place] * count,
        scratch_shapes=[pltpu.VMEM((5, size, rows, 128), f32) for _, size, _ in late]
        + [pltpu.VMEM((size, rows, 128), f32) for _, size, _ in late]
        + [pltpu.VMEM(a, f32) for a in away]
        + [
            pltpu.VMEM(fwd.shape, f32), pltpu.VMEM(inv.shape, f32),
            pltpu.VMEM(ct.shape, f32), pltpu.VMEM(st.shape, f32), pltpu.VMEM(local.shape, f32),
            pltpu.VMEM(shape, f32), pltpu.VMEM(shape, f32), pltpu.VMEM(shape, f32),
            pltpu.VMEM(shape, f32), pltpu.VMEM((256, 128), f32), pltpu.VMEM((128, 256), f32),
            pltpu.VMEM((5, 2, rows, 128), f32), pltpu.VMEM((2, rows, 128), f32),
            pltpu.VMEM((2, rows, 128), f32), pltpu.VMEM((5, 2, wide, 128), f32),
            pltpu.VMEM((1, 5, rows, 128), f32),
            pltpu.VMEM((1, rows, 128), f32),
            dma(()), dma((5,)), dma((peers,)), dma((peers,)), dma((peers,)), dma((peers,)),
            dma((6,)), dma((count, 2)), dma((count,)),
        ],
        compiler_params=pltpu.CompilerParams(
            collective_id=1, has_side_effects=True, vmem_limit_bytes=30 << 20
        ),
        cost_estimate=pl.CostEstimate(flops=8_000_000_000, bytes_accessed=60_000_000, transcendentals=0),
        name="polar_path",
    )(cot, vw, zc, *(hold(a) for a in (fwd, inv, ct, st, local)), got, ends, mask)


def column_maker(levels, front, cot, vw, smooth, edges, spread, below_ref):
    _, _, rows, _ = cot.shape
    tiles = rows // levels
    parts = rows // 8
    edge_at = jnp.where(front, levels - 1, 0)
    row = lax.broadcasted_iota(jnp.int32, (8, 128), 0)
    lane = lane_of((8, 128))
    k = lax.rem(row, levels)
    north = (row < levels) & (lane < POLAR)
    south = (row >= levels) & (lane >= 128 - POLAR)
    at = [pl.ds(8 * v, 8) for v in range(parts)]

    def column(l, side=0):
        for f in range(5):
            spread[side, f, pl.ds(edge_at, tiles, stride=levels), :] = edges(f, l)
        for n in range(levels):
            below_ref[side, pl.ds(n, tiles, stride=levels), :] = edges(5, l)
        wind = [vw[l, a] for a in at]
        under = [jnp.where(k > 0, a, 0.0) for a in wind]
        over = [jnp.where(k < levels - 1, a, 0.0) for a in wind]

        def field(f):
            whole, inner = [], []
            for v in range(parts):
                c = cot[f, l, at[v]]
                a = c + (pltpu.roll(under[v] * c, 7, 0) - pltpu.roll(over[v] * c, 1, 0))
                a = a + spread[side, f, at[v]]
                if f == 3:
                    run, r = cot[2, l, at[v]], 1
                    while r < levels:
                        run = run + jnp.where(k < levels - r, pltpu.roll(run, 8 - r, 0), 0.0)
                        r *= 2
                    a = a - COUPLE_B * (run + below_ref[side, at[v]])
                whole.append(a)
                if v == 0:
                    a = jnp.where(north, smooth[f, l], a)
                if v == parts - 1:
                    a = jnp.where(south, smooth[f, l], a)
                inner.append(a)
            return whole, inner

        return field

    return column


def lat_change(levels, m):
    row = lax.broadcasted_iota(jnp.int32, (8, 128), 0)
    lane = lane_of((8, 128))
    top = row < levels
    turned = [pltpu.roll(a, levels, 0) for a in m]
    zero = jnp.zeros((8, 128), jnp.float32)
    tile = [jnp.where(top, a, b) for a, b in zip([zero] + turned, turned + [zero])]
    out = []
    for v, a in enumerate(m):
        near = pltpu.roll(jnp.where(lane == 127, tile[v], a), 1, 1)
        far = pltpu.roll(jnp.where(lane == 0, tile[v + 1], a), 127, 1)
        out.append(far - near)
    return out


def strip_kernel(levels, start, steps, first, last, packed, seat, cot, vw, zc, mc, smooth, edges, *rest):
    rest = list(rest)
    if packed:
        polar, full = rest.pop(0), rest.pop()
    if not first:
        wait_in, prior_in, _ = rest.pop(0), rest.pop(0), rest.pop(0)
    if last:
        left, right, column_in = rest.pop(0), rest.pop(0), rest.pop(0)
    if first:
        column_out = rest.pop(1)
    out, wait, prior, ready, spread, below_ref, sems = rest[:7]
    _, chunk, rows, _ = cot.shape
    parts = rows // 8
    g = pl.program_id(0)
    slot = lax.rem(g, 2)

    def first_copy():
        return pltpu.make_async_copy(
            ready.at[0, :, pl.ds(2, chunk - 2)], out.at[:, pl.ds(1, chunk - 2)], sems.at[0]
        )

    def copy(at):
        s = lax.rem(at, 2)
        return pltpu.make_async_copy(
            ready.at[s], out.at[:, pl.ds(start + at * chunk - 1, chunk)], sems.at[s]
        )

    def act(at, what):
        if first:
            pl.when(at == 0)(lambda: getattr(first_copy(), what)())
            pl.when(at > 0)(lambda: getattr(copy(at), what)())
        else:
            getattr(copy(at), what)()

    @pl.when(g == 0)
    def _():
        spread[...] = jnp.zeros_like(spread)
        if first:
            prior[...] = jnp.zeros_like(prior)
            wait[...] = jnp.zeros_like(wait)
        else:
            prior[...] = prior_in[...]
            wait[...] = wait_in[...]

    pl.when(g >= 2)(lambda: act(g - 2, "wait"))
    if packed:
        tiles = rows // levels
        edge_unpack(tiles, edges, polar, full)
        flat = full.reshape(6 * tiles * chunk, 128)
        sent = lambda f, l: flat[pl.ds(f * tiles * chunk + l, tiles, stride=chunk), :]
    else:
        sent = lambda f, l: edges[f, l]
    column = column_maker(levels, seat[0] == 0, cot, vw, smooth, sent, spread, below_ref)
    at = [pl.ds(8 * v, 8) for v in range(parts)]

    def flux_of(l, side):
        field = column(l, side)
        zcs = [zc[l, a] for a in at]
        mcs = [mc[l, a] for a in at]
        whole3, f3 = field(3)
        half3 = [COUPLE_H * a for a in f3]
        parted, zonal = [None] * 5, [None] * 5

        def close(f, whole, inner, add_zonal=None, add_merid=None):
            z = [a * b for a, b in zip(zcs, inner)]
            m = [a * b for a, b in zip(mcs, inner)]
            if add_zonal is not None:
                z = [a + b for a, b in zip(z, add_zonal)]
            if add_merid is not None:
                m = [a + b for a, b in zip(m, add_merid)]
            zonal[f] = z
            parted[f] = [a + b for a, b in zip(whole, lat_change(levels, m))]

        whole, f0 = field(0)
        close(0, whole, f0, add_zonal=half3)
        whole, f1 = field(1)
        close(1, whole, f1, add_merid=half3)
        close(3, whole3, f3, [COUPLE_G * a for a in f0], [COUPLE_G * a for a in f1])
        for f in (2, 4):
            close(f, *field(f))
        return parted, zonal

    def one(l):
        parted, zonal = flux_of(l, 0)
        for f in range(5):
            for v in range(parts):
                ready[slot, f, l, at[v]] = wait[f, at[v]] + zonal[f][v]
                wait[f, at[v]] = parted[f][v] - prior[f, at[v]]
                prior[f, at[v]] = zonal[f][v]

    def two(n, _):
        l = 2 * n
        parted, zonal = flux_of(l, 0)
        for f in range(5):
            for v in range(parts):
                ready[slot, f, l, at[v]] = wait[f, at[v]] + zonal[f][v]
                parted[f][v] = parted[f][v] - prior[f, at[v]]
        later, after = flux_of(l + 1, 1)
        for f in range(5):
            for v in range(parts):
                ready[slot, f, l + 1, at[v]] = parted[f][v] + after[f][v]
                wait[f, at[v]] = later[f][v] - zonal[f][v]
                prior[f, at[v]] = after[f][v]
        return 0

    lax.fori_loop(0, chunk // 2, two, 0)
    if chunk % 2:
        one(chunk - 1)
    act(g, "start")
    if first:

        @pl.when(g == 0)
        def _():
            for f in range(5):
                column_out[f] = ready[0, f, 1]

    @pl.when(g == steps - 1)
    def _():
        if last:
            final, last_sem = rest[7:9]
            for f in range(5):
                final[0, f, 0] = column_in[f] - left[f]
                final[1, f, 0] = wait[f] + right[f]
            ends = [
                pltpu.make_async_copy(final.at[n], out.at[:, pl.ds(e, 1)], last_sem.at[n])
                for n, e in enumerate((0, start + steps * chunk - 1))
            ]
            for end in ends:
                end.start()
        if steps > 1:
            act(g - 1, "wait")
        act(g, "wait")
        if last:
            for end in ends:
                end.wait()


def strip(seat, cot, vw, zc, mc, smooth, edges, polar, state, borders, levels, start, steps, chunk):
    _, _, rows, _ = cot.shape
    tiles = rows // levels
    at = start // chunk
    first, last = not state, borders is not None
    field = lambda n: pl.BlockSpec((5, chunk, n, 128), lambda g, s: (0, at + g, 0, 0))
    plain = pl.BlockSpec((chunk, rows, 128), lambda g, s: (at + g, 0, 0))
    whole = pl.BlockSpec((5, rows, 128), lambda g, s: (0, 0, 0))
    place = pl.BlockSpec(memory_space=pl.ANY)
    packed = polar is not None
    in_specs = [field(rows), plain, plain, plain, field(2 * levels)]
    if packed:
        in_specs += [
            pl.BlockSpec((edges.shape[0], chunk, 128), lambda g, s: (0, g, 0)),
            pl.BlockSpec((6, chunk, 128), lambda g, s: (0, at + g, 0)),
        ]
    else:
        in_specs.append(pl.BlockSpec((6, chunk, tiles, 128), lambda g, s: (0, g, 0, 0)))
    in_specs += [] if first else [whole, whole, place]
    args = [seat, cot, vw, zc, mc, smooth, edges] + [polar] * packed + [*state]
    aliases = {} if first else {len(args) - 1: 0}
    if last:
        in_specs += [whole] * 3
        args += borders
    one = jax.ShapeDtypeStruct((5, rows, 128), jnp.float32)
    held = [pltpu.VMEM((5, rows, 128), jnp.float32)] * 2
    scratch = [
        pltpu.VMEM((2, 5, chunk, rows, 128), jnp.float32),
        pltpu.VMEM((2, 5, rows, 128), jnp.float32),
        pltpu.VMEM((2, rows, 128), jnp.float32),
        pltpu.SemaphoreType.DMA((2,)),
    ]
    if last:
        scratch = held + scratch + [
            pltpu.VMEM((2, 5, 1, rows, 128), jnp.float32), pltpu.SemaphoreType.DMA((2,)),
        ]
    if packed:
        scratch = scratch + [pltpu.VMEM((6 * tiles, chunk, 128), jnp.float32)]
    extra = 0 if last else 3 if first else 2
    got = pl.pallas_call(
        functools.partial(strip_kernel, levels, start, steps, first, last, packed),
        out_shape=[jax.ShapeDtypeStruct(cot.shape, jnp.float32)] + [one] * extra,
        grid_spec=pltpu.PrefetchScalarGridSpec(
            num_scalar_prefetch=1,
            grid=(steps,),
            in_specs=in_specs,
            out_specs=[place] + [whole] * extra,
            scratch_shapes=scratch,
        ),
        input_output_aliases=aliases,
        compiler_params=pltpu.CompilerParams(vmem_limit_bytes=SOME),
        cost_estimate=pl.CostEstimate(
            flops=30 * 5 * steps * chunk * rows * 128,
            bytes_accessed=4 * 14 * steps * chunk * rows * 128,
            transcendentals=0,
        ),
        name="strip",
    )(*args)
    return got[0] if last else [*got[-2:], got[0], *got[1:-2]]


def fast_body(cotangent, zonal_coef, merid_coef, vertical_wind, cutoff):
    levels, lon_dev, _ = cotangent.shape[1:]
    peers = lax.axis_size("lon")
    seat = lax.axis_index("lev").astype(jnp.int32)[None]
    cot, vw = to_rows(cotangent), to_rows(vertical_wind)
    zc, mc = to_rows(zonal_coef), to_rows(merid_coef)
    cot, vw, zc, mc = (hold(a) for a in (cot, vw, zc, mc))
    trade = lambda a: lax.ppermute(a, "lev", [(0, 1), (1, 0)])
    tail = lon_dev % 8 + 8
    whole = lon_dev - tail
    cuts = [0, 16, 16 + whole * 2 // 3 // 16 * 16, whole, lon_dev]
    parts = [(a, b - a) for a, b in zip(cuts, cuts[1:])]

    edges = []
    part = edge_run(seat, cot, vw, levels, 0, 16, 1)
    edges.append(trade(part))
    token, _ = lax.optimization_barrier((seat, part))
    sent, ends, local = opening(token, cot, vw, levels)
    polar_got = trade(sent)
    ends_got = trade(ends)
    token, _ = lax.optimization_barrier((token, sent))
    start, size = parts[1]
    part = edge_run(token, cot, vw, levels, start, 16, size // 16)
    edges.append(trade(part))
    polar_got, ends_got, _ = lax.optimization_barrier((polar_got, ends_got, part))
    late = (parts[2] + (True,), parts[3] + (False,))
    smooth, west, east, polar, *later = polar_path(
        cot, vw, zc, local, polar_got, ends_got, cutoff, levels, peers, late
    )
    edges += [trade(part) for part in later]
    state, borders, kept = [], None, None
    up = [(i, (i + 1) % peers) for i in range(peers)]
    for n, (start, size) in enumerate(parts):
        lanes, chunk = polar, math.gcd(start, size, 16)
        if n == len(parts) - 1:
            borders = [left, right, kept]
            lanes, chunk = None, math.gcd(start, size)
        state = strip(
            seat, cot, vw, zc, mc, smooth, edges[n], lanes, state, borders, levels, start,
            size // chunk, chunk,
        )
        if n == 0:
            kept = state.pop()
            west, east, state[0] = lax.optimization_barrier((west, east, state[0]))
            left = lax.ppermute(east, "lon", up)
            right = lax.ppermute(west, "lon", [(j, i) for i, j in up])
    return from_rows(state, levels)


def is_fast(mesh, levels, lon_dev, lat, count):
    peers = mesh.shape["lon"]
    return (
        mesh.shape["lev"] == 2 and levels * 2 == 8 and peers % (2 * levels) == 0 and lat % 256 == 0
        and count == 2 * POLAR and count * levels // peers % 16 == 0 and 128 < lon_dev <= 192
    )


def solution(mesh):
    specs = (
        P(None, "lev", "lon", None),
        P("lev", "lon", None),
        P("lev", "lon", None),
        P("lev", "lon", None),
        P(),
    )

    def spread_over(body):
        return jax.shard_map(body, mesh=mesh, in_specs=specs, out_specs=specs[0], check_vma=False)

    def step(cotangent, zonal_coef, merid_coef, vertical_wind, cutoff):
        _, nlev, nlon, lat = cotangent.shape
        levels, lon_dev = nlev // mesh.shape["lev"], nlon // mesh.shape["lon"]
        args = cotangent, zonal_coef, merid_coef, vertical_wind, cutoff
        if is_fast(mesh, levels, lon_dev, lat, cutoff.shape[0]):
            return spread_over(fast_body)(*args)
        return spread_over(plain_body)(*args)

    return step
```

```python
import functools
import math

import jax
import jax.numpy as jnp
import numpy as np
from jax import lax
from jax.experimental import pallas as pl
from jax.experimental.pallas import tpu as pltpu
from jax.sharding import PartitionSpec as P


POLAR = 32
KMAX = 360
COUPLE_G = 0.3
COUPLE_H = 0.3
COUPLE_B = 0.2
MESH = pl.DeviceIdType.MESH
HIGHEST = lax.Precision.HIGHEST
ROOM = 61 << 20
SOME = 36 << 20


def angles(left, right, period):
    phase = (left * right) % period * (2.0 * math.pi / period)
    return np.cos(phase).astype(np.float32), np.sin(phase).astype(np.float32)


def filter_kernel(
    peers, packed, x_ref, fwd_ref, inv_ref, ct_ref, st_ref, mask_ref, out_ref, held, made,
    own_sem, send_a, recv_a, send_b, recv_b,
):
    me = lax.axis_index("lon")
    kpad = ct_ref.shape[2]
    barrier = pltpu.get_barrier_semaphore()

    def greet(o, _):
        pl.semaphore_signal(
            barrier, inc=1, device_id={"lon": lax.rem(me + o, peers)}, device_id_type=MESH
        )
        return 0

    lax.fori_loop(1, peers, greet, 0)
    pl.semaphore_wait(barrier, peers - 1)

    def out_copy(o):
        d = lax.rem(me + o, peers)
        return pltpu.make_async_remote_copy(
            src_ref=x_ref.at[d], dst_ref=held.at[me], send_sem=send_a.at[d],
            recv_sem=recv_a.at[me], device_id={"lon": d}, device_id_type=MESH,
        )

    def in_copy(o):
        s = lax.rem(me + o, peers)
        return pltpu.make_async_remote_copy(
            src_ref=x_ref.at[s], dst_ref=held.at[s], send_sem=send_a.at[s],
            recv_sem=recv_a.at[s], device_id={"lon": s}, device_id_type=MESH,
        )

    def back_copy(o):
        d = lax.rem(me + o, peers)
        return pltpu.make_async_remote_copy(
            src_ref=made.at[d], dst_ref=out_ref.at[me], send_sem=send_b.at[d],
            recv_sem=recv_b.at[me], device_id={"lon": d}, device_id_type=MESH,
        )

    def home_copy(o):
        s = lax.rem(me + o, peers)
        return pltpu.make_async_remote_copy(
            src_ref=made.at[s], dst_ref=out_ref.at[s], send_sem=send_b.at[s],
            recv_sem=recv_b.at[s], device_id={"lon": s}, device_id_type=MESH,
        )

    lax.fori_loop(1, peers, lambda o, c: (out_copy(o).start(), c)[1], 0)
    own = pltpu.make_async_copy(x_ref.at[me], held.at[me], own_sem)
    own.start()
    own.wait()
    cols = mask_ref.shape[0]
    half = cols // 2
    zero = jnp.zeros((cols, kpad), jnp.float32)
    dot = functools.partial(jnp.dot, precision=HIGHEST, preferred_element_type=jnp.float32)

    def gather(s, carry):
        a, b = carry
        if packed:
            ends = held[s, cols:]
            ends = jnp.concatenate([ends[:, :64], ends[:, 64:]], 0)
            both = dot(held[s, :cols], fwd_ref[:128]) + dot(ends, fwd_ref[128:])
        else:
            both = dot(held[s], fwd_ref[...])
        c, v = both[:, :kpad], both[:, kpad:]
        ct, st = ct_ref[s], st_ref[s]
        return a + (ct * c - st * v), b + (st * c + ct * v)

    def arrive(o, carry):
        in_copy(o).wait_recv()
        return gather(lax.rem(me + o, peers), carry)

    a, b = lax.fori_loop(1, peers, arrive, gather(me, (zero, zero)))
    a = a * mask_ref[...]
    b = b * mask_ref[...]

    def spread(d):
        ct, st = ct_ref[d], st_ref[d]
        p, q = a * ct + b * st, b * ct - a * st
        if packed:
            y = dot(p, inv_ref[0]) + dot(q, inv_ref[1])
            made[d, :cols] = y[:, :128]
            made[d, cols:] = jnp.concatenate([y[:half, 128:], y[half:, 128:]], 1)
        else:
            made[d] = dot(p, inv_ref[0]) + dot(q, inv_ref[1])

    def depart(o, _):
        spread(lax.rem(me + o, peers))
        pl.when(o > 1)(lambda: back_copy(o - 1).start())
        return 0

    lax.fori_loop(1, peers, depart, 0)
    spread(me)
    back_copy(peers - 1).start()
    mine = pltpu.make_async_copy(made.at[me], out_ref.at[me], own_sem)
    mine.start()
    mine.wait()
    lax.fori_loop(1, peers, lambda o, c: (home_copy(o).wait_recv(), c)[1], 0)
    lax.fori_loop(1, peers, lambda o, c: (out_copy(o).wait_send(), c)[1], 0)
    lax.fori_loop(1, peers, lambda o, c: (back_copy(o).wait_send(), c)[1], 0)


def polar_filter(x, cutoff, peers):
    _, cols, lon_dev = x.shape
    nlon = peers * lon_dev
    rows = cutoff.shape[0] // peers
    kpad = (KMAX + 1 + 127) // 128 * 128
    wave = np.arange(kpad)
    fwd = np.concatenate(angles(np.arange(lon_dev)[:, None], wave[None, :], nlon), axis=1)
    inv = np.stack(angles(wave[:, None], np.arange(-1, lon_dev + 1)[None, :] % nlon, nlon))
    over, wider = lon_dev - 128, lon_dev + 2 - 128
    packed = over > 0 and wider <= 64 and cols % 16 == 0
    half = cols // 2
    if packed:
        fwd = np.pad(fwd, ((0, 64 - over), (0, 0)))
        inv = np.pad(inv, ((0, 0), (0, 0), (0, 64 - wider)))
        ends = jnp.pad(x[..., 128:], ((0, 0), (0, 0), (0, 64 - over)))
        x = jnp.concatenate([x[..., :128], jnp.concatenate([ends[:, :half], ends[:, half:]], 2)], 1)
        shape = (peers, cols + half, 128)
    else:
        shape = (peers, cols, lon_dev + 2)
    ct, st = angles(np.arange(peers)[:, None, None] * lon_dev, wave[None, None, :], nlon)
    mine = lax.dynamic_slice_in_dim(cutoff, lax.axis_index("lon") * rows, rows)
    weight = np.where(wave == 0, 1.0 / nlon, 2.0 / nlon).astype(np.float32)
    mask = jnp.where(jnp.asarray(wave, jnp.int32)[None, :] <= mine[:, None], weight[None, :], 0.0)
    mask = jnp.tile(mask, (cols // rows, 1))
    vmem = pl.BlockSpec(memory_space=pltpu.VMEM)
    dma = pltpu.SemaphoreType.DMA
    y = pl.pallas_call(
        functools.partial(filter_kernel, peers, packed),
        out_shape=jax.ShapeDtypeStruct(shape, jnp.float32),
        in_specs=[vmem] * 6,
        out_specs=vmem,
        scratch_shapes=[
            pltpu.VMEM(x.shape, jnp.float32),
            pltpu.VMEM(shape, jnp.float32),
            dma(()), dma((peers,)), dma((peers,)), dma((peers,)), dma((peers,)),
        ],
        compiler_params=pltpu.CompilerParams(
            collective_id=0, has_side_effects=True, vmem_limit_bytes=24 << 20
        ),
        cost_estimate=pl.CostEstimate(flops=8_000_000_000, bytes_accessed=60_000_000, transcendentals=0),
        name="polar_filter",
    )(x, fwd, inv, ct, st, mask)
    if not packed:
        return y
    ends = jnp.concatenate([y[:, cols:, :wider], y[:, cols:, 64 : 64 + wider]], 1)
    return jnp.concatenate([y[:, :cols], ends], 2)


def to_rows(x):
    *lead, levels, lon, lat = x.shape
    n = len(lead)
    x = x.reshape(*lead, levels, lon, lat // 128, 128)
    x = x.transpose(*range(n), n + 1, n + 2, n, n + 3)
    return x.reshape(*lead, lon, lat // 128 * levels, 128)


def from_rows(x, levels):
    *lead, lon, rows, _ = x.shape
    n = len(lead)
    x = x.reshape(*lead, lon, rows // levels, levels, 128)
    x = x.transpose(*range(n), n + 2, n, n + 1, n + 3)
    return x.reshape(*lead, levels, lon, rows // levels * 128)


def chunk_of(lon):
    return max(d for d in range(1, 21) if lon % d == 0)


def edge_kernel(levels, choose, seat, cot, vw, *outs):
    fields, chunk, rows, _ = cot.shape
    tiles = rows // levels
    flat_c = cot.reshape(fields * chunk * rows, 128)
    flat_v = vw.reshape(chunk * rows, 128)
    sends = outs[: 1 if choose else 2]

    def level(ref, count, k):
        return ref[pl.ds(k, count * tiles, stride=levels), :] if levels > 1 else ref[...]

    def product(k, sign, out):
        c = level(flat_c, fields * chunk, k).reshape(fields, chunk, tiles, 128)
        v = level(flat_v, chunk, k).reshape(1, chunk, tiles, 128)
        out[:fields] = sign * (v * c)

    flat_t = cot.at[2].reshape(chunk * rows, 128)
    total = level(flat_t, chunk, 0)
    for k in range(1, levels):
        total = total + level(flat_t, chunk, k)
    total = total.reshape(chunk, tiles, 128)
    if choose:
        sends[0][fields] = jnp.where(seat[0] == 0, 0.0, total)
        pl.when(seat[0] == 0)(lambda: product(levels - 1, -1.0, sends[0]))
        pl.when(seat[0] != 0)(lambda: product(0, 1.0, sends[0]))
    else:
        product(0, 1.0, sends[0])
        product(levels - 1, -1.0, sends[1])
        outs[2][...] = total


def edges_of(seat, cot, vw, levels, choose):
    fields, lon, rows, _ = cot.shape
    tiles = rows // levels
    chunk = chunk_of(lon)
    n = 1 if choose else 2
    wide = fields + 1 if choose else fields
    return pl.pallas_call(
        functools.partial(edge_kernel, levels, choose),
        out_shape=[jax.ShapeDtypeStruct((wide, lon, tiles, 128), jnp.float32)] * n
        + [jax.ShapeDtypeStruct((lon, tiles, 128), jnp.float32)] * (n - 1),
        grid_spec=pltpu.PrefetchScalarGridSpec(
            num_scalar_prefetch=1,
            grid=(lon // chunk,),
            in_specs=[
                pl.BlockSpec((fields, chunk, rows, 128), lambda g, s: (0, g, 0, 0)),
                pl.BlockSpec((chunk, rows, 128), lambda g, s: (g, 0, 0)),
            ],
            out_specs=[pl.BlockSpec((wide, chunk, tiles, 128), lambda g, s: (0, g, 0, 0))] * n
            + [pl.BlockSpec((chunk, tiles, 128), lambda g, s: (g, 0, 0))] * (n - 1),
        ),
        compiler_params=pltpu.CompilerParams(vmem_limit_bytes=24 << 20),
        cost_estimate=pl.CostEstimate(flops=10_000_000, bytes_accessed=22_000_000, transcendentals=0),
        name="edges",
    )(seat, cot, vw)


def coupled(coef, fields, first):
    flux = [coef * f for f in fields]
    flux[first] = flux[first] + COUPLE_H * fields[3]
    flux[3] = flux[3] + COUPLE_G * fields[first]
    return flux


def stencil_kernel(levels, steps, n_edge, seat, cot, vw, zc, mc, smooth, halo, *rest):
    edges = rest[:n_edge]
    tail = edges[0].at[5] if n_edge == 1 else rest[n_edge]
    rest = rest[1:] if n_edge > 1 else rest
    edge_at = (1 - seat[0]) * (levels - 1)
    out, ready, final, wait, prior, spread, below_ref, sems, last_sem = rest[n_edge:]
    _, chunk, rows, _ = cot.shape
    tiles = rows // levels
    g = pl.program_id(0)
    slot = lax.rem(g, 2)
    lane = lax.broadcasted_iota(jnp.int32, (rows, 128), 1)
    row = lax.broadcasted_iota(jnp.int32, (rows, 128), 0)
    k = lax.rem(row, levels)
    cap_lane = lax.broadcasted_iota(jnp.int32, (2 * levels, 128), 1)
    cap_row = lax.broadcasted_iota(jnp.int32, (2 * levels, 128), 0)
    north = (cap_row < levels) & (cap_lane < POLAR)
    south = (cap_row >= levels) & (cap_lane >= 128 - POLAR)

    def first_copy():
        return pltpu.make_async_copy(
            ready.at[0, :, pl.ds(1, chunk - 1)], out.at[:, pl.ds(0, chunk - 1)], sems.at[0]
        )

    def copy(at):
        s = lax.rem(at, 2)
        return pltpu.make_async_copy(
            ready.at[s], out.at[:, pl.ds(at * chunk - 1, chunk)], sems.at[s]
        )

    @pl.when(g == 0)
    def _():
        spread[...] = jnp.zeros_like(spread)
        for f in range(5):
            prior[f] = halo[f, 0]
            wait[f] = jnp.zeros((rows, 128), jnp.float32)

    pl.when(g == 2)(lambda: first_copy().wait())
    pl.when(g > 2)(lambda: copy(g - 2).wait())

    def put(ref, at, value):
        if levels > 1:
            ref[pl.ds(at, tiles, stride=levels), :] = value
        else:
            ref[...] = value

    def one(l, _):
        for f in range(5):
            if n_edge == 1:
                put(spread.at[0, f], edge_at, edges[0][f, l])
            else:
                put(spread.at[0, f], levels - 1, edges[0][f, l])
                put(spread.at[1, f], 0, edges[1][f, l])
        for at in range(levels):
            put(below_ref, at, tail[l])
        wind = vw[l]
        base, fields = [], []
        for f in range(5):
            c = cot[f, l]
            w = wind * c
            a = c
            if levels > 1:
                up = jnp.where(k < levels - 1, pltpu.roll(w, rows - 1, 0), 0.0)
                a = a + (up - jnp.where(k > 0, pltpu.roll(w, 1, 0), 0.0))
            for n in range(n_edge):
                a = a + spread[n, f]
            if f == 3:
                theta = cot[2, l]
                below = below_ref[...] + theta
                for r in range(1, levels):
                    below = below + jnp.where(k < levels - r, pltpu.roll(theta, rows - r, 0), 0.0)
                a = a - COUPLE_B * below
            base.append(a)
            s = smooth[f, l]
            top = jnp.where(north, s, a[: 2 * levels])
            low = jnp.where(south, s, a[rows - 2 * levels :])
            fields.append(jnp.concatenate([top, a[2 * levels : rows - 2 * levels], low], 0))
        zonal = coupled(zc[l], fields, 0)
        merid = coupled(mc[l], fields, 1)
        for f in range(5):
            ready[slot, f, l] = wait[f] + zonal[f]
            left = pltpu.roll(merid[f], 1, 1)
            over = jnp.where(row < levels, 0.0, pltpu.roll(left, levels, 0))
            left = jnp.where(lane == 0, over, left)
            right = pltpu.roll(merid[f], 127, 1)
            over = jnp.where(row >= rows - levels, 0.0, pltpu.roll(right, rows - levels, 0))
            right = jnp.where(lane == 127, over, right)
            wait[f] = base[f] + (right - left) - prior[f]
            prior[f] = zonal[f]
        return 0

    lax.fori_loop(0, chunk, one, 0)
    pl.when(g == 0)(lambda: first_copy().start())
    pl.when(g > 0)(lambda: copy(g).start())

    @pl.when(g == steps - 1)
    def _():
        for f in range(5):
            final[f, 0] = wait[f] + halo[f, 1]
        end = pltpu.make_async_copy(final, out.at[:, pl.ds(steps * chunk - 1, 1)], last_sem)
        end.start()
        copy(g - 1).wait() if steps > 2 else first_copy().wait()
        copy(g).wait()
        end.wait()


def stencil(seat, cot, vw, zc, mc, smooth, halo, edges, levels):
    _, lon, rows, _ = cot.shape
    tiles = rows // levels
    chunk = chunk_of(lon)
    steps = lon // chunk
    field = lambda n: pl.BlockSpec((5, chunk, n, 128), lambda g, s: (0, g, 0, 0))
    plain = lambda n: pl.BlockSpec((chunk, n, 128), lambda g, s: (g, 0, 0))
    return pl.pallas_call(
        functools.partial(stencil_kernel, levels, steps, min(len(edges), 2)),
        out_shape=jax.ShapeDtypeStruct(cot.shape, jnp.float32),
        grid_spec=pltpu.PrefetchScalarGridSpec(
            num_scalar_prefetch=1,
            grid=(steps,),
            in_specs=[field(rows), plain(rows), plain(rows), plain(rows), field(2 * levels),
                      pl.BlockSpec((5, 2, rows, 128), lambda g, s: (0, 0, 0, 0))]
            + [pl.BlockSpec((6, chunk, tiles, 128), lambda g, s: (0, g, 0, 0))]
            if len(edges) == 1
            else [field(rows), plain(rows), plain(rows), plain(rows), field(2 * levels),
                  pl.BlockSpec((5, 2, rows, 128), lambda g, s: (0, 0, 0, 0)),
                  field(tiles), field(tiles), plain(tiles)],
            out_specs=pl.BlockSpec(memory_space=pl.ANY),
            scratch_shapes=[
                pltpu.VMEM((2, 5, chunk, rows, 128), jnp.float32),
                pltpu.VMEM((5, 1, rows, 128), jnp.float32),
                pltpu.VMEM((5, rows, 128), jnp.float32),
                pltpu.VMEM((5, rows, 128), jnp.float32),
                pltpu.VMEM((min(len(edges), 2), 5, rows, 128), jnp.float32),
                pltpu.VMEM((rows, 128), jnp.float32),
                pltpu.SemaphoreType.DMA((2,)),
                pltpu.SemaphoreType.DMA(()),
            ],
        ),
        compiler_params=pltpu.CompilerParams(vmem_limit_bytes=40 << 20),
        cost_estimate=pl.CostEstimate(
            flops=30 * 5 * lon * rows * 128, bytes_accessed=4 * 14 * lon * rows * 128, transcendentals=0
        ),
        name="stencil",
    )(seat, cot, vw, zc, mc, smooth, halo, *edges)


def swap_levels(first, last, total):
    count = lax.axis_size("lev")
    if count == 2:
        seat = lax.axis_index("lev")
        lead = jnp.concatenate([first, total[None]], 0)
        trail = jnp.concatenate([last, jnp.zeros_like(total)[None]], 0)
        got = lax.ppermute(jnp.where(seat == 0, trail, lead), "lev", [(0, 1), (1, 0)])
        return jnp.where(seat == 0, got[:5], 0.0), jnp.where(seat == 1, got[:5], 0.0), got[5]
    up = lax.ppermute(first, "lev", [(i + 1, i) for i in range(count - 1)])
    down = lax.ppermute(last, "lev", [(i, i + 1) for i in range(count - 1)])
    return up, down, later_sum(total)


def later_sum(local):
    count = lax.axis_size("lev")
    total = jnp.zeros_like(local)
    for r in range(1, count):
        total = total + lax.ppermute(local, "lev", [(i + r, i) for i in range(count - r)])
    return total


def ask_levels(cot, vw):
    return swap_levels(vw[0] * cot[:, 0], vw[-1] * cot[:, -1], cot[2].sum(0))


def adjoint_part(cot, vw, up, down, later):
    weighted = vw[None] * cot
    above = jnp.concatenate([weighted[:, 1:], up[:, None]], 1)
    under = jnp.concatenate([down[:, None], weighted[:, :-1]], 1)
    below = [later + cot[2, -1]]
    for k in range(cot.shape[1] - 2, -1, -1):
        below.insert(0, below[0] + cot[2, k])
    parts = cot + (above - under)
    return jnp.concatenate(
        [parts[:3], parts[3:4] - COUPLE_B * jnp.stack(below)[None], parts[4:]], 0
    )


def polar_cut(x):
    return jnp.concatenate([x[..., :POLAR], x[..., x.shape[-1] - POLAR :]], -1)


def plain_body(cotangent, zonal_coef, merid_coef, vertical_wind, cutoff):
    levels, lon_dev, lat = cotangent.shape[1:]
    peers = lax.axis_size("lon")
    count = lax.axis_size("lev")
    seat = lax.axis_index("lev").astype(jnp.int32)[None]
    cot, vw = to_rows(cotangent), to_rows(vertical_wind)
    polar_cot = jnp.swapaxes(polar_cut(cotangent), 2, 3)
    polar_vw = jnp.swapaxes(polar_cut(vertical_wind), 1, 2)
    polar_got = ask_levels(polar_cot, polar_vw)
    ends_cot, ends_vw = cotangent[:, :, :: lon_dev - 1], vertical_wind[:, :: lon_dev - 1]
    ends_got = ask_levels(ends_cot, ends_vw)

    sends = edges_of(seat, cot, vw, levels, count == 2)
    polar_got, ends_got, sends = lax.optimization_barrier((polar_got, ends_got, sends))
    if count == 2:
        edges = [lax.ppermute(sends[0], "lev", [(0, 1), (1, 0)])]
    else:
        edges = [
            lax.ppermute(sends[0], "lev", [(i + 1, i) for i in range(count - 1)]),
            lax.ppermute(sends[1], "lev", [(i, i + 1) for i in range(count - 1)]),
            later_sum(sends[2]),
        ]
    polar = adjoint_part(polar_cot, polar_vw, *polar_got)
    ends_adj = adjoint_part(ends_cot, ends_vw, *ends_got)

    rows = 2 * POLAR // peers
    grouped = polar.reshape(5 * levels, peers, rows, lon_dev)
    grouped = jnp.swapaxes(grouped, 0, 1).reshape(peers, 5 * levels * rows, lon_dev)

    pack = jnp.concatenate([ends_adj.reshape(5 * levels, 2, lat), zonal_coef[:, :: lon_dev - 1]], 0)
    up = [(i, (i + 1) % peers) for i in range(peers)]
    down = [(j, i) for i, j in up]
    beyond = jnp.stack([lax.ppermute(pack[:, 1], "lon", up), lax.ppermute(pack[:, 0], "lon", down)], 1)
    halo_adj = beyond[: 5 * levels].reshape(5, levels, 2, lat)
    halo_zc = beyond[5 * levels :]

    smoothed = polar_filter(grouped, cutoff, peers)
    smoothed = smoothed.reshape(2, peers // 2, 5, levels, rows, lon_dev + 2)
    smoothed = smoothed.transpose(2, 5, 0, 3, 1, 4).reshape(5, lon_dev + 2, 2, levels, POLAR)
    north, south = smoothed[:, :, 0], smoothed[:, :, 1]
    gap = ((0, 0), (0, 0), (0, 0))
    smooth = jnp.concatenate(
        [jnp.pad(north, (*gap, (0, 128 - POLAR))), jnp.pad(south, (*gap, (128 - POLAR, 0)))], 2
    )[:, 1 : lon_dev + 1]
    outer = [jnp.swapaxes(x[:, :: lon_dev + 1], 1, 2) for x in (north, south)]
    halo_f = jnp.concatenate([outer[0], halo_adj[..., POLAR : lat - POLAR], outer[1]], 3)
    halo = jnp.stack(coupled(halo_zc, [halo_f[f] for f in range(5)], 0))
    out = stencil(
        seat, cot, vw, to_rows(zonal_coef), to_rows(merid_coef), smooth, to_rows(halo), edges, levels
    )
    return from_rows(out, levels)


def lane_of(shape):
    return lax.broadcasted_iota(jnp.int32, shape, len(shape) - 1)


def pair_up(a, b, lane):
    inner = jnp.where(lane < 64, pltpu.roll(b, POLAR, 1), pltpu.roll(b, 128 - POLAR, 1))
    return jnp.where((lane >= POLAR) & (lane < 128 - POLAR), inner, a)


def second_of(pair, lane):
    return jnp.where(lane < 64, pltpu.roll(pair, 128 - POLAR, 1), pltpu.roll(pair, POLAR, 1))


def polar_level(levels, north, south, k, lane):
    lon, rows, _ = north.shape
    near = north.reshape(lon * rows, 128)[pl.ds(k, lon, stride=rows), :]
    far = south.reshape(lon * rows, 128)[pl.ds(levels + k, lon, stride=rows), :]
    return jnp.where(lane < 64, near, far)


def edge_block(levels, front, cot, vw, out):
    fields, chunk, rows, _ = cot.shape
    tiles = rows // levels
    flat_c = cot.reshape(fields * chunk * rows, 128)
    flat_v = vw.reshape(chunk * rows, 128)
    flat_t = cot.at[2].reshape(chunk * rows, 128)

    def product(k, sign):
        c = flat_c[pl.ds(k, fields * chunk * tiles, stride=levels), :]
        v = flat_v[pl.ds(k, chunk * tiles, stride=levels), :]
        c = c.reshape(fields, chunk, tiles, 128)
        out[:fields] = sign * (v.reshape(1, chunk, tiles, 128) * c)

    total = flat_t[pl.ds(0, chunk * tiles, stride=levels), :]
    for k in range(1, levels):
        total = total + flat_t[pl.ds(k, chunk * tiles, stride=levels), :]
    out[fields] = jnp.where(front, 0.0, total.reshape(chunk, tiles, 128))
    pl.when(front)(lambda: product(levels - 1, -1.0))
    pl.when(jnp.logical_not(front))(lambda: product(0, 1.0))


def edge_pack(levels, front, cot, vw, out):
    _, chunk, rows, _ = cot.shape
    tiles = rows // levels
    lane = lane_of((chunk, 128))
    k = jnp.where(front, levels - 1, 0)
    sign = jnp.where(front, -1.0, 1.0)
    flat_v = vw.reshape(chunk * rows, 128)
    wind = [sign * flat_v[pl.ds(t * levels + k, chunk, stride=rows), :] for t in range(tiles)]
    spare = []
    for f in range(6):
        flat = cot.at[min(f, 4) if f < 5 else 2].reshape(chunk * rows, 128)
        w = []
        for t in range(tiles):
            if f < 5:
                w.append(wind[t] * flat[pl.ds(t * levels + k, chunk, stride=rows), :])
            else:
                total = flat[pl.ds(t * levels, chunk, stride=rows), :]
                for n in range(1, levels):
                    total = total + flat[pl.ds(t * levels + n, chunk, stride=rows), :]
                w.append(jnp.where(front, 0.0, total))
        at = f * (tiles - 1)
        out[at] = jnp.where(lane < POLAR, w[-1], w[0])
        for t in range(1, tiles - 1):
            out[at + t] = w[t]
        spare.append(w[-1])
        if f % 2:
            inner = (lane >= POLAR) & (lane < 128 - POLAR)
            out[6 * (tiles - 1) + f // 2] = jnp.where(inner, spare[f - 1], pltpu.roll(spare[f], 64, 1))


def edge_unpack(tiles, edges, polar, full):
    chunk = edges.shape[1]
    lane = lane_of((chunk, 128))
    for f in range(6):
        at = f * (tiles - 1)
        mixed, rest, near = edges[at], edges[6 * (tiles - 1) + f // 2], polar[f]
        if f % 2:
            rest = pltpu.roll(rest, 64, 1)
        full[f * tiles] = jnp.where(lane < POLAR, near, mixed)
        for t in range(1, tiles - 1):
            full[f * tiles + t] = edges[at + t]
        last = jnp.where(lane < 128 - POLAR, rest, near)
        full[f * tiles + tiles - 1] = jnp.where(lane < POLAR, mixed, last)


def open_kernel(levels, seat, cot, vw, sent, ends, local, cn, cs, vn, vs, ec, ev, below, made, sems, out_sems):
    _, lon, rows, _ = cot.shape
    wide = 2 * levels
    lane = lane_of((lon, 128))
    front = seat[0] == 0
    near, far = pl.ds(0, wide), pl.ds(rows - wide, wide)
    jobs = [(vw.at[:, near], vn), (vw.at[:, far], vs)]
    order = (2, 0, 1, 3, 4)
    for f in order:
        jobs += [(cot.at[f, :, near], cn.at[f]), (cot.at[f, :, far], cs.at[f])]
    for n, e in enumerate((0, lon - 1)):
        jobs += [(cot.at[:, e], ec.at[:, n]), (vw.at[e], ev.at[n])]
    jobs = [pltpu.make_async_copy(a, b, sems.at[n]) for n, (a, b) in enumerate(jobs)]
    for job in jobs:
        job.start()
    jobs[0].wait()
    jobs[1].wait()
    v = [polar_level(levels, vn, vs, k, lane) for k in range(levels)]
    half, away = levels // 2, []
    for n, f in enumerate(order):
        jobs[2 + 2 * n].wait()
        jobs[3 + 2 * n].wait()
        c = [polar_level(levels, cn.at[f], cs.at[f], k, lane) for k in range(levels)]
        w = [a * b for a, b in zip(v, c)]
        edge = jnp.where(front, -w[levels - 1], w[0])
        if f == 2:
            run = c[levels - 1]
            below[levels - 1] = run
            for k in range(levels - 2, -1, -1):
                run = run + c[k]
                below[k] = run
            total = jnp.where(front, 0.0, run)
            sent[2] = total
        if f == 4:
            sent[2] = pair_up(edge, sent[2], lane)
        elif f == 2:
            sent[1] = edge
        elif f % 2:
            sent[f // 2] = pair_up(sent[f // 2], edge, lane)
        else:
            sent[f // 2] = edge
        for k in range(0, levels, 2):
            pieces = []
            for at in (k, k + 1):
                a = c[at]
                if at < levels - 1:
                    a = a + w[at + 1]
                if at > 0:
                    a = a - w[at - 1]
                if f == 3:
                    a = a - COUPLE_B * below[at]
                pieces.append(a)
            made[f * half + k // 2] = pair_up(pieces[0], pieces[1], lane)
        mine = pl.ds(f * half, half)
        away.append(pltpu.make_async_copy(made.at[mine], local.at[mine], out_sems.at[f]))
        away[-1].start()
    for job in jobs[12:]:
        job.wait()
    edge_block(levels, front, ec, ev, ends)
    for job in away:
        job.wait()


def opening(seat, cot, vw, levels):
    _, lon, rows, _ = cot.shape
    tiles, wide = rows // levels, 2 * levels
    f32 = jnp.float32
    place = pl.BlockSpec(memory_space=pltpu.HBM)
    vmem = pl.BlockSpec(memory_space=pltpu.VMEM)
    return pl.pallas_call(
        functools.partial(open_kernel, levels),
        out_shape=[
            jax.ShapeDtypeStruct((3, lon, 128), f32),
            jax.ShapeDtypeStruct((6, 2, tiles, 128), f32),
            pltpu.HBM((5 * levels // 2, lon, 128), f32),
        ],
        in_specs=[pl.BlockSpec(memory_space=pltpu.SMEM), place, place],
        out_specs=[vmem, vmem, place],
        scratch_shapes=[
            pltpu.VMEM((5, lon, wide, 128), f32), pltpu.VMEM((5, lon, wide, 128), f32),
            pltpu.VMEM((lon, wide, 128), f32), pltpu.VMEM((lon, wide, 128), f32),
            pltpu.VMEM((5, 2, rows, 128), f32), pltpu.VMEM((2, rows, 128), f32),
            pltpu.VMEM((levels, lon, 128), f32), pltpu.VMEM((5 * levels // 2, lon, 128), f32),
            pltpu.SemaphoreType.DMA((16,)), pltpu.SemaphoreType.DMA((5,)),
        ],
        compiler_params=pltpu.CompilerParams(vmem_limit_bytes=ROOM),
        cost_estimate=pl.CostEstimate(flops=9_000_000, bytes_accessed=10_000_000, transcendentals=0),
        name="opening",
    )(seat, cot, vw)


def edge_run_kernel(levels, start, chunk, count, seat, cot, vw, out, cbuf, vbuf, sems):
    def jobs(n):
        at = pl.ds(start + n * chunk, chunk)
        return (
            pltpu.make_async_copy(cot.at[:, at], cbuf.at[n], sems.at[n, 0]),
            pltpu.make_async_copy(vw.at[at], vbuf.at[n], sems.at[n, 1]),
        )

    for n in range(count):
        for job in jobs(n):
            job.start()
    for n in range(count):
        for job in jobs(n):
            job.wait()
        edge_pack(
            levels, seat[0] == 0, cbuf.at[n], vbuf.at[n], out.at[:, pl.ds(n * chunk, chunk)]
        )


def packed_rows(tiles):
    return 6 * (tiles - 1) + 3


def edge_run(seat, cot, vw, levels, start, chunk, count):
    fields, _, rows, _ = cot.shape
    tiles = rows // levels
    place = pl.BlockSpec(memory_space=pl.ANY)
    size = count * chunk
    return pl.pallas_call(
        functools.partial(edge_run_kernel, levels, start, chunk, count),
        out_shape=jax.ShapeDtypeStruct((packed_rows(tiles), size, 128), jnp.float32),
        in_specs=[pl.BlockSpec(memory_space=pltpu.SMEM), place, place],
        out_specs=pl.BlockSpec(memory_space=pltpu.VMEM),
        scratch_shapes=[
            pltpu.VMEM((count, fields, chunk, rows, 128), jnp.float32),
            pltpu.VMEM((count, chunk, rows, 128), jnp.float32),
            pltpu.SemaphoreType.DMA((count, 2)),
        ],
        compiler_params=pltpu.CompilerParams(vmem_limit_bytes=SOME),
        cost_estimate=pl.CostEstimate(
            flops=50_000 * size, bytes_accessed=120_000 * size, transcendentals=0
        ),
        name="edge_run",
    )(seat, cot, vw)


def slots_of(k, nq):
    north, south = range(nq // 2), range(nq // 2, nq)
    return (
        [(k, q) for q in north] + [(k + 1, q) for q in north]
        + [(k + 1, q) for q in south] + [(k, q) for q in south]
    )


def polar_kernel(
    peers, levels, late,
    cot, vw, zc, fwd, inv, ct, st, local, got, ends, mask_ref,
    smooth, flux_west, flux_east, polar, *rest,
):
    late_out, rest = rest[: len(late)], rest[len(late) :]
    count = len(late)
    cbufs, vbufs, ebufs = rest[:count], rest[count : 2 * count], rest[2 * count : 3 * count]
    (fwd_ref, inv_ref, ct_ref, st_ref, mine_ref, x_ref, held, made, back, z, zt, ec, ev, ez, es, spread, below_ref,
     own_sem, wave_sem, send_a, recv_a, send_b, recv_b, col_sem, late_in, late_sem) = rest[3 * count :]
    me = lax.axis_index("lon")
    front = lax.axis_index("lev") == 0
    _, lon, rows, _ = cot.shape
    wide = 2 * levels
    nq = peers // levels
    span = 2 * POLAR // nq
    cols = 5 * span
    half = cols // 2
    kpad = ct_ref.shape[2]
    lane = lane_of((lon, 128))
    barrier = pltpu.get_barrier_semaphore()

    def ahead(o):
        return lax.rem(me + o, peers)

    def behind(o):
        return lax.rem(me + peers - o, peers)

    def greet(o, _):
        pl.semaphore_signal(barrier, inc=1, device_id={"lon": ahead(o)}, device_id_type=MESH)
        return 0

    own_part = pltpu.make_async_copy(local, mine_ref, wave_sem.at[4])
    own_part.start()
    lax.fori_loop(1, peers, greet, 0)

    column_jobs = []
    for n, e in enumerate((0, lon - 1)):
        for m, (a, b) in enumerate(
            ((cot.at[:, e], ec.at[:, n]), (vw.at[e], ev.at[n]), (zc.at[e], ez.at[n]))
        ):
            column_jobs.append(pltpu.make_async_copy(a, b, col_sem.at[3 * n + m]))
    late_jobs, late_outs = [], []
    for n, (out, (start, size, _)) in enumerate(zip(late_out, late)):
        where = pl.ds(start, size)
        late_jobs.append((
            pltpu.make_async_copy(cot.at[:, where], cbufs[n], late_in.at[n, 0]),
            pltpu.make_async_copy(vw.at[where], vbufs[n], late_in.at[n, 1]),
        ))
        late_outs.append(pltpu.make_async_copy(ebufs[n], out, late_sem.at[n]))
    wave_jobs = [
        pltpu.make_async_copy(fwd, fwd_ref, wave_sem.at[0]),
        pltpu.make_async_copy(inv, inv_ref, wave_sem.at[1]),
        pltpu.make_async_copy(ct, ct_ref, wave_sem.at[2]),
        pltpu.make_async_copy(st, st_ref, wave_sem.at[3]),
    ]
    for job in column_jobs + wave_jobs:
        job.start()
    for jobs in late_jobs:
        for job in jobs:
            job.start()

    z[...] = jnp.zeros_like(z)
    own_part.wait()
    for f in range(5):
        pair = got[f // 2]
        edge = second_of(pair, lane) if f % 2 else pair
        tail = second_of(got[2], lane) if f == 3 else None
        for k in range(0, levels, 2):
            add = []
            for at in (k, k + 1):
                a = jnp.zeros((lon, 128), jnp.float32)
                if at == levels - 1:
                    a = a + jnp.where(front, edge, 0.0)
                if at == 0:
                    a = a + jnp.where(front, 0.0, edge)
                if f == 3:
                    a = a - COUPLE_B * tail
                add.append(a)
            z[:lon] = mine_ref[f * levels // 2 + k // 2] + pair_up(add[0], add[1], lane)
            zt[...] = z[...].T
            for n, (at, q) in enumerate(slots_of(k, nq)):
                d = at * nq + q
                x_ref[d, f * span : (f + 1) * span] = zt[n * span : (n + 1) * span, :128]
                for h in range(0, span, 8):
                    to = f * span + h
                    end = zt[n * span + h : n * span + h + 8, 128:]
                    if to < half:
                        x_ref[d, cols + to : cols + to + 8] = end
                    else:
                        to += cols - half
                        x_ref[d, to : to + 8] += pltpu.roll(end, 64, 1)

    def out_copy(d):
        return pltpu.make_async_remote_copy(
            src_ref=x_ref.at[d], dst_ref=held.at[me], send_sem=send_a.at[d],
            recv_sem=recv_a.at[me], device_id={"lon": d}, device_id_type=MESH,
        )

    def in_copy(s):
        return pltpu.make_async_remote_copy(
            src_ref=x_ref.at[s], dst_ref=held.at[s], send_sem=send_a.at[s],
            recv_sem=recv_a.at[s], device_id={"lon": s}, device_id_type=MESH,
        )

    def back_copy(d):
        return pltpu.make_async_remote_copy(
            src_ref=made.at[d], dst_ref=back.at[me], send_sem=send_b.at[d],
            recv_sem=recv_b.at[me], device_id={"lon": d}, device_id_type=MESH,
        )

    def home_copy(s):
        return pltpu.make_async_remote_copy(
            src_ref=made.at[s], dst_ref=back.at[s], send_sem=send_b.at[s],
            recv_sem=recv_b.at[s], device_id={"lon": s}, device_id_type=MESH,
        )

    pl.semaphore_wait(barrier, peers - 1)
    lax.fori_loop(1, peers, lambda o, c: (out_copy(ahead(o)).start(), c)[1], 0)
    own = pltpu.make_async_copy(x_ref.at[me], held.at[me], own_sem)
    own.start()

    for n, jobs in enumerate(late_jobs):
        for job in jobs:
            job.wait()
        (edge_pack if late[n][2] else edge_block)(levels, front, cbufs[n], vbufs[n], ebufs[n])
        late_outs[n].start()

    for job in wave_jobs:
        job.wait()
    for f in range(6):
        polar[f] = second_of(got[f // 2], lane) if f % 2 else got[f // 2]
    own.wait()
    zero = jnp.zeros((cols, kpad), jnp.float32)
    dot = functools.partial(jnp.dot, precision=HIGHEST, preferred_element_type=jnp.float32)

    def gather(s, carry):
        a, b = carry
        ends = held[s, cols:]
        ends = jnp.concatenate([ends[:, :64], ends[:, 64:]], 0)
        both = dot(held[s, :cols], fwd_ref[:128]) + dot(ends, fwd_ref[128:])
        c, v = both[:, :kpad], both[:, kpad:]
        cos, sin = ct_ref[s], st_ref[s]
        return a + (cos * c - sin * v), b + (sin * c + cos * v)

    def arrive(o, carry):
        s = behind(o)
        in_copy(s).wait_recv()
        return gather(s, carry)

    a, b = lax.fori_loop(1, peers, arrive, gather(me, (zero, zero)))
    mask = jnp.concatenate([mask_ref[...]] * 5, 0)
    a = a * mask
    b = b * mask

    def turn(d):
        cos, sin = ct_ref[d], st_ref[d]
        p, q = a * cos + b * sin, b * cos - a * sin
        y = dot(p, inv_ref[0]) + dot(q, inv_ref[1])
        made[d, :cols] = y[:, :128]
        made[d, cols:] = jnp.concatenate([y[:half, 128:], y[half:, 128:]], 1)

    far = peers - peers // 2

    def turn_of(n):
        return ahead(jnp.where(n < far, n + peers // 2, n - far + 1))

    def depart(n, _):
        turn(turn_of(n))
        pl.when(n > 0)(lambda: back_copy(turn_of(n - 1)).start())
        return 0

    lax.fori_loop(0, peers - 1, depart, 0)
    turn(me)
    back_copy(turn_of(peers - 2)).start()
    mine = pltpu.make_async_copy(made.at[me], back.at[me], own_sem)
    mine.start()
    for job in late_outs:
        job.wait()
    for job in column_jobs:
        job.wait()
    mine.wait()
    lax.fori_loop(1, peers, lambda o, c: (home_copy(behind(o)).wait_recv(), c)[1], 0)

    for f in range(5):
        flat = smooth.at[f].reshape(lon * wide, 128)
        for k in range(0, levels, 2):
            for n, (at, q) in enumerate(slots_of(k, nq)):
                d = at * nq + q
                zt[n * span : (n + 1) * span, :128] = back[d, f * span : (f + 1) * span]
                for h in range(0, span, 8):
                    to = f * span + h
                    if to < half:
                        end = back[d, cols + to : cols + to + 8]
                    else:
                        to += cols - half
                        end = pltpu.roll(back[d, to : to + 8], 64, 1)
                    zt[n * span + h : n * span + h + 8, 128:] = end
            z[...] = zt[...].T
            first = z[:lon]
            flat[pl.ds(k, lon, stride=wide), :] = first
            flat[pl.ds(levels + k, lon, stride=wide), :] = first
            flat[pl.ds(k + 1, lon, stride=wide), :] = pltpu.roll(first, 128 - POLAR, 1)
            flat[pl.ds(levels + k + 1, lon, stride=wide), :] = pltpu.roll(first, POLAR, 1)

    for f in range(5):
        for n, e in enumerate((0, lon - 1)):
            es[f, n] = smooth[f, e]
    spread[...] = jnp.zeros_like(spread)
    column = column_maker(levels, front, ec, ev, es, lambda f, l: ends[f, l], spread, below_ref)
    for n in range(2):
        field = column(n)
        fields = [field(f)[1] for f in range(5)]
        for v in range(rows // 8):
            zonal = coupled(ez[n, 8 * v : 8 * v + 8], [fields[f][v] for f in range(5)], 0)
            for f in range(5):
                (flux_west, flux_east)[n][f, 8 * v : 8 * v + 8] = zonal[f]
    lax.fori_loop(1, peers, lambda o, c: (out_copy(ahead(o)).wait_send(), c)[1], 0)
    lax.fori_loop(1, peers, lambda o, c: (back_copy(ahead(o)).wait_send(), c)[1], 0)


def hold(a):
    return pltpu.with_memory_space_constraint(jnp.asarray(a), pltpu.HBM)


def polar_path(cot, vw, zc, local, got, ends, cutoff, levels, peers, late):
    _, lon, rows, _ = cot.shape
    tiles, wide = rows // levels, 2 * levels
    nq = peers // levels
    nlon = peers * lon
    span = cutoff.shape[0] // nq
    kpad = (KMAX + 1 + 127) // 128 * 128
    wave = np.arange(kpad)
    fwd = np.concatenate(angles(np.arange(lon)[:, None], wave[None, :], nlon), axis=1)
    inv = np.stack(angles(wave[:, None], np.arange(lon)[None, :], nlon))
    short = 192 - lon
    fwd = np.pad(fwd, ((0, short), (0, 0)))
    inv = np.pad(inv, ((0, 0), (0, 0), (0, short)))
    ct, st = angles(np.arange(peers)[:, None, None] * lon, wave[None, None, :], nlon)
    mine = lax.dynamic_slice_in_dim(cutoff, lax.axis_index("lon") % nq * span, span)
    weight = np.where(wave == 0, 1.0 / nlon, 2.0 / nlon).astype(np.float32)
    mask = jnp.where(jnp.asarray(wave, jnp.int32)[None, :] <= mine[:, None], weight[None, :], 0.0)
    vmem = pl.BlockSpec(memory_space=pltpu.VMEM)
    place = pl.BlockSpec(memory_space=pltpu.HBM)
    dma = pltpu.SemaphoreType.DMA
    f32 = jnp.float32
    shape = (peers, 5 * span + 5 * span // 2, 128)
    count = len(late)
    away = [
        (packed_rows(tiles), size, 128) if packed else (6, size, tiles, 128) for _, size, packed in late
    ]
    return pl.pallas_call(
        functools.partial(polar_kernel, peers, levels, late),
        out_shape=[
            jax.ShapeDtypeStruct((5, lon, wide, 128), f32),
            jax.ShapeDtypeStruct((5, rows, 128), f32),
            jax.ShapeDtypeStruct((5, rows, 128), f32),
            jax.ShapeDtypeStruct((6, lon, 128), f32),
        ] + [jax.ShapeDtypeStruct(a, f32) for a in away],
        in_specs=[place] * 8 + [vmem] * 3,
        out_specs=[vmem] * 4 + [place] * count,
        scratch_shapes=[pltpu.VMEM((5, size, rows, 128), f32) for _, size, _ in late]
        + [pltpu.VMEM((size, rows, 128), f32) for _, size, _ in late]
        + [pltpu.VMEM(a, f32) for a in away]
        + [
            pltpu.VMEM(fwd.shape, f32), pltpu.VMEM(inv.shape, f32),
            pltpu.VMEM(ct.shape, f32), pltpu.VMEM(st.shape, f32), pltpu.VMEM(local.shape, f32),
            pltpu.VMEM(shape, f32), pltpu.VMEM(shape, f32), pltpu.VMEM(shape, f32),
            pltpu.VMEM(shape, f32), pltpu.VMEM((256, 128), f32), pltpu.VMEM((128, 256), f32),
            pltpu.VMEM((5, 2, rows, 128), f32), pltpu.VMEM((2, rows, 128), f32),
            pltpu.VMEM((2, rows, 128), f32), pltpu.VMEM((5, 2, wide, 128), f32),
            pltpu.VMEM((1, 5, rows, 128), f32),
            pltpu.VMEM((1, rows, 128), f32),
            dma(()), dma((5,)), dma((peers,)), dma((peers,)), dma((peers,)), dma((peers,)),
            dma((6,)), dma((count, 2)), dma((count,)),
        ],
        compiler_params=pltpu.CompilerParams(
            collective_id=1, has_side_effects=True, vmem_limit_bytes=30 << 20
        ),
        cost_estimate=pl.CostEstimate(flops=8_000_000_000, bytes_accessed=60_000_000, transcendentals=0),
        name="polar_path",
    )(cot, vw, zc, *(hold(a) for a in (fwd, inv, ct, st, local)), got, ends, mask)


def column_maker(levels, front, cot, vw, smooth, edges, spread, below_ref):
    _, _, rows, _ = cot.shape
    tiles = rows // levels
    parts = rows // 8
    edge_at = jnp.where(front, levels - 1, 0)
    row = lax.broadcasted_iota(jnp.int32, (8, 128), 0)
    lane = lane_of((8, 128))
    k = lax.rem(row, levels)
    north = (row < levels) & (lane < POLAR)
    south = (row >= levels) & (lane >= 128 - POLAR)
    at = [pl.ds(8 * v, 8) for v in range(parts)]

    def column(l, side=0):
        for f in range(5):
            spread[side, f, pl.ds(edge_at, tiles, stride=levels), :] = edges(f, l)
        for n in range(levels):
            below_ref[side, pl.ds(n, tiles, stride=levels), :] = edges(5, l)
        wind = [vw[l, a] for a in at]
        under = [jnp.where(k > 0, a, 0.0) for a in wind]
        over = [jnp.where(k < levels - 1, a, 0.0) for a in wind]

        def field(f):
            whole, inner = [], []
            for v in range(parts):
                c = cot[f, l, at[v]]
                a = c + (pltpu.roll(under[v] * c, 7, 0) - pltpu.roll(over[v] * c, 1, 0))
                a = a + spread[side, f, at[v]]
                if f == 3:
                    run, r = cot[2, l, at[v]], 1
                    while r < levels:
                        run = run + jnp.where(k < levels - r, pltpu.roll(run, 8 - r, 0), 0.0)
                        r *= 2
                    a = a - COUPLE_B * (run + below_ref[side, at[v]])
                whole.append(a)
                if v == 0:
                    a = jnp.where(north, smooth[f, l], a)
                if v == parts - 1:
                    a = jnp.where(south, smooth[f, l], a)
                inner.append(a)
            return whole, inner

        return field

    return column


def lat_inputs(levels, m):
    row = lax.broadcasted_iota(jnp.int32, (8, 128), 0)
    lane = lane_of((8, 128))
    top = row < levels
    turned = [pltpu.roll(a, levels, 0) for a in m]
    zero = jnp.zeros((8, 128), jnp.float32)
    tile = [jnp.where(top, a, b) for a, b in zip([zero] + turned, turned + [zero])]
    near = [jnp.where(lane == 127, tile[v], a) for v, a in enumerate(m)]
    far = [jnp.where(lane == 0, tile[v + 1], a) for v, a in enumerate(m)]
    return near, far


def lat_change(near, far):
    return pltpu.roll(far, 127, 1) - pltpu.roll(near, 1, 1)


def strip_kernel(levels, start, steps, turns, first, last, packed, seat, cot, vw, zc, mc, smooth, edges, *rest):
    rest = list(rest)
    more = rest.pop(0) if turns < steps else None
    if packed:
        polar, full = rest.pop(0), rest.pop()
    if not first:
        wait_in, prior_in, _ = rest.pop(0), rest.pop(0), rest.pop(0)
    if last:
        left, right, column_in = rest.pop(0), rest.pop(0), rest.pop(0)
    if first:
        column_out = rest.pop(1)
    out, wait, prior, ready, spread, below_ref, turn, sems = rest[:8]
    _, chunk, rows, _ = cot.shape
    parts = rows // 8
    g = pl.program_id(0)
    slot = lax.rem(g, 2)

    def first_copy():
        return pltpu.make_async_copy(
            ready.at[0, :, pl.ds(2, chunk - 2)], out.at[:, pl.ds(1, chunk - 2)], sems.at[0]
        )

    def copy(at):
        s = lax.rem(at, 2)
        return pltpu.make_async_copy(
            ready.at[s], out.at[:, pl.ds(start + at * chunk - 1, chunk)], sems.at[s]
        )

    def act(at, what):
        if first:
            pl.when(at == 0)(lambda: getattr(first_copy(), what)())
            pl.when(at > 0)(lambda: getattr(copy(at), what)())
        else:
            getattr(copy(at), what)()

    @pl.when(g == 0)
    def _():
        spread[...] = jnp.zeros_like(spread)
        turn[...] = jnp.zeros_like(turn)
        if first:
            prior[...] = jnp.zeros_like(prior)
            wait[...] = jnp.zeros_like(wait)
        else:
            prior[...] = prior_in[...]
            wait[...] = wait_in[...]

    pl.when(g >= 2)(lambda: act(g - 2, "wait"))
    if packed:
        tiles = rows // levels
        if more is None:
            edge_unpack(tiles, edges, polar, full)
        else:
            pl.when(g < turns)(lambda: edge_unpack(tiles, edges, polar, full))
            pl.when(g >= turns)(lambda: edge_unpack(tiles, more, polar, full))
        flat = full.reshape(6 * tiles * chunk, 128)
        sent = lambda f, l: flat[pl.ds(f * tiles * chunk + l, tiles, stride=chunk), :]
    else:
        sent = lambda f, l: edges[f, l]
    column = column_maker(levels, seat[0] == 0, cot, vw, smooth, sent, spread, below_ref)
    at = [pl.ds(8 * v, 8) for v in range(parts)]

    def flux_of(l, side):
        field = column(l, side)
        zcs = [zc[l, a] for a in at]
        mcs = [mc[l, a] for a in at]
        whole3, f3 = field(3)
        half3 = [COUPLE_H * a for a in f3]
        parted, zonal, sides = [None] * 5, [None] * 5, [None] * 5

        def close(f, whole, inner, add_zonal=None, add_merid=None):
            z = [a * b for a, b in zip(zcs, inner)]
            m = [a * b for a, b in zip(mcs, inner)]
            if add_zonal is not None:
                z = [a + b for a, b in zip(z, add_zonal)]
            if add_merid is not None:
                m = [a + b for a, b in zip(m, add_merid)]
            zonal[f] = z
            parted[f] = whole
            sides[f] = lat_inputs(levels, m)

        whole, f0 = field(0)
        close(0, whole, f0, add_zonal=half3)
        whole, f1 = field(1)
        close(1, whole, f1, add_merid=half3)
        close(3, whole3, f3, [COUPLE_G * a for a in f0], [COUPLE_G * a for a in f1])
        for f in (2, 4):
            close(f, *field(f))
        return parted, zonal, sides

    grid = [(f, v) for f in range(5) for v in range(parts)]

    def fetch(f, v):
        return lat_change(turn[0, f, at[v]], turn[1, f, at[v]])

    def keep(f, v, whole, zonal, sides, before):
        wait[f, at[v]] = whole[f][v] - before
        prior[f, at[v]] = zonal[f][v]
        turn[0, f, at[v]] = sides[f][0][v]
        turn[1, f, at[v]] = sides[f][1][v]

    def one(l):
        behind = {(f, v): wait[f, at[v]] + fetch(f, v) for f, v in grid}
        whole, zonal, sides = flux_of(l, 0)
        for f, v in grid:
            ready[slot, f, l, at[v]] = behind[f, v] + zonal[f][v]
            keep(f, v, whole, zonal, sides, prior[f, at[v]])

    def two(n, _):
        l = 2 * n
        behind = {(f, v): wait[f, at[v]] + fetch(f, v) for f, v in grid}
        whole, zonal, sides = flux_of(l, 0)
        for f, v in grid:
            ready[slot, f, l, at[v]] = behind[f, v] + zonal[f][v]
            behind[f, v] = whole[f][v] - prior[f, at[v]] + lat_change(sides[f][0][v], sides[f][1][v])
        whole, after, sides = flux_of(l + 1, 1)
        for f, v in grid:
            ready[slot, f, l + 1, at[v]] = behind[f, v] + after[f][v]
            keep(f, v, whole, after, sides, zonal[f][v])
        return 0

    lax.fori_loop(0, chunk // 2, two, 0)
    if chunk % 2:
        one(chunk - 1)
    act(g, "start")
    if first:

        @pl.when(g == 0)
        def _():
            for f in range(5):
                column_out[f] = ready[0, f, 1]

    @pl.when(g == steps - 1)
    def _():
        for f, v in grid:
            wait[f, at[v]] += fetch(f, v)
        if last:
            final, last_sem = rest[8:10]
            for f in range(5):
                final[0, f, 0] = column_in[f] - left[f]
                final[1, f, 0] = wait[f] + right[f]
            ends = [
                pltpu.make_async_copy(final.at[n], out.at[:, pl.ds(e, 1)], last_sem.at[n])
                for n, e in enumerate((0, start + steps * chunk - 1))
            ]
            for end in ends:
                end.start()
        if steps > 1:
            act(g - 1, "wait")
        act(g, "wait")
        if last:
            for end in ends:
                end.wait()


def strip(seat, cot, vw, zc, mc, smooth, edges, polar, state, borders, levels, start, steps, chunk):
    _, _, rows, _ = cot.shape
    tiles = rows // levels
    at = start // chunk
    first, last = not state, borders is not None
    field = lambda n: pl.BlockSpec((5, chunk, n, 128), lambda g, s: (0, at + g, 0, 0))
    plain = pl.BlockSpec((chunk, rows, 128), lambda g, s: (at + g, 0, 0))
    whole = pl.BlockSpec((5, rows, 128), lambda g, s: (0, 0, 0))
    place = pl.BlockSpec(memory_space=pl.ANY)
    packed = polar is not None
    in_specs = [field(rows), plain, plain, plain, field(2 * levels)]
    turns = steps
    if packed:
        turns = edges[0].shape[1] // chunk
        shape = (edges[0].shape[0], chunk, 128)
        in_specs.append(pl.BlockSpec(shape, lambda g, s: (0, jnp.minimum(g, turns - 1), 0)))
        if turns < steps:
            in_specs.append(pl.BlockSpec(shape, lambda g, s: (0, jnp.maximum(g - turns, 0), 0)))
        in_specs.append(pl.BlockSpec((6, chunk, 128), lambda g, s: (0, at + g, 0)))
    else:
        in_specs.append(pl.BlockSpec((6, chunk, tiles, 128), lambda g, s: (0, g, 0, 0)))
    in_specs += [] if first else [whole, whole, place]
    args = [seat, cot, vw, zc, mc, smooth, *edges] + [polar] * packed + [*state]
    aliases = {} if first else {len(args) - 1: 0}
    if last:
        in_specs += [whole] * 3
        args += borders
    one = jax.ShapeDtypeStruct((5, rows, 128), jnp.float32)
    held = [pltpu.VMEM((5, rows, 128), jnp.float32)] * 2
    scratch = [
        pltpu.VMEM((2, 5, chunk, rows, 128), jnp.float32),
        pltpu.VMEM((2, 5, rows, 128), jnp.float32),
        pltpu.VMEM((2, rows, 128), jnp.float32),
        pltpu.VMEM((2, 5, rows, 128), jnp.float32),
        pltpu.SemaphoreType.DMA((2,)),
    ]
    if last:
        scratch = held + scratch + [
            pltpu.VMEM((2, 5, 1, rows, 128), jnp.float32), pltpu.SemaphoreType.DMA((2,)),
        ]
    if packed:
        scratch = scratch + [pltpu.VMEM((6 * tiles, chunk, 128), jnp.float32)]
    extra = 0 if last else 3 if first else 2
    got = pl.pallas_call(
        functools.partial(strip_kernel, levels, start, steps, turns, first, last, packed),
        out_shape=[jax.ShapeDtypeStruct(cot.shape, jnp.float32)] + [one] * extra,
        grid_spec=pltpu.PrefetchScalarGridSpec(
            num_scalar_prefetch=1,
            grid=(steps,),
            in_specs=in_specs,
            out_specs=[place] + [whole] * extra,
            scratch_shapes=scratch,
        ),
        input_output_aliases=aliases,
        compiler_params=pltpu.CompilerParams(vmem_limit_bytes=SOME),
        cost_estimate=pl.CostEstimate(
            flops=30 * 5 * steps * chunk * rows * 128,
            bytes_accessed=4 * 14 * steps * chunk * rows * 128,
            transcendentals=0,
        ),
        name="strip",
    )(*args)
    return got[0] if last else [*got[-2:], got[0], *got[1:-2]]


def fast_body(cotangent, zonal_coef, merid_coef, vertical_wind, cutoff):
    levels, lon_dev, _ = cotangent.shape[1:]
    peers = lax.axis_size("lon")
    seat = lax.axis_index("lev").astype(jnp.int32)[None]
    cot, vw = to_rows(cotangent), to_rows(vertical_wind)
    zc, mc = to_rows(zonal_coef), to_rows(merid_coef)
    cot, vw, zc, mc = (hold(a) for a in (cot, vw, zc, mc))
    trade = lambda a: lax.ppermute(a, "lev", [(0, 1), (1, 0)])
    tail = lon_dev % 8 + 16
    whole = lon_dev - tail
    cuts = [0, 16, 16 + whole * 3 // 4 // 16 * 16, whole, lon_dev]
    parts = [(a, b - a) for a, b in zip(cuts, cuts[1:])]

    edges = []
    part = edge_run(seat, cot, vw, levels, 0, 16, 1)
    edges.append(trade(part))
    token, _ = lax.optimization_barrier((seat, part))
    sent, ends, local = opening(token, cot, vw, levels)
    polar_got = trade(sent)
    ends_got = trade(ends)
    token, _ = lax.optimization_barrier((token, sent))
    start, size = parts[1]
    part = edge_run(token, cot, vw, levels, start, 16, size // 16)
    edges.append(trade(part))
    polar_got, ends_got, _ = lax.optimization_barrier((polar_got, ends_got, part))
    late = (parts[2] + (True,), parts[3] + (False,))
    smooth, west, east, polar, *later = polar_path(
        cot, vw, zc, local, polar_got, ends_got, cutoff, levels, peers, late
    )
    edges += [trade(part) for part in later]
    state, borders, kept = [], None, None
    up = [(i, (i + 1) % peers) for i in range(peers)]
    joined = [((0, parts[0][1] + parts[1][1]), edges[:2])] + [(a, [b]) for a, b in zip(parts[2:], edges[2:])]
    for n, ((start, size), part) in enumerate(joined):
        lanes, chunk = polar, math.gcd(start, size, 16)
        if n == len(joined) - 1:
            borders = [left, right, kept]
            lanes, chunk = None, math.gcd(start, size)
            chunk = chunk // 2 if chunk % 2 == 0 else chunk
        state = strip(
            seat, cot, vw, zc, mc, smooth, part, lanes, state, borders, levels, start,
            size // chunk, chunk,
        )
        if n == 0:
            kept = state.pop()
            west, east, state[0] = lax.optimization_barrier((west, east, state[0]))
            left = lax.ppermute(east, "lon", up)
            right = lax.ppermute(west, "lon", [(j, i) for i, j in up])
    return from_rows(state, levels)


def is_fast(mesh, levels, lon_dev, lat, count):
    peers = mesh.shape["lon"]
    return (
        mesh.shape["lev"] == 2 and levels * 2 == 8 and peers % (2 * levels) == 0 and lat % 256 == 0
        and count == 2 * POLAR and count * levels // peers % 16 == 0 and 128 < lon_dev <= 192
    )


def solution(mesh):
    specs = (
        P(None, "lev", "lon", None),
        P("lev", "lon", None),
        P("lev", "lon", None),
        P("lev", "lon", None),
        P(),
    )

    def spread_over(body):
        return jax.shard_map(body, mesh=mesh, in_specs=specs, out_specs=specs[0], check_vma=False)

    def step(cotangent, zonal_coef, merid_coef, vertical_wind, cutoff):
        _, nlev, nlon, lat = cotangent.shape
        levels, lon_dev = nlev // mesh.shape["lev"], nlon // mesh.shape["lon"]
        args = cotangent, zonal_coef, merid_coef, vertical_wind, cutoff
        if is_fast(mesh, levels, lon_dev, lat, cutoff.shape[0]):
            return spread_over(fast_body)(*args)
        return spread_over(plain_body)(*args)

    return step
```
